128 devices in a mesh: dp: 16 (over x, z_hi, core), ctx: 8 (over z_lo, y).
Axes of the slice: x: 4, y: 4, z: 4 (z_hi: 2, z_lo: 2; z = z_hi * 2 + z_lo), core: 2. Of those that a mesh axis runs over, the one named last changes fastest.
Arguments:
- light_flux: float32 [16, 6, 4096], P('dp', None, 'ctx'), may hold values from -6 to 6
- lengths: int32 [16], P('dp'), may hold values from 1024 to 4096, as said below
- offsets: int32 [16, 4096], P('dp', 'ctx'), may hold values from 0 to 3
- start_weight: float32 [512, 3], replicated, may hold values from -3.5 to 3.5
- conv_weight: bfloat16 [2, 1024, 1536], P(None, 'dp'), may hold values from -0.15625 to 0.15625
- gate_bias: float32 [2, 1024], replicated, may hold values from -4 to 4
- mix_first: bfloat16 [1024, 512], P('dp'), may hold values from -0.25 to 0.25
- mix_last: bfloat16 [512, 512], P('dp'), may hold values from -0.25 to 0.25
- end_weight: float32 [6, 512], replicated, may hold values from -0.25 to 0.25
- cotangent: float32 [16, 3, 4096], P('dp', None, 'ctx'), may hold values from -0.0234375 to 0.0234375
Outputs:
- coupled: float32 [16, 3, 4096], P('dp', None, 'ctx')
- grad_start: float32 [512, 3], replicated
- grad_conv: float32 [2, 1024, 1536], P(None, 'dp')
- grad_bias: float32 [2, 1024], replicated
- grad_mix_first: float32 [1024, 512], P('dp')
- grad_mix_last: float32 [512, 512], P('dp')
- grad_end: float32 [6, 512], replicated
The draws below stay inside these ranges and needn't reach their ends.
Inputs may be any that keep to these rules, and one draw needn't show every extreme that they name: `lengths`: epochs at or past a curve's length are padding; at least one curve has no padding.
All inputs are finite; a program needn't handle non-finite values.
Results may differ from the reference program's by a relative error of at most 0.0091.
Values may be sent and summed in bfloat16 or wider, within the bound.
No kernel may reach another device: no remote copies, remote signals or barrier semaphores. Data moves between devices by JAX's collectives and lax.ppermute only.
A program may use at most 128 MiB of HBM per device.

```python
import jax
import jax.numpy as jnp
from jax import lax

C = 512
BANDS = 6
HALF = 3
BUCKETS = 4
LAYERS = 2
EPOCH_DEV = 512
EPOCHS = 4096
CURVES = 16
N_DP = 16


def draw_lengths(key, part):
    drawn = jax.random.randint(key, (CURVES,), EPOCHS // 4, EPOCHS + 1, dtype=jnp.int32)
    return drawn.at[0].set(EPOCHS)


def with_ends(result, own_key, least, largest):
    index_at = [jax.random.randint(jax.random.fold_in(own_key, axis), (), 0, length) for axis, length in enumerate(result.shape)]
    longest = result.shape.index(max(result.shape))
    next_to = index_at[:longest] + [(index_at[longest] + 1) % result.shape[longest]] + index_at[longest + 1:]
    return result.at[tuple(index_at)].set(least).at[tuple(next_to)].set(largest)


def level_of(own_key, extent, shards, low, top_value):
    loudness, own = 1.0, jax.random.fold_in(own_key, 6)
    for position, parts in shards:
        heights = jnp.exp(jax.random.uniform(jax.random.fold_in(own, position), (parts,), jnp.float32, low / len(shards), top_value / len(shards)))
        loudness = loudness * jnp.repeat(heights, extent[position] // parts).reshape([-1 if axis == position else 1 for axis in range(len(extent))])
    return loudness


def scatter_about(key, dims, width, most, split=(), kind=jnp.bfloat16):
    entries = width * jax.random.normal(key, dims, jnp.float32)
    if split:
        entries = entries * level_of(key, dims, split, -0.22, 0.18)
    return jnp.clip(entries, -most, most).astype(kind)


def setup_inputs(seed: int = 0) -> dict:
    key_of = jax.random.split(jax.random.key(seed), 11)
    return {
        "light_flux": scatter_about(key_of[0], (CURVES, BANDS, EPOCHS), 1.0, 6.0, ((0, 16), (2, 8)), jnp.float32),
        "lengths": draw_lengths(jax.random.fold_in(key_of[10], 71), 0),
        "offsets": with_ends(jax.random.randint(key_of[2], (CURVES, EPOCHS), 0, BUCKETS), jax.random.fold_in(key_of[2], 1), 0, BUCKETS - 1).astype(jnp.int32),
        "start_weight": scatter_about(key_of[3], (C, HALF), HALF ** -0.5, 3.5, (), jnp.float32),
        "conv_weight": scatter_about(key_of[4], (LAYERS, 2 * C, 3 * C), (3 * C) ** -0.5, 0.15625, ((1, 16),)),
        "gate_bias": scatter_about(key_of[5], (LAYERS, 2 * C), 1.0, 4.0, (), jnp.float32),
        "mix_first": scatter_about(key_of[6], (2 * C, C), C ** -0.5, 0.25, ((0, 16),)),
        "mix_last": scatter_about(key_of[7], (C, C), C ** -0.5, 0.25, ((0, 16),)),
        "end_weight": scatter_about(key_of[8], (BANDS, C), C ** -0.5, 0.25, (), jnp.float32),
        "cotangent": scatter_about(key_of[9], (CURVES, HALF, EPOCHS), ((EPOCHS * N_DP) ** -0.5), 0.0234375, ((0, 16), (2, 8)), jnp.float32),
    }


highest = lax.Precision.HIGHEST


def tap_stack(padded, bucket, dilation, reach_len, col_count):
    centre = lax.slice_in_dim(padded, reach_len, reach_len + col_count, axis=1)
    left_tap = lax.slice_in_dim(padded, reach_len - dilation, reach_len - dilation + col_count, axis=1)
    right_tap = lax.slice_in_dim(padded, reach_len + dilation, reach_len + dilation + col_count, axis=1)
    for shift_k in range(1, BUCKETS):
        chosen = (bucket == shift_k)[None, :]
        left_start = reach_len - dilation - shift_k
        right_start = reach_len + dilation + shift_k
        left_tap = jnp.where(chosen, lax.slice_in_dim(padded, left_start, left_start + col_count, axis=1), left_tap)
        right_tap = jnp.where(chosen, lax.slice_in_dim(padded, right_start, right_start + col_count, axis=1), right_tap)
    return jnp.concatenate([left_tap, centre, right_tap], axis=0)


def place_piece(piece, start_col, total_len):
    return jnp.pad(piece, ((0, 0), (start_col, total_len - start_col - piece.shape[1])))


def tap_transpose(d_stacked, bucket, dilation, reach_len, col_count, channels):
    total_len = col_count + 2 * reach_len
    d_left = d_stacked[:channels]
    d_centre = d_stacked[channels:2 * channels]
    d_right = d_stacked[2 * channels:]
    window = place_piece(d_centre, reach_len, total_len)
    for shift_k in range(BUCKETS):
        chosen = (bucket == shift_k)[None, :]
        left_part = jnp.where(chosen, d_left, 0.0)
        right_part = jnp.where(chosen, d_right, 0.0)
        window = window + place_piece(left_part, reach_len - dilation - shift_k, total_len)
        window = window + place_piece(right_part, reach_len + dilation + shift_k, total_len)
    return window


def gate_forward(preact):
    channels = preact.shape[0] // 2
    return jnp.tanh(preact[:channels]) * jax.nn.sigmoid(preact[channels:])


def gate_backward(preact, d_gated):
    channels = preact.shape[0] // 2
    tangent = jnp.tanh(preact[:channels])
    sigmoid_part = jax.nn.sigmoid(preact[channels:])
    d_upper = d_gated * sigmoid_part * (1.0 - tangent * tangent)
    d_lower = d_gated * tangent * sigmoid_part * (1.0 - sigmoid_part)
    return jnp.concatenate([d_upper, d_lower], axis=0).astype(jnp.bfloat16)


def contract_rows(left_op, right_op, precision=None):
    return lax.dot_general(left_op, right_op, (((1,), (1,)), ((), ())), precision=precision, preferred_element_type=jnp.float32)


def contract_cols(left_op, right_op, precision=None):
    return lax.dot_general(left_op, right_op, (((0,), (0,)), ((), ())), precision=precision, preferred_element_type=jnp.float32)


def one_curve(one_flux, length, bucket, cot_curve, weight_set):
    start_weight, conv_weight, gate_bias, mix_first, mix_last, end_weight = weight_set
    col_count = one_flux.shape[1]
    channels = start_weight.shape[0]
    dilations = (EPOCH_DEV // 4, EPOCH_DEV + EPOCH_DEV // 2)
    reaches = (dilations[0] + BUCKETS - 1, dilations[1] + BUCKETS - 1)
    valid_mask = (jnp.arange(col_count, dtype=jnp.int32) < length).astype(jnp.float32)
    first_half = one_flux[:HALF]
    second_half = one_flux[HALF:]
    hidden_first = (jnp.dot(start_weight, first_half, precision=highest) * valid_mask).astype(jnp.bfloat16)
    padded_first = jnp.pad(hidden_first, ((0, 0), (reaches[0], reaches[0])))
    stacked_first = tap_stack(padded_first, bucket, dilations[0], reaches[0], col_count)
    pre_first = jnp.dot(conv_weight[0], stacked_first, preferred_element_type=jnp.float32) + gate_bias[0][:, None]
    gated_first = gate_forward(pre_first).astype(jnp.bfloat16)
    mixed_first = jnp.dot(mix_first, gated_first, preferred_element_type=jnp.float32)
    hidden_second = ((hidden_first.astype(jnp.float32) + mixed_first[:channels]) * valid_mask).astype(jnp.bfloat16)
    padded_second = jnp.pad(hidden_second, ((0, 0), (reaches[1], reaches[1])))
    stacked_second = tap_stack(padded_second, bucket, dilations[1], reaches[1], col_count)
    pre_second = jnp.dot(conv_weight[1], stacked_second, preferred_element_type=jnp.float32) + gate_bias[1][:, None]
    gated_second = gate_forward(pre_second).astype(jnp.bfloat16)
    mixed_second = jnp.dot(mix_last, gated_second, preferred_element_type=jnp.float32)
    skip_total = mixed_first[channels:] + mixed_second
    end_out = jnp.dot(end_weight, skip_total, precision=highest)
    growth = jnp.exp(end_out[:HALF])
    coupled = (growth * second_half + end_out[HALF:]) * valid_mask

    d_coupled = cot_curve * valid_mask
    d_end = jnp.concatenate([d_coupled * growth * second_half, d_coupled], axis=0)
    grad_end = contract_rows(d_end, skip_total, highest)
    d_skip = contract_cols(end_weight, d_end, highest)
    d_skip_b = d_skip.astype(jnp.bfloat16)
    d_gated_second = contract_cols(mix_last, d_skip_b)
    grad_mix_last = contract_rows(d_skip_b, gated_second)
    dz_second = gate_backward(pre_second, d_gated_second)
    grad_conv_second = contract_rows(dz_second, stacked_second)
    bias_second = jnp.sum(dz_second.astype(jnp.float32), axis=1)
    d_stacked_second = contract_cols(conv_weight[1], dz_second)
    d_window_second = tap_transpose(d_stacked_second, bucket, dilations[1], reaches[1], col_count, channels)
    d_field_second = d_window_second[:, reaches[1]:reaches[1] + col_count]
    d_mixed_first = jnp.concatenate([d_field_second * valid_mask, d_skip], axis=0).astype(jnp.bfloat16)
    d_gated_first = contract_cols(mix_first, d_mixed_first)
    grad_mix_first = contract_rows(d_mixed_first, gated_first)
    dz_first = gate_backward(pre_first, d_gated_first)
    grad_conv_first = contract_rows(dz_first, stacked_first)
    bias_first = jnp.sum(dz_first.astype(jnp.float32), axis=1)
    d_stacked_first = contract_cols(conv_weight[0], dz_first)
    d_window_first = tap_transpose(d_stacked_first, bucket, dilations[0], reaches[0], col_count, channels)
    d_hidden_first = d_field_second * valid_mask + d_window_first[:, reaches[0]:reaches[0] + col_count]
    grad_start = contract_rows(d_hidden_first * valid_mask, first_half, highest)
    grads = (grad_start, jnp.stack([grad_conv_first, grad_conv_second]), jnp.stack([bias_first, bias_second]), grad_mix_first, grad_mix_last, grad_end)
    return coupled, grads


def reference(light_flux, lengths, offsets, start_weight, conv_weight, gate_bias, mix_first, mix_last, end_weight, cotangent):
    weight_set = (start_weight, conv_weight, gate_bias, mix_first, mix_last, end_weight)

    def step_fn(running, curve_items):
        one_flux, length, bucket, cot_curve = curve_items
        coupled, grads = one_curve(one_flux, length, bucket, cot_curve, weight_set)
        return tuple(first_term + second_term for first_term, second_term in zip(running, grads)), coupled

    zero_init = (
        jnp.zeros(start_weight.shape, jnp.float32),
        jnp.zeros(conv_weight.shape, jnp.float32),
        jnp.zeros(gate_bias.shape, jnp.float32),
        jnp.zeros(mix_first.shape, jnp.float32),
        jnp.zeros(mix_last.shape, jnp.float32),
        jnp.zeros(end_weight.shape, jnp.float32),
    )
    totals, coupled = lax.scan(step_fn, zero_init, (light_flux, lengths, offsets, cotangent))
    return (coupled, totals[0], totals[1], totals[2], totals[3], totals[4], totals[5])
```

```python
import functools

import jax
import jax.numpy as jnp
from jax import lax
from jax.experimental import pallas as pl
from jax.experimental.pallas import tpu as pltpu
from jax.sharding import PartitionSpec as P

BUCKETS = 4
highest = lax.Precision.HIGHEST
bf16 = jnp.bfloat16
f32 = jnp.float32


def dot(a, b, ca=1, cb=0, precision=None):
    return lax.dot_general(
        a, b, (((ca,), (cb,)), ((), ())), precision=precision, preferred_element_type=f32
    )


def split(x):
    hi = lax.reduce_precision(x, 8, 7)
    return hi.astype(bf16), (x - hi).astype(bf16)


def pad_to(x, rows, cols):
    return jnp.pad(x, ((0, rows - x.shape[0]), (0, cols - x.shape[1])))


def shift(x, n):
    total = x.shape[1]
    if n > 0:
        return jnp.pad(x[:, : total - n], ((0, 0), (n, 0)))
    return jnp.pad(x[:, -n:], ((0, 0), (0, -n)))


def tap_of(x, off, dilation, side):
    out = shift(x, side * dilation)
    for step in range(1, BUCKETS):
        out = jnp.where(off == step, shift(x, side * (dilation + step)), out)
    return out


def tap_back(x, off, dilation, side):
    out = 0.0
    for step in range(BUCKETS):
        out = out + shift(jnp.where(off == step, x, 0.0), -side * (dilation + step))
    return out


def exchange(x, axis):
    return lax.all_to_all(x, axis, 0, 0, tiled=True)


def nt(a, b):
    return dot(a, b, 1, 1)


def rolled(x, start, width):
    if start % 128 == 0:
        return x[:, start : start + width]
    return pltpu.roll(x, x.shape[1] - start, 1)[:, :width]


def valid_row(c, width, length):
    at = lax.broadcasted_iota(jnp.int32, (1, width), 1) + c * width
    return (at < length).astype(f32)


def forward_kernel(
    dil0, dil1, half,
    info, fields, a_cat, w_cat, mix, w_taps, bias1, e_pair,
    g0_out, du0_out, dv0_out, h1_out, s_out, gown_out, du1_out, dv1_out, packet,
    fpad, s_cat, prod, g_keep,
):
    i = pl.program_id(0)
    nb = fields.shape[0]
    bw = fields.shape[2]
    rows = gown_out.shape[0] // 2
    channels = mix.shape[0]
    pad0 = 256
    pad1 = dil1 + 128
    length = info[0]
    k = info[1]

    @pl.when(i == 0)
    def _():
        fpad[:, 0:pad0] = jnp.zeros((8, pad0), f32)
        fpad[:, pad0 + nb * bw :] = jnp.zeros((8, pad0), f32)
        prod[:, 0:pad1] = jnp.zeros((prod.shape[0], pad1), f32)
        prod[:, pad1 + nb * bw :] = jnp.zeros((prod.shape[0], pad1), f32)
        s_cat[...] = jnp.zeros(s_cat.shape, f32)
        s_cat[27:29, :] = jnp.ones((2, bw), f32)
        packet[:, 24:32, :] = jnp.zeros((nb, 8, bw), f32)
        for c in range(nb):
            block = fields[c].astype(f32)
            valid = valid_row(c, bw, length)
            at = slice(pad0 + c * bw, pad0 + (c + 1) * bw)
            fpad[0:half, at] = block[0:half] * valid
            fpad[half : 2 * half, at] = block[2 * half : 3 * half] * valid
            fpad[6:7, at] = block[6 * half : 6 * half + 1]
            fpad[7:8, at] = valid

    base = pl.multiple_of(i * bw, bw)
    near = fpad[:, pl.ds(pl.multiple_of(pad0 + base, 128), bw)]
    off = near[6:7]
    valid = near[7:8]
    behind = fpad[:, pl.ds(pl.multiple_of(base, 128), bw + 2 * dil0)]
    ahead = fpad[:, pl.ds(pl.multiple_of(pad0 + base, 128), bw + 2 * dil0)]
    left = rolled(behind, dil0, bw)
    right = rolled(ahead, dil0, bw)
    for step in range(1, BUCKETS):
        left = jnp.where(off == step, rolled(behind, dil0 - step, bw), left)
        right = jnp.where(off == step, rolled(ahead, dil0 + step, bw), right)
    for part, at in ((left, 0), (near, 3), (right, 6)):
        s_cat[at : at + half, :] = part[0:half]
        s_cat[9 + at : 9 + at + half, :] = part[half : 2 * half]
        s_cat[18 + at : 18 + at + half, :] = part[0:half]
    s_b = s_cat[...].astype(bf16)
    s_out[...] = s_b
    step_rows = 128
    for r in range(0, channels, step_rows):
        u = dot(a_cat[r : r + step_rows, :], s_b)
        v = dot(a_cat[channels + r : channels + r + step_rows, :], s_b)
        t = jnp.tanh(u)
        s = 0.5 * jnp.tanh(0.5 * v) + 0.5
        g = t * s
        g0_out[r : r + step_rows, :] = g.astype(bf16)
        du0_out[r : r + step_rows, :] = (s - g * t).astype(bf16)
        dv0_out[r : r + step_rows, :] = (g - g * s).astype(bf16)
    h1 = dot(mix[...], g0_out[...]) + dot(w_cat[...], s_b)
    h1 = (h1 * valid).astype(bf16)
    h1_out[...] = h1
    prod[:, pl.ds(pl.multiple_of(pad1 + base, 128), bw)] = dot(w_taps[...], h1)
    g_keep[:, pl.ds(base, bw)] = g0_out[pl.ds(pl.multiple_of(rows * k, rows), rows), :]

    @pl.when(i == nb - 1)
    def _():
        def body(c, carry):
            base = pl.multiple_of(c * bw, bw)
            off = fpad[6:7, pl.ds(pl.multiple_of(pad0 + base, 128), bw)]
            pair = 2 * rows
            window = bw + 128
            behind = prod[0:pair, pl.ds(pl.multiple_of(base, 128), window)]
            ahead = prod[2 * pair :, pl.ds(pl.multiple_of(pad1 + dil1 + base, 128), window)]
            left = rolled(behind, 128, bw)
            right = rolled(ahead, 0, bw)
            for step in range(1, BUCKETS):
                left = jnp.where(off == step, rolled(behind, 128 - step, bw), left)
                right = jnp.where(off == step, rolled(ahead, step, bw), right)
            centre = prod[pair : 2 * pair, pl.ds(pl.multiple_of(pad1 + base, 128), bw)]
            pre = left + centre + right + bias1[...]
            t = jnp.tanh(pre[:rows])
            s = 0.5 * jnp.tanh(0.5 * pre[rows:]) + 0.5
            g = t * s
            du1_out[:, pl.ds(base, bw)] = s - g * t
            dv1_out[:, pl.ds(base, bw)] = g - g * s
            gown_out[0:rows, pl.ds(base, bw)] = g_keep[:, pl.ds(base, bw)]
            gown_out[rows:, pl.ds(base, bw)] = g.astype(bf16)
            part = dot(e_pair[...], gown_out[:, pl.ds(base, bw)])
            part = part[0 : 2 * half] + part[8 : 8 + 2 * half]
            for d in range(nb):
                for h in range(half):
                    packet[d, pl.ds(h * nb + c, 1), :] = part[h : h + 1]
            packet[c, 24 : 24 + half, :] = part[half : 2 * half]
            return carry

        lax.fori_loop(0, nb, body, 0)


def backward_kernel(
    dil1, half,
    info, got, fields, flux, e_up, gown, du1, dv1, w_taps_t, mix_t,
    g0, du0, dv0, h1, s_in,
    coupled, packet,
    ends, d_cat, dz_pad, off_pad, d_e0, d_taps, acc_conv, acc_mix, acc_m, acc_s, acc_g, acc_b,
    dg, m_rows, share,
):
    i = pl.program_id(0)
    nb = fields.shape[0]
    bw = fields.shape[2]
    pair = gown.shape[0]
    rows = pair // 2
    channels = mix_t.shape[0]
    n_dp = packet.shape[0]
    pad1 = dil1 + 128
    length = info[0]
    k = info[1]

    @pl.when(i == 0)
    def _():
        for ref in (acc_conv, acc_mix, acc_m, acc_s, acc_g, acc_b, d_cat, m_rows, share):
            ref[...] = jnp.zeros(ref.shape, f32)
        dz_pad[:, 0:pad1] = jnp.zeros((pair, pad1), f32)
        dz_pad[:, pad1 + nb * bw :] = jnp.zeros((pair, pad1), f32)
        off_pad[:, 0:pad1] = jnp.full((8, pad1), -1.0, f32)
        off_pad[:, pad1 + nb * bw :] = jnp.full((8, pad1), -1.0, f32)
        total = got[0]
        for src in range(1, nb):
            total = total + got[src]
        ends[...] = total
        mine = valid_row(k, bw, length)
        for h in range(half):
            growth = jnp.exp(ends[pl.ds(h * nb + k, 1), :])
            coupled[0, h : h + 1, :] = (
                growth * flux[half + h : half + h + 1] + ends[24 + h : 25 + h, :]
            ) * mine

        def first(c, carry):
            base = pl.multiple_of(c * bw, bw)
            at = pl.multiple_of(pad1 + base, 128)
            block = fields[c].astype(f32)
            valid = valid_row(c, bw, length)
            off_pad[0:1, pl.ds(at, bw)] = block[6 * half : 6 * half + 1]
            flux2 = block[half : 2 * half] + block[3 * half : 4 * half]
            cot = (block[4 * half : 5 * half] + block[5 * half : 6 * half]) * valid
            for h in range(half):
                growth = jnp.exp(ends[pl.ds(h * nb + c, 1), :])
                d_cat[h : h + 1, :] = cot[h : h + 1] * growth * flux2[h : h + 1]
            d_cat[half : 2 * half, :] = cot
            full = d_cat[0:8, :]
            hi = full.astype(bf16).astype(f32)
            lo = full - hi
            d_cat[8:16, :] = lo
            d_cat[16:24, :] = hi
            d_gated = dot(e_up[...], d_cat[...].astype(bf16))
            acc_g[...] += nt(d_cat[8:24, :].astype(bf16), gown[:, pl.ds(base, bw)])
            d_e0[:, pl.ds(base, bw)] = d_gated[:rows]
            up = d_gated[rows : 2 * rows]
            dz_pad[0:rows, pl.ds(at, bw)] = up * du1[:, pl.ds(base, bw)]
            dz_pad[rows:, pl.ds(at, bw)] = up * dv1[:, pl.ds(base, bw)]
            return carry

        lax.fori_loop(0, nb, first, 0)

        def second(c, carry):
            base = pl.multiple_of(c * bw, bw)
            window = bw + 128
            ahead = dz_pad[:, pl.ds(pl.multiple_of(pad1 + dil1 + base, 128), window)]
            off_a = off_pad[0:1, pl.ds(pl.multiple_of(pad1 + dil1 + base, 128), window)]
            behind = dz_pad[:, pl.ds(base, window)]
            off_b = off_pad[0:1, pl.ds(base, window)]
            left = 0.0
            right = 0.0
            for step in range(BUCKETS):
                left = left + rolled(jnp.where(off_a == step, ahead, 0.0), step, bw)
                right = right + rolled(jnp.where(off_b == step, behind, 0.0), 128 - step, bw)
            centre = dz_pad[:, pl.ds(pl.multiple_of(pad1 + base, 128), bw)].astype(bf16)
            d_taps[0:pair, pl.ds(base, bw)] = left.astype(bf16)
            d_taps[pair : 2 * pair, pl.ds(base, bw)] = centre
            d_taps[2 * pair :, pl.ds(base, bw)] = right.astype(bf16)
            acc_b[...] += nt(jnp.ones((16, bw), bf16), centre)
            return carry

        lax.fori_loop(0, nb, second, 0)

    base = pl.multiple_of(i * bw, bw)
    d_blk = d_taps[:, pl.ds(base, bw)]
    acc_conv[...] += nt(d_blk, h1[...])
    field = (dot(w_taps_t[...], d_blk) * valid_row(i, bw, length)).astype(bf16)
    s_b = s_in[...]
    acc_mix[...] += nt(field, g0[...])
    acc_s[...] += nt(s_b, field)
    dg[...] = dot(mix_t[...], field)
    own = pl.ds(pl.multiple_of(rows * k, rows), rows)
    dg[own, :] = dg[own, :] + d_e0[:, pl.ds(base, bw)]
    up = dg[...]
    acc_m[:, 0:channels] += nt(s_b, (up * du0[...].astype(f32)).astype(bf16))
    acc_m[:, channels:] += nt(s_b, (up * dv0[...].astype(f32)).astype(bf16))

    @pl.when(i == nb - 1)
    def _():
        per_mix = channels // n_dp
        eighth = pair // n_dp
        m_rows[0:9, :] = acc_m[0:9, :] + acc_m[9:18, :]
        m_rows[9:10, :] = acc_m[27:28, :]
        starts = acc_s[3 : 3 + half, :] + acc_s[12 : 12 + half, :]
        share[0:1, 0:128] = acc_b[0:1, :]
        share[0 : 2 * half, 128:256] = acc_g[8 : 8 + 2 * half, :] + acc_g[0 : 2 * half, :]
        for j in range(n_dp):
            row = 64 * (j % (n_dp // 2)) + per_mix * (j // (n_dp // 2))
            packet[j, 0:per_mix, :] = acc_mix[row : row + per_mix, :].astype(bf16)
            for tap in range(3):
                at = per_mix + tap * eighth
                row = tap * pair + j * eighth
                packet[j, at : at + eighth, :] = acc_conv[row : row + eighth, :].astype(bf16)
            if j < channels // 128:
                share[1 : 1 + half, 0:128] = starts[:, 128 * j : 128 * (j + 1)]
            else:
                share[1 : 1 + half, 0:128] = jnp.zeros((half, 128), f32)
            at = per_mix + 3 * eighth
            cols = slice(128 * (j // 2), 128 * (j // 2) + 128)
            share[6:8, 0:128] = m_rows[8:10, cols]
            packet[j, at : at + 8, 0:128] = m_rows[0:8, cols].astype(bf16)
            packet[j, at : at + 8, 128:256] = share[:, 0:128].astype(bf16)
            packet[j, at : at + 8, 256:384] = share[:, 128:256].astype(bf16)
            packet[j, at : at + 8, 384:512] = jnp.zeros((8, 128), bf16)


def whole(shape):
    return pl.BlockSpec(shape, lambda i: (0,) * len(shape))


def columns(rows, width):
    return pl.BlockSpec((rows, width), lambda i: (0, i))


def local(
    light_flux,
    lengths,
    offsets,
    start_weight,
    conv_weight,
    gate_bias,
    mix_first,
    mix_last,
    end_weight,
    cotangent,
):
    n_dp = lax.axis_size("dp")
    n_ctx = lax.axis_size("ctx")
    half_dp = n_dp // 2
    dp = lax.axis_index("dp")
    k = lax.axis_index("ctx")
    low = dp < half_dp
    shard_len = light_flux.shape[2]
    half = light_flux.shape[1] // 2
    channels = start_weight.shape[0]
    epochs = shard_len * n_ctx
    dilations = (shard_len // 4, shard_len + shard_len // 2)
    rows = conv_weight.shape[1]
    last_rows = mix_last.shape[0]
    conv0, conv1 = conv_weight[0], conv_weight[1]
    part = rows // n_ctx
    n_e = 2 * half

    def strided(x):
        lead = x.shape[0]
        cols = x.shape[1]
        view = x.reshape(lead, cols // rows, n_ctx, part)
        return lax.dynamic_slice(
            view, (0, 0, k, 0), (lead, cols // rows, 1, part)
        ).reshape(lead, cols // n_ctx)

    flux_hi, flux_lo = split(light_flux[0])
    cot_hi, cot_lo = split(cotangent[0])
    n_in = 6 * half + 1
    inputs = jnp.concatenate(
        [flux_hi, flux_lo, cot_hi, cot_lo, offsets.astype(bf16)], axis=0
    )
    n_pad = -(-n_in // 8) * 8
    inputs = pad_to(inputs, n_pad, shard_len)

    sw_hi, sw_lo = split(start_weight)
    sw_pair = jnp.concatenate([sw_hi, sw_lo], axis=1)
    a_rows = []
    for tap in range(3):
        parts = dot(sw_pair, conv0[:, tap * channels : (tap + 1) * channels], 0, 1)
        a_rows.append(parts[:half] + parts[half:])
    a_own = jnp.concatenate(a_rows, axis=0)
    ew_last = lax.dynamic_slice(end_weight, (0, last_rows * dp), (n_e, last_rows))
    ew_skip = lax.dynamic_slice(
        end_weight, (0, rows * jnp.maximum(dp - half_dp, 0)), (n_e, rows)
    )
    ew_skip = jnp.where(low, 0.0, ew_skip)
    mix_last_k = strided(mix_last).astype(f32)
    mix_skip_k = lax.dynamic_slice(mix_first, (0, rows * k), (rows, rows)).astype(f32)
    e_own = jnp.concatenate(
        [
            dot(ew_skip, mix_skip_k, precision=highest),
            dot(ew_last, mix_last_k, precision=highest),
        ],
        axis=1,
    )
    a_hi, a_lo = split(a_own)
    e_hi, e_lo = split(e_own)
    a_block = pad_to(jnp.concatenate([a_hi, a_lo], axis=0), 20, rows).reshape(5, 4 * rows)
    small = jnp.concatenate(
        [pad_to(jnp.concatenate([e_hi, e_lo], axis=1), 8, 4 * rows), pad_to(a_block, 8, 4 * rows)],
        axis=1,
    )
    conv_k = lax.dynamic_slice(conv1, (part * k, 0), (part, 3 * channels))
    mix_k = lax.dynamic_slice(mix_first, (part * k, 0), (part, channels))
    packet = jnp.concatenate(
        [conv_k[:, tap * channels : (tap + 1) * channels] for tap in range(3)] + [mix_k, small],
        axis=0,
    )
    per = packet.shape[0]
    got = exchange(
        jnp.broadcast_to(packet[None], (n_dp, per, channels)).reshape(n_dp * per, channels), "dp"
    ).reshape(n_dp, per, channels)
    w_taps = got[:, : 3 * part].reshape(n_dp, 3, part, channels).transpose(1, 0, 2, 3)
    w_taps = w_taps.reshape(6 * rows, channels)
    mix_part = got[:half_dp, 3 * part : 4 * part].reshape(rows, channels)
    both = jnp.concatenate([inputs, mix_part], axis=0)
    ctx_got = exchange(
        jnp.broadcast_to(both[None], (n_ctx,) + both.shape).reshape(-1, channels), "ctx"
    ).reshape((n_ctx,) + both.shape)
    fields = ctx_got[:, :n_pad]
    mix_res = ctx_got[:, n_pad:].reshape(n_ctx, half_dp, part, channels).transpose(1, 0, 2, 3)
    mix_res = mix_res.reshape(channels, channels)
    e_k = got[:, 4 * part : 4 * part + n_e, : 4 * rows].astype(f32).sum(axis=0)
    e_cat = e_k[:, : 2 * rows] + e_k[:, 2 * rows :]
    a_all = got[:, 4 * part : 4 * part + 5, 4 * rows :].reshape(n_dp, 20, rows)
    a_all = a_all[:, :18].transpose(1, 0, 2).reshape(18, n_dp * rows)
    a_hi, a_lo = a_all[:9], a_all[9:]

    length = lengths[0]
    b_hi, b_lo = split(gate_bias[0][None])
    a_cat = jnp.concatenate(
        [a_hi, a_hi, a_lo, b_hi, b_lo, jnp.zeros((3, 2 * channels), bf16)], axis=0
    ).T
    gap = jnp.zeros((6, channels), bf16)
    w_cat = jnp.concatenate(
        [gap[:3], sw_hi.T, gap, sw_hi.T, gap, sw_lo.T, gap[:3], gap[:5]], axis=0
    ).T
    ec_hi, ec_lo = split(e_cat)
    gap = jnp.zeros((2, 2 * rows), bf16)
    e_pair = jnp.concatenate([ec_hi, gap, ec_lo, gap], axis=0)
    e_up = pad_to(jnp.concatenate([ec_hi, gap, ec_hi, gap, ec_lo], axis=0), 32, 2 * rows).T
    bias1 = strided(gate_bias[1][None]).T
    info = jnp.stack([length, k])
    pair = 2 * rows
    wide = epochs + 2 * (dilations[1] + 128)
    smem = pl.BlockSpec(memory_space=pltpu.SMEM)
    shapes = jax.ShapeDtypeStruct
    params = pltpu.CompilerParams(
        dimension_semantics=("arbitrary",), vmem_limit_bytes=60000 * 1024
    )
    forward = pl.pallas_call(
        functools.partial(forward_kernel, dilations[0], dilations[1], half),
        grid=(n_ctx,),
        in_specs=[
            smem,
            whole((n_ctx, n_pad, shard_len)),
            whole(a_cat.shape),
            whole(w_cat.shape),
            whole(mix_res.shape),
            whole(w_taps.shape),
            whole(bias1.shape),
            whole(e_pair.shape),
        ],
        out_specs=[columns(channels, shard_len)] * 4
        + [columns(32, shard_len), whole((pair, epochs)), whole((rows, epochs)),
           whole((rows, epochs)), whole((n_ctx, 32, shard_len))],
        out_shape=[shapes((channels, epochs), bf16)] * 4
        + [shapes((32, epochs), bf16), shapes((pair, epochs), bf16), shapes((rows, epochs), f32),
           shapes((rows, epochs), f32), shapes((n_ctx, 32, shard_len), f32)],
        scratch_shapes=[
            pltpu.VMEM((8, epochs + 512), f32),
            pltpu.VMEM((32, shard_len), f32),
            pltpu.VMEM((3 * pair, wide), f32),
            pltpu.VMEM((rows, epochs), bf16),
        ],
        compiler_params=params,
        name="layers_forward",
    )
    g0, du0, dv0, h1, s_all, g_own, du1, dv1, packed = forward(
        info, fields, a_cat, w_cat, mix_res, w_taps, bias1, e_pair
    )
    got = exchange(packed.reshape(n_ctx * 32, shard_len), "ctx").reshape(n_ctx, 32, shard_len)

    n_mix = channels // n_dp
    n_conv = 3 * pair // n_dp
    per = n_mix + n_conv + 8
    backward = pl.pallas_call(
        functools.partial(backward_kernel, dilations[1], half),
        grid=(n_ctx,),
        in_specs=[
            smem,
            whole((n_ctx, 32, shard_len)),
            whole((n_ctx, n_pad, shard_len)),
            whole((2 * half, shard_len)),
            whole((pair, 32)),
            whole((pair, epochs)),
            whole((rows, epochs)),
            whole((rows, epochs)),
            whole((channels, 3 * pair)),
            whole((channels, channels)),
        ]
        + [columns(channels, shard_len)] * 4
        + [columns(32, shard_len)],
        out_specs=[whole((1, half, shard_len)), whole((n_dp, per, channels))],
        out_shape=[shapes((1, half, shard_len), f32), shapes((n_dp, per, channels), bf16)],
        scratch_shapes=[
            pltpu.VMEM((32, shard_len), f32),
            pltpu.VMEM((32, shard_len), f32),
            pltpu.VMEM((pair, wide), f32),
            pltpu.VMEM((8, wide), f32),
            pltpu.VMEM((rows, epochs), f32),
            pltpu.VMEM((3 * pair, epochs), bf16),
            pltpu.VMEM((3 * pair, channels), f32),
            pltpu.VMEM((channels, channels), f32),
            pltpu.VMEM((32, 2 * channels), f32),
            pltpu.VMEM((32, channels), f32),
            pltpu.VMEM((16, pair), f32),
            pltpu.VMEM((16, pair), f32),
            pltpu.VMEM((channels, shard_len), f32),
            pltpu.VMEM((16, 2 * channels), f32),
            pltpu.VMEM((8, 256), f32),
        ],
        compiler_params=params,
        name="layers_backward",
    )
    coupled, packed = backward(
        info, got, fields, light_flux[0], e_up, g_own, du1, dv1, w_taps.T, mix_res.T,
        g0, du0, dv0, h1, s_all,
    )
    got = exchange(packed.reshape(n_dp * per, channels), "dp").reshape(n_dp, per, channels)
    got = got.astype(f32).sum(axis=0)
    mix_piece = got[:n_mix]
    conv_piece = got[n_mix : n_mix + n_conv].astype(bf16)
    smalls = got[n_mix + n_conv :]
    near = lax.dynamic_slice(smalls, (0, rows * (dp % 2)), (8, rows))
    far = lax.dynamic_slice(smalls, (6, 128 + rows * (dp % 2)), (2, rows))
    m_own = jnp.concatenate([near, far], axis=0)
    start_own = jnp.where(dp < channels // 128, smalls[1 : 1 + half, 128:256], 0.0)
    g_own_sum = smalls[: 2 * half, 256:384]
    bias1_own = smalls[0:1, 128:256]
    mo_hi, mo_lo = split(m_own)
    mo_pair = jnp.concatenate([mo_hi[:9], mo_lo[:9]], axis=0)
    start_t = 0.0
    for tap in range(3):
        up = dot(mo_pair, conv0[:, tap * channels : (tap + 1) * channels])
        start_t = start_t + up[half * tap : half * tap + half] + up[9 + half * tap : 9 + half * tap + half]
    spot = lax.dynamic_update_slice(
        jnp.zeros((half, channels), f32), start_own, (0, 128 * (dp % (channels // 128)))
    )
    start_t = start_t + spot
    end_last = dot(g_own_sum[:, rows:], mix_last_k, 1, 1, highest)
    end_skip = jnp.where(low, 0.0, dot(g_own_sum[:, :rows], mix_skip_k, 1, 1, highest))
    g_rows = jnp.concatenate([g_own_sum, bias1_own], axis=0)
    parts = jnp.concatenate(
        [
            m_own,
            pad_to(g_rows, 10, 2 * rows),
            pad_to(jnp.concatenate([end_last, end_skip], axis=1), 10, last_rows + rows),
        ],
        axis=1,
    )
    width = parts.shape[1]
    pack_rows = [
        conv_piece,
        mix_piece.astype(bf16),
        pad_to(parts, 10, channels).astype(bf16),
        start_t.astype(bf16),
    ]
    packed = jnp.concatenate(pack_rows, axis=0)
    per0 = packed.shape[0]
    per = -(-per0 // 8) * 8
    packed = pad_to(packed, per, channels)
    got = exchange(
        jnp.broadcast_to(packed[None], (n_ctx, per, channels)).reshape(n_ctx * per, channels), "ctx"
    ).reshape(n_ctx, per, channels)
    grad_conv1 = got[:, :n_conv].reshape(n_ctx, 3, part, channels).transpose(0, 2, 1, 3)
    grad_conv1 = grad_conv1.reshape(rows, 3 * channels).astype(f32)
    mix_rows = got[:, n_conv : n_conv + n_mix].astype(f32).sum(axis=0)
    base = n_conv + n_mix
    parts = got[:, base : base + 10, :width].astype(f32)
    start_t = got[:, base + 10 : base + 10 + half].astype(f32).sum(axis=0)
    m_own = parts[:, :, :rows].sum(axis=0)
    g_all = parts[:, : 2 * half, rows : 3 * rows]
    g0_all = g_all[:, :, :rows].transpose(1, 0, 2).reshape(2 * half, channels)
    g1_all = g_all[:, :, rows:].reshape(n_ctx, 2 * half, half_dp, part).transpose(1, 2, 0, 3)
    g1_all = g1_all.reshape(2 * half, channels)
    bias1_all = parts[:, 2 * half, rows : 3 * rows].reshape(n_ctx, n_dp, part).transpose(1, 0, 2)
    bias1_all = bias1_all.reshape(2 * channels)
    end_both = parts[:, : 2 * half, 3 * rows :].sum(axis=0)
    a_grad = m_own[:9].T
    grad_conv0 = jnp.concatenate(
        [
            dot(a_grad[:, half * tap : half * tap + half], start_weight, 1, 1, highest)
            for tap in range(3)
        ],
        axis=1,
    )
    grad_mix_last = dot(ew_last, g1_all, 0, 0, highest)
    skip_rows = dot(ew_skip, g0_all, 0, 0, highest)

    other = lax.ppermute(mix_rows, "dp", [(i + half_dp, i) for i in range(half_dp)])
    final = jnp.concatenate(
        [
            start_t.reshape(-1, 128),
            pad_to(end_both, 2 * half, 128),
            pad_to(m_own[9:10], 1, 128),
        ],
        axis=0,
    )
    per0 = final.shape[0]
    per = -(-per0 // 8) * 8
    final = pad_to(final, per, 128)
    got = exchange(
        jnp.broadcast_to(final[None], (n_dp, per, 128)).reshape(n_dp * per, 128), "dp"
    ).reshape(n_dp, per, 128)
    n_start = half * channels // 128
    grad_start = got[:, :n_start].sum(axis=0).reshape(half, channels).T
    ends = got[:, n_start : n_start + 2 * half]
    grad_end = ends[:, :, :last_rows].transpose(1, 0, 2).reshape(2 * half, channels)
    grad_end = grad_end + ends[half_dp:, :, last_rows : last_rows + rows].transpose(
        1, 0, 2
    ).reshape(2 * half, channels)
    bias0_all = got[:, n_start + 2 * half, :rows].reshape(2 * channels)
    grad_bias = jnp.stack([bias0_all, bias1_all])
    residual = jnp.concatenate([mix_rows, other], axis=0)
    grad_mix_first = jnp.where(low, residual, skip_rows)
    grad_conv = jnp.stack([grad_conv0, grad_conv1])
    return (coupled, grad_start, grad_conv, grad_bias, grad_mix_first, grad_mix_last, grad_end)


def solution(mesh):
    in_specs = (
        P("dp", None, "ctx"),
        P("dp"),
        P("dp", "ctx"),
        P(),
        P(None, "dp", None),
        P(),
        P("dp", None),
        P("dp", None),
        P(),
        P("dp", None, "ctx"),
    )
    out_specs = (
        P("dp", None, "ctx"),
        P(),
        P(None, "dp", None),
        P(),
        P("dp", None),
        P("dp", None),
        P(),
    )
    return jax.shard_map(local, mesh=mesh, in_specs=in_specs, out_specs=out_specs, check_vma=False)
```

```python
import functools

import jax
import jax.numpy as jnp
from jax import lax
from jax.experimental import pallas as pl
from jax.experimental.pallas import tpu as pltpu
from jax.sharding import PartitionSpec as P

BUCKETS = 4
highest = lax.Precision.HIGHEST
bf16 = jnp.bfloat16
f32 = jnp.float32


def dot(a, b, ca=1, cb=0, precision=None):
    return lax.dot_general(
        a, b, (((ca,), (cb,)), ((), ())), precision=precision, preferred_element_type=f32
    )


def split(x):
    hi = lax.reduce_precision(x, 8, 7)
    return hi.astype(bf16), (x - hi).astype(bf16)


def pad_to(x, rows, cols):
    return jnp.pad(x, ((0, rows - x.shape[0]), (0, cols - x.shape[1])))


def shift(x, n):
    total = x.shape[1]
    if n > 0:
        return jnp.pad(x[:, : total - n], ((0, 0), (n, 0)))
    return jnp.pad(x[:, -n:], ((0, 0), (0, -n)))


def tap_of(x, off, dilation, side):
    out = shift(x, side * dilation)
    for step in range(1, BUCKETS):
        out = jnp.where(off == step, shift(x, side * (dilation + step)), out)
    return out


def tap_back(x, off, dilation, side):
    out = 0.0
    for step in range(BUCKETS):
        out = out + shift(jnp.where(off == step, x, 0.0), -side * (dilation + step))
    return out


def exchange(x, axis):
    return lax.all_to_all(x, axis, 0, 0, tiled=True)


def nt(a, b):
    return dot(a, b, 1, 1)


def rolled(x, start, width):
    if start % 128 == 0:
        return x[:, start : start + width]
    return pltpu.roll(x, x.shape[1] - start, 1)[:, :width]


def steps_apart(shape):
    return (
        lax.broadcasted_iota(jnp.int32, shape, 0) - lax.broadcasted_iota(jnp.int32, shape, 1)
    ).astype(f32)


def one_hot(apart, target):
    return jnp.where(apart == target, 1.0, 0.0).astype(bf16)


def valid_row(c, width, length):
    at = lax.broadcasted_iota(jnp.int32, (1, width), 1) + c * width
    return (at < length).astype(f32)


def forward_kernel(
    dil0, dil1, half,
    info, fields, a_cat, w_hi, w_lo, mix, w_taps, bias1, e_pair,
    g0_out, du0_out, dv0_out, s_out, gown_out, du1_out, dv1_out, packet,
    fpad, s_cat, prod, centre, pre_s, g_keep, w_mix, w_start,
):
    i = pl.program_id(0)
    nb = fields.shape[0]
    bw = fields.shape[2]
    rows = gown_out.shape[0] // 2
    channels = mix.shape[0]
    pad0 = 256
    pad1 = dil1 + 128
    length = info[0]
    k = info[1]

    @pl.when(i == 0)
    def _():
        fpad[:, 0:pad0] = jnp.zeros((8, pad0), f32)
        fpad[:, pad0 + nb * bw :] = jnp.zeros((8, pad0), f32)
        prod[:, 0:pad1] = jnp.zeros((prod.shape[0], pad1), bf16)
        prod[:, pad1 + nb * bw :] = jnp.zeros((prod.shape[0], pad1), bf16)
        w_mix[...] = dot(w_taps[...], mix[...]).astype(bf16)
        full = dot(w_taps[...], w_hi[...]) + dot(w_taps[...], w_lo[...])
        top = full.astype(bf16).astype(f32)
        col = lax.broadcasted_iota(jnp.int32, full.shape, 1)
        w_start[...] = jnp.where(col < 18, top, full - top).astype(bf16)
        s_cat[...] = jnp.zeros(s_cat.shape, f32)
        s_cat[27:29, :] = jnp.ones((2, bw), f32)
        packet[:, 24:32, :] = jnp.zeros((nb, 8, bw), f32)
        for c in range(nb):
            block = fields[c ^ k].astype(f32)
            valid = valid_row(c, bw, length)
            at = slice(pad0 + c * bw, pad0 + (c + 1) * bw)
            fpad[0:half, at] = block[0:half] * valid
            fpad[half : 2 * half, at] = block[2 * half : 3 * half] * valid
            fpad[6:7, at] = block[6 * half : 6 * half + 1]
            fpad[7:8, at] = valid

    base = pl.multiple_of(i * bw, bw)
    near = fpad[:, pl.ds(pl.multiple_of(pad0 + base, 128), bw)]
    off = near[6:7]
    valid = near[7:8]
    behind = fpad[:, pl.ds(pl.multiple_of(base, 128), bw + 2 * dil0)]
    ahead = fpad[:, pl.ds(pl.multiple_of(pad0 + base, 128), bw + 2 * dil0)]
    left = rolled(behind, dil0, bw)
    right = rolled(ahead, dil0, bw)
    for step in range(1, BUCKETS):
        left = jnp.where(off == step, rolled(behind, dil0 - step, bw), left)
        right = jnp.where(off == step, rolled(ahead, dil0 + step, bw), right)
    for part, at in ((left, 0), (near, 3), (right, 6)):
        s_cat[at : at + half, :] = part[0:half]
        s_cat[9 + at : 9 + at + half, :] = part[half : 2 * half]
        s_cat[18 + at : 18 + at + half, :] = part[0:half]
    s_b = s_cat[...].astype(bf16)
    s_out[...] = s_b
    step_rows = 128
    for r in range(0, channels, step_rows):
        u = dot(a_cat[r : r + step_rows, :], s_b)
        v = dot(a_cat[channels + r : channels + r + step_rows, :], s_b)
        t = jnp.tanh(u)
        s = 0.5 * jnp.tanh(0.5 * v) + 0.5
        g = t * s
        g0_out[r : r + step_rows, :] = (g * valid).astype(bf16)
        du0_out[r : r + step_rows, :] = (s - g * t).astype(bf16)
        dv0_out[r : r + step_rows, :] = (g - g * s).astype(bf16)
    pair = 2 * rows
    g_b = g0_out[...]
    for tap in range(3):
        at = slice(tap * pair, (tap + 1) * pair)
        part = dot(w_mix[at, :], g_b) + dot(w_start[at, :], s_b)
        if tap == 1:
            centre[:, pl.ds(base, bw)] = part
        else:
            to = tap // 2 * pair
            cols = pl.ds(pl.multiple_of(pad1 + base, 128), bw)
            prod[to : to + pair, cols] = part.astype(bf16)
    g_keep[:, pl.ds(base, bw)] = g0_out[pl.ds(pl.multiple_of(rows * k, rows), rows), :]

    @pl.when(i == nb - 1)
    def _():
        apart = steps_apart((256, 128))

        def body(c, carry):
            base = pl.multiple_of(c * bw, bw)
            off = fpad[6:7, pl.ds(pl.multiple_of(pad0 + base, 128), bw)]
            for tile in range(bw // 128):
                lane = slice(tile * 128, (tile + 1) * 128)
                behind = prod[0:pair, pl.ds(pl.multiple_of(base + tile * 128, 128), 256)]
                ahead = prod[
                    pair:,
                    pl.ds(pl.multiple_of(pad1 + dil1 + base + tile * 128, 128), 256),
                ]
                pre_s[:, lane] = dot(behind, one_hot(apart, 128.0 - off[:, lane])) + dot(
                    ahead, one_hot(apart, off[:, lane])
                )
            pre = pre_s[...] + centre[:, pl.ds(base, bw)] + bias1[...]
            t = jnp.tanh(pre[:rows])
            s = 0.5 * jnp.tanh(0.5 * pre[rows:]) + 0.5
            g = t * s
            du1_out[:, pl.ds(base, bw)] = s - g * t
            dv1_out[:, pl.ds(base, bw)] = g - g * s
            gown_out[0:rows, pl.ds(base, bw)] = g_keep[:, pl.ds(base, bw)]
            gown_out[rows:, pl.ds(base, bw)] = g.astype(bf16)
            part = dot(e_pair[...], gown_out[:, pl.ds(base, bw)])
            part = part[0 : 2 * half] + part[8 : 8 + 2 * half]
            for d in range(nb):
                for h in range(half):
                    packet[d, pl.ds(h * nb + c, 1), :] = part[h : h + 1]
            packet[c, 24 : 24 + half, :] = part[half : 2 * half]
            return carry

        lax.fori_loop(0, nb, body, 0)


def backward_kernel(
    dil1, half,
    info, got, fields, flux, e_up, gown, du1, dv1, w_taps, w_taps_t, mix, w_mix_t, w_start,
    g0, du0, dv0, s_in,
    coupled, packet,
    ends, d_cat, dz_pad, off_pad, d_e0, d_taps, acc_q, acc_mix, acc_m, acc_s, acc_g, acc_b,
    dg, m_rows, share, acc_conv, small,
):
    i = pl.program_id(0)
    nb = fields.shape[0]
    bw = fields.shape[2]
    pair = gown.shape[0]
    rows = pair // 2
    channels = mix.shape[0]
    n_dp = packet.shape[0]
    pad1 = dil1 + 128
    length = info[0]
    k = info[1]

    @pl.when(i == 0)
    def _():
        for ref in (acc_q, acc_m, acc_s, acc_g, acc_b, d_cat, m_rows, share, small):
            ref[...] = jnp.zeros(ref.shape, f32)
        dz_pad[:, 0:pad1] = jnp.zeros((pair, pad1), bf16)
        dz_pad[:, pad1 + nb * bw :] = jnp.zeros((pair, pad1), bf16)
        off_pad[:, 0:pad1] = jnp.full((8, pad1), -1.0, f32)
        off_pad[:, pad1 + nb * bw :] = jnp.full((8, pad1), -1.0, f32)
        total = got[0]
        for src in range(1, nb):
            total = total + got[src]
        ends[...] = total
        mine = valid_row(k, bw, length)
        for h in range(half):
            growth = jnp.exp(ends[pl.ds(h * nb + k, 1), :])
            coupled[0, h : h + 1, :] = (
                growth * flux[half + h : half + h + 1] + ends[24 + h : 25 + h, :]
            ) * mine

        def first(c, carry):
            base = pl.multiple_of(c * bw, bw)
            at = pl.multiple_of(pad1 + base, 128)
            block = fields[c ^ k].astype(f32)
            valid = valid_row(c, bw, length)
            off_pad[0:1, pl.ds(at, bw)] = block[6 * half : 6 * half + 1]
            flux2 = block[half : 2 * half] + block[3 * half : 4 * half]
            cot = (block[4 * half : 5 * half] + block[5 * half : 6 * half]) * valid
            for h in range(half):
                growth = jnp.exp(ends[pl.ds(h * nb + c, 1), :])
                d_cat[h : h + 1, :] = cot[h : h + 1] * growth * flux2[h : h + 1]
            d_cat[half : 2 * half, :] = cot
            full = d_cat[0:8, :]
            hi = full.astype(bf16).astype(f32)
            lo = full - hi
            d_cat[8:16, :] = lo
            d_cat[16:24, :] = hi
            d_gated = dot(e_up[...], d_cat[...].astype(bf16))
            acc_g[...] += nt(d_cat[8:24, :].astype(bf16), gown[:, pl.ds(base, bw)])
            d_e0[:, pl.ds(base, bw)] = d_gated[:rows]
            up = d_gated[rows : 2 * rows]
            dz_pad[0:rows, pl.ds(at, bw)] = (up * du1[:, pl.ds(base, bw)]).astype(bf16)
            dz_pad[rows:, pl.ds(at, bw)] = (up * dv1[:, pl.ds(base, bw)]).astype(bf16)
            return carry

        lax.fori_loop(0, nb, first, 0)

        apart = steps_apart((128, 256))

        def second(c, carry):
            base = pl.multiple_of(c * bw, bw)
            valid = valid_row(c, bw, length)
            for tile in range(bw // 128):
                lane = pl.ds(pl.multiple_of(base + tile * 128, 128), 128)
                late = pl.ds(pl.multiple_of(pad1 + dil1 + base + tile * 128, 128), 256)
                early = pl.ds(pl.multiple_of(base + tile * 128, 128), 256)
                left = nt(dz_pad[:, late], one_hot(apart, -off_pad[0:1, late]))
                right = nt(dz_pad[:, early], one_hot(apart, off_pad[0:1, early] - 128.0))
                d_taps[0:pair, lane] = left.astype(bf16)
                d_taps[2 * pair :, lane] = (
                    right * valid[:, tile * 128 : (tile + 1) * 128]
                ).astype(bf16)
            centre = dz_pad[:, pl.ds(pl.multiple_of(pad1 + base, 128), bw)]
            d_taps[pair : 2 * pair, pl.ds(base, bw)] = centre
            acc_b[...] += nt(jnp.ones((16, bw), bf16), centre)
            return carry

        lax.fori_loop(0, nb, second, 0)

    base = pl.multiple_of(i * bw, bw)
    d_blk = d_taps[:, pl.ds(base, bw)]
    s_b = s_in[...]
    acc_q[...] += nt(d_blk, g0[...])
    acc_s[...] += nt(s_b, d_blk)
    dg[...] = dot(w_mix_t[...], d_blk)
    own = pl.ds(pl.multiple_of(rows * k, rows), rows)
    dg[own, :] = dg[own, :] + d_e0[:, pl.ds(base, bw)]
    up = dg[...]
    acc_m[:, 0:channels] += nt(s_b, (up * du0[...].astype(f32)).astype(bf16))
    acc_m[:, channels:] += nt(s_b, (up * dv0[...].astype(f32)).astype(bf16))

    @pl.when(i == nb - 1)
    def _():
        per_mix = channels // n_dp
        eighth = pair // n_dp
        q = acc_q[...]
        q_hi = q.astype(bf16)
        q_lo = (q - q_hi.astype(f32)).astype(bf16)
        small[0:half, :] = acc_s[3 : 3 + half, :] + acc_s[12 : 12 + half, :]
        seen = small[0:8, :]
        seen_hi = seen.astype(bf16).astype(f32)
        small[8:16, :] = seen - seen_hi
        small[16:24, :] = seen
        d_start = small[...].astype(bf16)
        acc_conv[...] = nt(q_hi, mix[...]) + nt(q_lo, mix[...]) + dot(d_start, w_start[...], 0, 0)
        acc_mix[...] = dot(w_taps_t[...], q_hi) + dot(w_taps_t[...], q_lo)
        starts = dot(d_start, w_taps[...])
        starts = starts[0:half] + starts[8 : 8 + half]
        m_rows[0:9, :] = acc_m[0:9, :] + acc_m[9:18, :]
        m_rows[9:10, :] = acc_m[27:28, :]
        bias = acc_b[0:1, :]
        share[0:1, 0:128] = bias
        share[6:7, 128:256] = bias - bias.astype(bf16).astype(f32)
        share[0 : 2 * half, 128:256] = acc_g[8 : 8 + 2 * half, :] + acc_g[0 : 2 * half, :]
        for j in range(n_dp):
            row = 64 * (j % (n_dp // 2)) + per_mix * (j // (n_dp // 2))
            packet[j, 0:per_mix, :] = acc_mix[row : row + per_mix, :].astype(bf16)
            for tap in range(3):
                at = per_mix + tap * eighth
                row = tap * pair + j * eighth
                packet[j, at : at + eighth, :] = acc_conv[row : row + eighth, :].astype(bf16)
            if j < channels // 128:
                share[1 : 1 + half, 0:128] = starts[:, 128 * j : 128 * (j + 1)]
            else:
                share[1 : 1 + half, 0:128] = jnp.zeros((half, 128), f32)
            at = per_mix + 3 * eighth
            cols = slice(128 * (j // 2), 128 * (j // 2) + 128)
            share[6:8, 0:128] = m_rows[8:10, cols]
            low = m_rows[0:10, cols]
            low = low - low.astype(bf16).astype(f32)
            share[4:6, 0:128] = low[8:10]
            packet[j, at : at + 8, 0:128] = m_rows[0:8, cols].astype(bf16)
            packet[j, at : at + 8, 128:256] = share[:, 0:128].astype(bf16)
            packet[j, at : at + 8, 256:384] = share[:, 128:256].astype(bf16)
            packet[j, at : at + 8, 384:512] = low[0:8].astype(bf16)


def whole(shape):
    return pl.BlockSpec(shape, lambda i: (0,) * len(shape))


def columns(rows, width):
    return pl.BlockSpec((rows, width), lambda i: (0, i))


def local(
    light_flux,
    lengths,
    offsets,
    start_weight,
    conv_weight,
    gate_bias,
    mix_first,
    mix_last,
    end_weight,
    cotangent,
):
    n_dp = lax.axis_size("dp")
    n_ctx = lax.axis_size("ctx")
    half_dp = n_dp // 2
    dp = lax.axis_index("dp")
    k = lax.axis_index("ctx")
    low = dp < half_dp
    shard_len = light_flux.shape[2]
    half = light_flux.shape[1] // 2
    channels = start_weight.shape[0]
    epochs = shard_len * n_ctx
    dilations = (shard_len // 4, shard_len + shard_len // 2)
    rows = conv_weight.shape[1]
    last_rows = mix_last.shape[0]
    conv0, conv1 = conv_weight[0], conv_weight[1]
    part = rows // n_ctx
    n_e = 2 * half

    def strided(x):
        lead = x.shape[0]
        cols = x.shape[1]
        view = x.reshape(lead, cols // rows, n_ctx, part)
        return lax.dynamic_slice(
            view, (0, 0, k, 0), (lead, cols // rows, 1, part)
        ).reshape(lead, cols // n_ctx)

    flux_hi, flux_lo = split(light_flux[0])
    cot_hi, cot_lo = split(cotangent[0])
    n_in = 6 * half + 1
    inputs = jnp.concatenate(
        [flux_hi, flux_lo, cot_hi, cot_lo, offsets.astype(bf16)], axis=0
    )
    n_pad = -(-n_in // 8) * 8
    inputs = pad_to(inputs, n_pad, shard_len)

    fields = inputs[None]
    while fields.shape[0] < n_ctx:
        hop = fields.shape[0]
        other = lax.ppermute(fields, "ctx", [(c, c ^ hop) for c in range(n_ctx)])
        fields = jnp.concatenate([fields, other], axis=0)
    half_rows = rows // 2
    mix_far = lax.ppermute(
        mix_first[half_rows:], "dp", [(i, i + half_dp) for i in range(half_dp)]
    )
    mix_send = jnp.where(low, mix_first[:half_rows], mix_far)

    sw_hi, sw_lo = split(start_weight)
    sw_pair = jnp.concatenate([sw_hi, sw_lo], axis=1)
    a_rows = []
    for tap in range(3):
        parts = dot(sw_pair, conv0[:, tap * channels : (tap + 1) * channels], 0, 1)
        a_rows.append(parts[:half] + parts[half:])
    a_own = jnp.concatenate(a_rows, axis=0)
    ew_last = lax.dynamic_slice(end_weight, (0, last_rows * dp), (n_e, last_rows))
    ew_skip = lax.dynamic_slice(
        end_weight, (0, rows * jnp.maximum(dp - half_dp, 0)), (n_e, rows)
    )
    ew_skip = jnp.where(low, 0.0, ew_skip)
    mix_last_k = strided(mix_last).astype(f32)
    mix_skip_k = lax.dynamic_slice(mix_first, (0, rows * k), (rows, rows)).astype(f32)
    e_own = jnp.concatenate(
        [
            dot(ew_skip, mix_skip_k, precision=highest),
            dot(ew_last, mix_last_k, precision=highest),
        ],
        axis=1,
    )
    a_hi, a_lo = split(a_own)
    e_hi, e_lo = split(e_own)
    a_block = pad_to(jnp.concatenate([a_hi, a_lo], axis=0), 20, rows).reshape(5, 4 * rows)
    small = jnp.concatenate(
        [pad_to(jnp.concatenate([e_hi, e_lo], axis=1), 8, 4 * rows), pad_to(a_block, 8, 4 * rows)],
        axis=1,
    )
    conv_k = lax.dynamic_slice(conv1, (part * k, 0), (part, 3 * channels))
    packet = jnp.concatenate(
        [conv_k[:, tap * channels : (tap + 1) * channels] for tap in range(3)] + [small, mix_send],
        axis=0,
    )
    per = packet.shape[0]
    got = exchange(
        jnp.broadcast_to(packet[None], (n_dp, per, channels)).reshape(n_dp * per, channels), "dp"
    ).reshape(n_dp, per, channels)
    w_taps = got[:, : 3 * part].reshape(n_dp, 3, part, channels).transpose(1, 0, 2, 3)
    w_taps = w_taps.reshape(6 * rows, channels)
    mix_res = got[:, 4 * part :].reshape(2, half_dp, half_rows, channels).transpose(1, 0, 2, 3)
    mix_res = mix_res.reshape(channels, channels)
    e_k = got[:, 3 * part : 3 * part + n_e, : 4 * rows].astype(f32).sum(axis=0)
    e_cat = e_k[:, : 2 * rows] + e_k[:, 2 * rows :]
    a_all = got[:, 3 * part : 3 * part + 5, 4 * rows :].reshape(n_dp, 20, rows)
    a_all = a_all[:, :18].transpose(1, 0, 2).reshape(18, n_dp * rows)
    a_hi, a_lo = a_all[:9], a_all[9:]

    length = lengths[0]
    b_hi, b_lo = split(gate_bias[0][None])
    a_cat = jnp.concatenate(
        [a_hi, a_hi, a_lo, b_hi, b_lo, jnp.zeros((3, 2 * channels), bf16)], axis=0
    ).T
    w_hi, w_lo = (
        jnp.concatenate([jnp.pad(x, ((0, 0), (3, 6 - half)))] * 3 + [jnp.zeros((channels, 5), bf16)], axis=1)
        for x in (sw_hi, sw_lo)
    )
    gap = jnp.zeros((8 - half, channels), bf16)
    w_start = jnp.concatenate(
        [sw_hi.T, gap, sw_hi.T, gap, sw_lo.T, gap, jnp.zeros((8, channels), bf16)], axis=0
    )
    ec_hi, ec_lo = split(e_cat)
    gap = jnp.zeros((2, 2 * rows), bf16)
    e_pair = jnp.concatenate([ec_hi, gap, ec_lo, gap], axis=0)
    e_up = pad_to(jnp.concatenate([ec_hi, gap, ec_hi, gap, ec_lo], axis=0), 32, 2 * rows).T
    bias1 = strided(gate_bias[1][None]).T
    info = jnp.stack([length, k])
    pair = 2 * rows
    wide = epochs + 2 * (dilations[1] + 128)
    smem = pl.BlockSpec(memory_space=pltpu.SMEM)
    shapes = jax.ShapeDtypeStruct
    params = pltpu.CompilerParams(
        dimension_semantics=("arbitrary",), vmem_limit_bytes=60000 * 1024
    )
    forward = pl.pallas_call(
        functools.partial(forward_kernel, dilations[0], dilations[1], half),
        grid=(n_ctx,),
        in_specs=[
            smem,
            whole((n_ctx, n_pad, shard_len)),
            whole(a_cat.shape),
            whole(w_hi.shape),
            whole(w_lo.shape),
            whole(mix_res.shape),
            whole(w_taps.shape),
            whole(bias1.shape),
            whole(e_pair.shape),
        ],
        out_specs=[columns(channels, shard_len)] * 3
        + [columns(32, shard_len), whole((pair, epochs)), whole((rows, epochs)),
           whole((rows, epochs)), whole((n_ctx, 32, shard_len))],
        out_shape=[shapes((channels, epochs), bf16)] * 3
        + [shapes((32, epochs), bf16), shapes((pair, epochs), bf16), shapes((rows, epochs), f32),
           shapes((rows, epochs), f32), shapes((n_ctx, 32, shard_len), f32)],
        scratch_shapes=[
            pltpu.VMEM((8, epochs + 512), f32),
            pltpu.VMEM((32, shard_len), f32),
            pltpu.VMEM((2 * pair, wide), bf16),
            pltpu.VMEM((pair, epochs), f32),
            pltpu.VMEM((pair, shard_len), f32),
            pltpu.VMEM((rows, epochs), bf16),
            pltpu.VMEM((3 * pair, channels), bf16),
            pltpu.VMEM((3 * pair, 32), bf16),
        ],
        compiler_params=params,
        name="layers_forward",
    )
    g0, du0, dv0, s_all, g_own, du1, dv1, packed = forward(
        info, fields, a_cat, w_hi, w_lo, mix_res, w_taps, bias1, e_pair
    )
    got = exchange(packed.reshape(n_ctx * 32, shard_len), "ctx").reshape(n_ctx, 32, shard_len)

    n_mix = channels // n_dp
    n_conv = 3 * pair // n_dp
    per = n_mix + n_conv + 8
    backward = pl.pallas_call(
        functools.partial(backward_kernel, dilations[1], half),
        grid=(n_ctx,),
        in_specs=[
            smem,
            whole((n_ctx, 32, shard_len)),
            whole((n_ctx, n_pad, shard_len)),
            whole((2 * half, shard_len)),
            whole((pair, 32)),
            whole((pair, epochs)),
            whole((rows, epochs)),
            whole((rows, epochs)),
            whole((3 * pair, channels)),
            whole((channels, 3 * pair)),
            whole((channels, channels)),
            whole((channels, 3 * pair)),
            whole((32, channels)),
        ]
        + [columns(channels, shard_len)] * 3
        + [columns(32, shard_len)],
        out_specs=[whole((1, half, shard_len)), whole((n_dp, per, channels))],
        out_shape=[shapes((1, half, shard_len), f32), shapes((n_dp, per, channels), bf16)],
        scratch_shapes=[
            pltpu.VMEM((32, shard_len), f32),
            pltpu.VMEM((32, shard_len), f32),
            pltpu.VMEM((pair, wide), bf16),
            pltpu.VMEM((8, wide), f32),
            pltpu.VMEM((rows, epochs), f32),
            pltpu.VMEM((3 * pair, epochs), bf16),
            pltpu.VMEM((3 * pair, channels), f32),
            pltpu.VMEM((channels, channels), f32),
            pltpu.VMEM((32, 2 * channels), f32),
            pltpu.VMEM((32, 3 * pair), f32),
            pltpu.VMEM((16, pair), f32),
            pltpu.VMEM((16, pair), f32),
            pltpu.VMEM((channels, shard_len), f32),
            pltpu.VMEM((16, 2 * channels), f32),
            pltpu.VMEM((8, 256), f32),
            pltpu.VMEM((3 * pair, channels), f32),
            pltpu.VMEM((32, 3 * pair), f32),
        ],
        compiler_params=params,
        name="layers_backward",
    )
    coupled, packed = backward(
        info, got, fields, light_flux[0], e_up, g_own, du1, dv1, w_taps, w_taps.T, mix_res,
        dot(mix_res, w_taps, 0, 1).astype(bf16), w_start, g0, du0, dv0, s_all,
    )
    got = exchange(packed.reshape(n_dp * per, channels), "dp").reshape(n_dp, per, channels)
    got = got.astype(f32).sum(axis=0)
    mix_piece = got[:n_mix]
    conv_piece = got[n_mix : n_mix + n_conv].astype(bf16)
    smalls = got[n_mix + n_conv :]
    m_first = smalls[:, :128] + smalls[:, 384:]
    m_rest = smalls[4:6, 128:256] + smalls[6:8, 128:256]
    m_own = lax.dynamic_slice(
        jnp.concatenate([m_first, m_rest], axis=0), (0, rows * (dp % 2)), (10, rows)
    )
    start_own = jnp.where(dp < channels // 128, smalls[1 : 1 + half, 128:256], 0.0)
    g_own_sum = smalls[: 2 * half, 256:384]
    bias1_own = smalls[0:1, 128:256] + smalls[6:7, 256:384]
    mo_hi, mo_lo = split(m_own)
    mo_pair = jnp.concatenate([mo_hi[:9], mo_lo[:9]], axis=0)
    start_t = 0.0
    for tap in range(3):
        up = dot(mo_pair, conv0[:, tap * channels : (tap + 1) * channels])
        start_t = start_t + up[half * tap : half * tap + half] + up[9 + half * tap : 9 + half * tap + half]
    spot = lax.dynamic_update_slice(
        jnp.zeros((half, channels), f32), start_own, (0, 128 * (dp % (channels // 128)))
    )
    start_t = start_t + spot
    end_last = dot(g_own_sum[:, rows:], mix_last_k, 1, 1, highest)
    end_skip = jnp.where(low, 0.0, dot(g_own_sum[:, :rows], mix_skip_k, 1, 1, highest))
    g_rows = jnp.concatenate([g_own_sum, bias1_own], axis=0)
    parts = jnp.concatenate(
        [
            m_own,
            pad_to(g_rows, 10, 2 * rows),
            pad_to(jnp.concatenate([end_last, end_skip], axis=1), 10, last_rows + rows),
        ],
        axis=1,
    )
    width = parts.shape[1]
    parts_hi, parts_lo = split(parts)
    start_hi, start_lo = split(start_t)
    pack_rows = [
        conv_piece,
        mix_piece.astype(bf16),
        pad_to(jnp.concatenate([parts_hi, parts_lo[:, : 3 * rows]], axis=1), 10, channels),
        start_hi,
        start_lo,
    ]
    packed = jnp.concatenate(pack_rows, axis=0)
    per0 = packed.shape[0]
    per = -(-per0 // 8) * 8
    packed = pad_to(packed, per, channels)
    got = exchange(
        jnp.broadcast_to(packed[None], (n_ctx, per, channels)).reshape(n_ctx * per, channels), "ctx"
    ).reshape(n_ctx, per, channels)
    grad_conv1 = got[:, :n_conv].reshape(n_ctx, 3, part, channels).transpose(0, 2, 1, 3)
    grad_conv1 = grad_conv1.reshape(rows, 3 * channels).astype(f32)
    mix_rows = got[:, n_conv : n_conv + n_mix].astype(f32).sum(axis=0)
    base = n_conv + n_mix
    parts = got[:, base : base + 10].astype(f32)
    parts_lo = parts[:, :, width : width + 3 * rows]
    parts = jnp.concatenate(
        [parts[:, :, : 3 * rows] + parts_lo, parts[:, :, 3 * rows : width]], axis=2
    )
    start_t = got[:, base + 10 : base + 10 + 2 * half].astype(f32).sum(axis=0)
    start_t = start_t[:half] + start_t[half:]
    m_own = parts[:, :, :rows].sum(axis=0)
    g_all = parts[:, : 2 * half, rows : 3 * rows]
    g0_all = g_all[:, :, :rows].transpose(1, 0, 2).reshape(2 * half, channels)
    g1_all = g_all[:, :, rows:].reshape(n_ctx, 2 * half, half_dp, part).transpose(1, 2, 0, 3)
    g1_all = g1_all.reshape(2 * half, channels)
    bias1_all = parts[:, 2 * half, rows : 3 * rows].reshape(n_ctx, n_dp, part).transpose(1, 0, 2)
    bias1_all = bias1_all.reshape(2 * channels)
    end_both = parts[:, : 2 * half, 3 * rows :].sum(axis=0)
    a_grad = m_own[:9].T
    grad_conv0 = jnp.concatenate(
        [
            dot(a_grad[:, half * tap : half * tap + half], start_weight, 1, 1, highest)
            for tap in range(3)
        ],
        axis=1,
    )
    grad_mix_last = dot(ew_last, g1_all, 0, 0, highest)
    skip_rows = dot(ew_skip, g0_all, 0, 0, highest)

    other = lax.ppermute(mix_rows, "dp", [(i + half_dp, i) for i in range(half_dp)])
    final = jnp.concatenate(
        [
            start_t.reshape(-1, 128),
            pad_to(end_both, 2 * half, 128),
            pad_to(m_own[9:10], 1, 128),
        ],
        axis=0,
    )
    per0 = final.shape[0]
    per = -(-per0 // 8) * 8
    final = pad_to(final, per, 128)
    got = exchange(
        jnp.broadcast_to(final[None], (n_dp, per, 128)).reshape(n_dp * per, 128), "dp"
    ).reshape(n_dp, per, 128)
    n_start = half * channels // 128
    grad_start = got[:, :n_start].sum(axis=0).reshape(half, channels).T
    ends = got[:, n_start : n_start + 2 * half]
    grad_end = ends[:, :, :last_rows].transpose(1, 0, 2).reshape(2 * half, channels)
    grad_end = grad_end + ends[half_dp:, :, last_rows : last_rows + rows].transpose(
        1, 0, 2
    ).reshape(2 * half, channels)
    bias0_all = got[:, n_start + 2 * half, :rows].reshape(2 * channels)
    grad_bias = jnp.stack([bias0_all, bias1_all])
    residual = jnp.concatenate([mix_rows, other], axis=0)
    grad_mix_first = jnp.where(low, residual, skip_rows)
    grad_conv = jnp.stack([grad_conv0, grad_conv1])
    return (coupled, grad_start, grad_conv, grad_bias, grad_mix_first, grad_mix_last, grad_end)


def solution(mesh):
    in_specs = (
        P("dp", None, "ctx"),
        P("dp"),
        P("dp", "ctx"),
        P(),
        P(None, "dp", None),
        P(),
        P("dp", None),
        P("dp", None),
        P(),
        P("dp", None, "ctx"),
    )
    out_specs = (
        P("dp", None, "ctx"),
        P(),
        P(None, "dp", None),
        P(),
        P("dp", None),
        P("dp", None),
        P(),
    )
    return jax.shard_map(local, mesh=mesh, in_specs=in_specs, out_specs=out_specs, check_vma=False)
```

```python
import functools

import jax
import jax.numpy as jnp
from jax import lax
from jax.experimental import pallas as pl
from jax.experimental.pallas import tpu as pltpu
from jax.sharding import PartitionSpec as P

BUCKETS = 4
highest = lax.Precision.HIGHEST
bf16 = jnp.bfloat16
f32 = jnp.float32


def dot(a, b, ca=1, cb=0, precision=None):
    return lax.dot_general(
        a, b, (((ca,), (cb,)), ((), ())), precision=precision, preferred_element_type=f32
    )


def split(x):
    hi = lax.reduce_precision(x, 8, 7)
    return hi.astype(bf16), (x - hi).astype(bf16)


def pad_to(x, rows, cols):
    return jnp.pad(x, ((0, rows - x.shape[0]), (0, cols - x.shape[1])))


def shift(x, n):
    total = x.shape[1]
    if n > 0:
        return jnp.pad(x[:, : total - n], ((0, 0), (n, 0)))
    return jnp.pad(x[:, -n:], ((0, 0), (0, -n)))


def tap_of(x, off, dilation, side):
    out = shift(x, side * dilation)
    for step in range(1, BUCKETS):
        out = jnp.where(off == step, shift(x, side * (dilation + step)), out)
    return out


def tap_back(x, off, dilation, side):
    out = 0.0
    for step in range(BUCKETS):
        out = out + shift(jnp.where(off == step, x, 0.0), -side * (dilation + step))
    return out


def exchange(x, axis):
    return lax.all_to_all(x, axis, 0, 0, tiled=True)


def nt(a, b):
    return dot(a, b, 1, 1)


def rolled(x, start, width):
    if start % 128 == 0:
        return x[:, start : start + width]
    return pltpu.roll(x, x.shape[1] - start, 1)[:, :width]


def steps_apart(shape):
    return (
        lax.broadcasted_iota(jnp.int32, shape, 0) - lax.broadcasted_iota(jnp.int32, shape, 1)
    ).astype(f32)


def one_hot(apart, target):
    return jnp.where(apart == target, 1.0, 0.0).astype(bf16)


def valid_row(c, width, length):
    at = lax.broadcasted_iota(jnp.int32, (1, width), 1) + c * width
    return (at < length).astype(f32)


def packet_kernel(
    info, conv, mix_first, mix_far, mix_last, start, ends,
    packet,
    sw, low_rows, ew, turn,
):
    dp = info[0]
    k = info[1]
    n_dp, per, channels = packet.shape
    half = start.shape[0]
    rows = mix_first.shape[0]
    last_rows = mix_last.shape[0]
    n_e = ends.shape[0]
    part = (per - 8 - rows // 2) // 3
    upper = dp >= n_dp // 2

    group = conv[1, pl.ds(pl.multiple_of((k // 2) * 2 * part, 2 * part), 2 * part), :].astype(f32)
    mine = jnp.where(k % 2 == 1, group[part:], group[:part]).astype(bf16)

    sw[...] = jnp.zeros(sw.shape, f32)
    sw[0:half, :] = start[...]
    full = sw[...]
    sw_hi = full.astype(bf16)
    sw_lo = (full - sw_hi.astype(f32)).astype(bf16)
    turn[...] = jnp.zeros(turn.shape, f32)
    for tap in range(3):
        block = conv[0, :, tap * channels : (tap + 1) * channels]
        one = nt(sw_hi, block) + nt(sw_lo, block)
        turn[half * tap : half * (tap + 1), 0:rows] = one[0:half]
    a_t = turn[...]
    a_hi = a_t[0:16].astype(bf16).astype(f32)
    a_lo = a_t[0:16] - a_hi
    lane = lax.broadcasted_iota(jnp.int32, (8, 128), 1)
    row = lax.broadcasted_iota(jnp.int32, (8, 128), 0)
    near = jnp.where(lane < rows, a_hi[0:8], pltpu.roll(a_lo[0:8], rows, 1))
    far = jnp.where(row == 0, a_hi[8:16], pltpu.roll(a_lo[8:16], 1, 0))

    ew[...] = jnp.zeros(ew.shape, f32)
    ew[0:n_e, :] = ends[...]
    e_all = ew[...]
    wide = lax.broadcasted_iota(jnp.int32, (8, 128), 1)

    def product(shift, count, source, keep):
        moved = pltpu.roll(e_all, lax.rem(channels - shift, channels), 1)[:, 0:128]
        moved = jnp.where(jnp.logical_and(wide < count, keep), moved, 0.0)
        hi = moved.astype(bf16)
        low = (moved - hi.astype(f32)).astype(bf16)
        low_rows[...] = jnp.zeros(low_rows.shape, bf16)
        low_rows[0:count, :] = source[...]
        out = dot(hi, low_rows[...]) + dot(low, low_rows[...])
        out_hi = out.astype(bf16)
        return out_hi, (out - out_hi.astype(f32)).astype(bf16)

    at = lax.broadcasted_iota(jnp.int32, (channels, 128), 0)
    col = lax.broadcasted_iota(jnp.int32, (channels, 128), 1)
    m = col - rows
    pick0 = jnp.where(jnp.logical_and(col < rows, at == rows * k + col), 1.0, 0.0).astype(bf16)
    target = (m >> 3) * rows + part * k + (m & 7)
    pick1 = jnp.where(jnp.logical_and(m >= 0, at == target), 1.0, 0.0).astype(bf16)
    e0_hi, e0_lo = product(
        rows * jnp.maximum(dp - n_dp // 2, 0), rows, mix_first, upper
    )
    e1_hi, e1_lo = product(last_rows * dp, last_rows, mix_last, dp >= 0)
    e_hi = dot(e0_hi, pick0) + dot(e1_hi, pick1)
    e_lo = dot(e0_lo, pick0) + dot(e1_lo, pick1)

    send = jnp.where(upper, mix_far[...].astype(f32), mix_first[0 : rows // 2, :].astype(f32))
    send = send.astype(bf16)
    base = 3 * part
    for j in range(n_dp):
        for tap in range(3):
            packet[j, tap * part : (tap + 1) * part, :] = mine[
                :, tap * channels : (tap + 1) * channels
            ]
        packet[j, base : base + 8, 0:128] = e_hi.astype(bf16)
        packet[j, base : base + 8, 128:256] = e_lo.astype(bf16)
        packet[j, base : base + 8, 256:384] = near.astype(bf16)
        packet[j, base : base + 8, 384:512] = far.astype(bf16)
        packet[j, base + 8 :, :] = send


def forward_kernel(
    dil0, dil1, half,
    info, fields, a_cat, w_hi, w_lo, mix, w_taps, bias1, e_pair,
    g0_out, du0_out, dv0_out, s_out, gown_out, du1_out, dv1_out, packet,
    fpad, s_cat, prod, centre, pre_s, g_keep, w_mix, w_start,
):
    i = pl.program_id(0)
    nb = fields.shape[0]
    bw = fields.shape[2]
    rows = gown_out.shape[0] // 2
    channels = mix.shape[0]
    pad0 = 256
    pad1 = dil1 + 128
    length = info[0]
    k = info[1]

    @pl.when(i == 0)
    def _():
        fpad[:, 0:pad0] = jnp.zeros((8, pad0), f32)
        fpad[:, pad0 + nb * bw :] = jnp.zeros((8, pad0), f32)
        prod[:, 0:pad1] = jnp.zeros((prod.shape[0], pad1), bf16)
        prod[:, pad1 + nb * bw :] = jnp.zeros((prod.shape[0], pad1), bf16)
        w_mix[...] = dot(w_taps[...], mix[...]).astype(bf16)
        full = dot(w_taps[...], w_hi[...]) + dot(w_taps[...], w_lo[...])
        top = full.astype(bf16).astype(f32)
        col = lax.broadcasted_iota(jnp.int32, full.shape, 1)
        w_start[...] = jnp.where(col < 18, top, full - top).astype(bf16)
        s_cat[...] = jnp.zeros(s_cat.shape, f32)
        s_cat[27:29, :] = jnp.ones((2, g0_out.shape[1]), f32)
        packet[:, 24:32, :] = jnp.zeros((nb, 8, bw), f32)
        for c in range(nb):
            block = fields[c ^ k].astype(f32)
            valid = valid_row(c, bw, length)
            at = slice(pad0 + c * bw, pad0 + (c + 1) * bw)
            fpad[0:half, at] = block[0:half] * valid
            fpad[half : 2 * half, at] = block[2 * half : 3 * half] * valid
            fpad[6:7, at] = block[6 * half : 6 * half + 1]
            fpad[7:8, at] = valid

    mw = g0_out.shape[1]
    base = pl.multiple_of(i * mw, mw)
    near = fpad[:, pl.ds(pl.multiple_of(pad0 + base, 128), mw)]
    off = near[6:7]
    valid = near[7:8]
    behind = fpad[:, pl.ds(pl.multiple_of(base, 128), mw + 2 * dil0)]
    ahead = fpad[:, pl.ds(pl.multiple_of(pad0 + base, 128), mw + 2 * dil0)]
    left = rolled(behind, dil0, mw)
    right = rolled(ahead, dil0, mw)
    for step in range(1, BUCKETS):
        left = jnp.where(off == step, rolled(behind, dil0 - step, mw), left)
        right = jnp.where(off == step, rolled(ahead, dil0 + step, mw), right)
    for part, at in ((left, 0), (near, 3), (right, 6)):
        s_cat[at : at + half, :] = part[0:half]
        s_cat[9 + at : 9 + at + half, :] = part[half : 2 * half]
        s_cat[18 + at : 18 + at + half, :] = part[0:half]
    s_b = s_cat[...].astype(bf16)
    s_out[...] = s_b
    step_rows = 128
    for r in range(0, channels, step_rows):
        u = dot(a_cat[r : r + step_rows, :], s_b)
        v = dot(a_cat[channels + r : channels + r + step_rows, :], s_b)
        t = jnp.tanh(u)
        s = 0.5 * jnp.tanh(0.5 * v) + 0.5
        g = t * s
        g0_out[r : r + step_rows, :] = (g * valid).astype(bf16)
        du0_out[r : r + step_rows, :] = (s - g * t).astype(bf16)
        dv0_out[r : r + step_rows, :] = (g - g * s).astype(bf16)
    pair = 2 * rows
    g_b = g0_out[...]
    for tap in range(3):
        at = slice(tap * pair, (tap + 1) * pair)
        part = dot(w_mix[at, :], g_b) + dot(w_start[at, :], s_b)
        if tap == 1:
            centre[:, pl.ds(base, mw)] = part
        else:
            to = tap // 2 * pair
            cols = pl.ds(pl.multiple_of(pad1 + base, 128), mw)
            prod[to : to + pair, cols] = part.astype(bf16)
    g_keep[:, pl.ds(base, mw)] = g0_out[pl.ds(pl.multiple_of(rows * k, rows), rows), :]

    @pl.when(i == pl.num_programs(0) - 1)
    def _():
        apart = steps_apart((256, 128))

        def body(c, carry):
            base = pl.multiple_of(c * bw, bw)
            off = fpad[6:7, pl.ds(pl.multiple_of(pad0 + base, 128), bw)]
            for tile in range(bw // 128):
                lane = slice(tile * 128, (tile + 1) * 128)
                behind = prod[0:pair, pl.ds(pl.multiple_of(base + tile * 128, 128), 256)]
                ahead = prod[
                    pair:,
                    pl.ds(pl.multiple_of(pad1 + dil1 + base + tile * 128, 128), 256),
                ]
                pre_s[:, lane] = dot(behind, one_hot(apart, 128.0 - off[:, lane])) + dot(
                    ahead, one_hot(apart, off[:, lane])
                )
            pre = pre_s[...] + centre[:, pl.ds(base, bw)] + bias1[...]
            t = jnp.tanh(pre[:rows])
            s = 0.5 * jnp.tanh(0.5 * pre[rows:]) + 0.5
            g = t * s
            du1_out[:, pl.ds(base, bw)] = s - g * t
            dv1_out[:, pl.ds(base, bw)] = g - g * s
            gown_out[0:rows, pl.ds(base, bw)] = g_keep[:, pl.ds(base, bw)]
            gown_out[rows:, pl.ds(base, bw)] = g.astype(bf16)
            part = dot(e_pair[...], gown_out[:, pl.ds(base, bw)])
            part = part[0 : 2 * half] + part[8 : 8 + 2 * half]
            for d in range(nb):
                for h in range(half):
                    packet[d, pl.ds(h * nb + c, 1), :] = part[h : h + 1]
            packet[c, 24 : 24 + half, :] = part[half : 2 * half]
            return carry

        lax.fori_loop(0, nb, body, 0, unroll=2)


def backward_kernel(
    dil1, half,
    info, got, fields, flux, e_up, gown, du1, dv1, w_taps, w_taps_t, mix, w_mix_t, w_start,
    g0, du0, dv0, s_in,
    coupled, packet,
    ends, d_cat, dz_pad, off_pad, d_e0, d_taps, acc_q, acc_mix, acc_m, acc_s, acc_g, acc_b,
    dg, m_rows, share, acc_conv, small,
):
    i = pl.program_id(0)
    nb = fields.shape[0]
    bw = fields.shape[2]
    pair = gown.shape[0]
    rows = pair // 2
    channels = mix.shape[0]
    n_dp = packet.shape[0]
    pad1 = dil1 + 128
    length = info[0]
    k = info[1]

    @pl.when(i == 0)
    def _():
        for ref in (acc_q, acc_m, acc_s, acc_g, acc_b, d_cat, m_rows, share, small):
            ref[...] = jnp.zeros(ref.shape, f32)
        dz_pad[:, 0:pad1] = jnp.zeros((pair, pad1), bf16)
        dz_pad[:, pad1 + nb * bw :] = jnp.zeros((pair, pad1), bf16)
        off_pad[:, 0:pad1] = jnp.full((8, pad1), -1.0, f32)
        off_pad[:, pad1 + nb * bw :] = jnp.full((8, pad1), -1.0, f32)
        total = got[0]
        for src in range(1, nb):
            total = total + got[src]
        ends[...] = total
        mine = valid_row(k, bw, length)
        for h in range(half):
            growth = jnp.exp(ends[pl.ds(h * nb + k, 1), :])
            coupled[0, h : h + 1, :] = (
                growth * flux[half + h : half + h + 1] + ends[24 + h : 25 + h, :]
            ) * mine

        def first(c, carry):
            base = pl.multiple_of(c * bw, bw)
            at = pl.multiple_of(pad1 + base, 128)
            block = fields[c ^ k].astype(f32)
            valid = valid_row(c, bw, length)
            off_pad[0:1, pl.ds(at, bw)] = block[6 * half : 6 * half + 1]
            flux2 = block[half : 2 * half] + block[3 * half : 4 * half]
            cot = (block[4 * half : 5 * half] + block[5 * half : 6 * half]) * valid
            for h in range(half):
                growth = jnp.exp(ends[pl.ds(h * nb + c, 1), :])
                d_cat[h : h + 1, :] = cot[h : h + 1] * growth * flux2[h : h + 1]
            d_cat[half : 2 * half, :] = cot
            full = d_cat[0:8, :]
            hi = full.astype(bf16).astype(f32)
            lo = full - hi
            d_cat[8:16, :] = lo
            d_cat[16:24, :] = hi
            d_gated = dot(e_up[...], d_cat[...].astype(bf16))
            acc_g[...] += nt(d_cat[8:24, :].astype(bf16), gown[:, pl.ds(base, bw)])
            d_e0[:, pl.ds(base, bw)] = d_gated[:rows]
            up = d_gated[rows : 2 * rows]
            dz_pad[0:rows, pl.ds(at, bw)] = (up * du1[:, pl.ds(base, bw)]).astype(bf16)
            dz_pad[rows:, pl.ds(at, bw)] = (up * dv1[:, pl.ds(base, bw)]).astype(bf16)
            return carry

        lax.fori_loop(0, nb, first, 0, unroll=2)

        apart = steps_apart((128, 256))

        def second(c, carry):
            base = pl.multiple_of(c * bw, bw)
            valid = valid_row(c, bw, length)
            for tile in range(bw // 128):
                lane = pl.ds(pl.multiple_of(base + tile * 128, 128), 128)
                late = pl.ds(pl.multiple_of(pad1 + dil1 + base + tile * 128, 128), 256)
                early = pl.ds(pl.multiple_of(base + tile * 128, 128), 256)
                left = nt(dz_pad[:, late], one_hot(apart, -off_pad[0:1, late]))
                right = nt(dz_pad[:, early], one_hot(apart, off_pad[0:1, early] - 128.0))
                d_taps[0:pair, lane] = left.astype(bf16)
                d_taps[2 * pair :, lane] = (
                    right * valid[:, tile * 128 : (tile + 1) * 128]
                ).astype(bf16)
            centre = dz_pad[:, pl.ds(pl.multiple_of(pad1 + base, 128), bw)]
            d_taps[pair : 2 * pair, pl.ds(base, bw)] = centre
            acc_b[...] += nt(jnp.ones((16, bw), bf16), centre)
            return carry

        lax.fori_loop(0, nb, second, 0, unroll=2)

    mw = g0.shape[1]
    base = pl.multiple_of(i * mw, mw)
    d_blk = d_taps[:, pl.ds(base, mw)]
    s_b = s_in[...]
    acc_q[...] += nt(d_blk, g0[...])
    acc_s[...] += nt(s_b, d_blk)
    dg[...] = dot(w_mix_t[...], d_blk)
    own = pl.ds(pl.multiple_of(rows * k, rows), rows)
    dg[own, :] = dg[own, :] + d_e0[:, pl.ds(base, mw)]
    up = dg[...]
    acc_m[:, 0:channels] += nt(s_b, (up * du0[...].astype(f32)).astype(bf16))
    acc_m[:, channels:] += nt(s_b, (up * dv0[...].astype(f32)).astype(bf16))

    @pl.when(i == pl.num_programs(0) - 1)
    def _():
        per_mix = channels // n_dp
        eighth = pair // n_dp
        q = acc_q[...]
        q_hi = q.astype(bf16)
        small[0:half, :] = acc_s[3 : 3 + half, :] + acc_s[12 : 12 + half, :]
        seen = small[0:8, :]
        seen_hi = seen.astype(bf16).astype(f32)
        small[8:16, :] = seen - seen_hi
        small[16:24, :] = seen
        d_start = small[...].astype(bf16)
        acc_conv[...] = nt(q_hi, mix[...]) + dot(d_start, w_start[...], 0, 0)
        acc_mix[...] = dot(w_taps_t[...], q_hi)
        starts = dot(d_start, w_taps[...])
        starts = starts[0:half] + starts[8 : 8 + half]
        m_rows[0:9, :] = acc_m[0:9, :] + acc_m[9:18, :]
        m_rows[9:10, :] = acc_m[27:28, :]
        bias = acc_b[0:1, :]
        share[0:1, 0:128] = bias
        share[6:7, 128:256] = bias - bias.astype(bf16).astype(f32)
        share[0 : 2 * half, 128:256] = acc_g[8 : 8 + 2 * half, :] + acc_g[0 : 2 * half, :]
        for j in range(n_dp):
            row = 64 * (j % (n_dp // 2)) + per_mix * (j // (n_dp // 2))
            packet[j, 0:per_mix, :] = acc_mix[row : row + per_mix, :].astype(bf16)
            for tap in range(3):
                at = per_mix + tap * eighth
                row = tap * pair + j * eighth
                packet[j, at : at + eighth, :] = acc_conv[row : row + eighth, :].astype(bf16)
            if j < channels // 128:
                share[1 : 1 + half, 0:128] = starts[:, 128 * j : 128 * (j + 1)]
            else:
                share[1 : 1 + half, 0:128] = jnp.zeros((half, 128), f32)
            at = per_mix + 3 * eighth
            cols = slice(128 * (j // 2), 128 * (j // 2) + 128)
            share[6:8, 0:128] = m_rows[8:10, cols]
            low = m_rows[0:10, cols]
            low = low - low.astype(bf16).astype(f32)
            share[4:6, 0:128] = low[8:10]
            packet[j, at : at + 8, 0:128] = m_rows[0:8, cols].astype(bf16)
            packet[j, at : at + 8, 128:256] = share[:, 0:128].astype(bf16)
            packet[j, at : at + 8, 256:384] = share[:, 128:256].astype(bf16)
            packet[j, at : at + 8, 384:512] = low[0:8].astype(bf16)


def whole(shape):
    return pl.BlockSpec(shape, lambda i: (0,) * len(shape))


def columns(rows, width):
    return pl.BlockSpec((rows, width), lambda i: (0, i))


def local(
    light_flux,
    lengths,
    offsets,
    start_weight,
    conv_weight,
    gate_bias,
    mix_first,
    mix_last,
    end_weight,
    cotangent,
):
    n_dp = lax.axis_size("dp")
    n_ctx = lax.axis_size("ctx")
    half_dp = n_dp // 2
    dp = lax.axis_index("dp")
    k = lax.axis_index("ctx")
    low = dp < half_dp
    shard_len = light_flux.shape[2]
    half = light_flux.shape[1] // 2
    channels = start_weight.shape[0]
    epochs = shard_len * n_ctx
    dilations = (shard_len // 4, shard_len + shard_len // 2)
    rows = conv_weight.shape[1]
    last_rows = mix_last.shape[0]
    conv0, conv1 = conv_weight[0], conv_weight[1]
    part = rows // n_ctx
    n_e = 2 * half

    def strided(x):
        lead = x.shape[0]
        cols = x.shape[1]
        view = x.reshape(lead, cols // rows, n_ctx, part)
        return lax.dynamic_slice(
            view, (0, 0, k, 0), (lead, cols // rows, 1, part)
        ).reshape(lead, cols // n_ctx)

    half_rows = rows // 2
    mix_far = lax.ppermute(
        mix_first[half_rows:], "dp", [(i, i + half_dp) for i in range(half_dp)]
    )
    sw_hi, sw_lo = split(start_weight)
    ew_last = lax.dynamic_slice(end_weight, (0, last_rows * dp), (n_e, last_rows))
    ew_skip = lax.dynamic_slice(
        end_weight, (0, rows * jnp.maximum(dp - half_dp, 0)), (n_e, rows)
    )
    ew_skip = jnp.where(low, 0.0, ew_skip)
    mix_last_k = strided(mix_last).astype(f32)
    mix_skip_k = lax.dynamic_slice(mix_first, (0, rows * k), (rows, rows)).astype(f32)
    per = 3 * part + 8 + half_rows
    smem = pl.BlockSpec(memory_space=pltpu.SMEM)
    packets = pl.pallas_call(
        packet_kernel,
        in_specs=[smem] + [pl.BlockSpec(memory_space=pltpu.VMEM)] * 6,
        out_specs=pl.BlockSpec(memory_space=pltpu.VMEM),
        out_shape=jax.ShapeDtypeStruct((n_dp, per, channels), bf16),
        scratch_shapes=[
            pltpu.VMEM((16, channels), f32),
            pltpu.VMEM((128, channels), bf16),
            pltpu.VMEM((8, channels), f32),
            pltpu.VMEM((16, 128), f32),
        ],
        name="weight_packets",
    )(jnp.stack([dp, k]), conv_weight, mix_first, mix_far, mix_last, start_weight.T, end_weight)
    got = exchange(packets.reshape(n_dp * per, channels), "dp").reshape(n_dp, per, channels)
    flux_hi, flux_lo = split(light_flux[0])
    cot_hi, cot_lo = split(cotangent[0])
    n_in = 6 * half + 1
    inputs = jnp.concatenate(
        [flux_hi, flux_lo, cot_hi, cot_lo, offsets.astype(bf16)], axis=0
    )
    n_pad = -(-n_in // 8) * 8
    inputs = pad_to(inputs, n_pad, shard_len)

    fields = inputs[None]
    while fields.shape[0] < n_ctx:
        hop = fields.shape[0]
        other = lax.ppermute(fields, "ctx", [(c, c ^ hop) for c in range(n_ctx)])
        fields = jnp.concatenate([fields, other], axis=0)
    w_taps = got[:, : 3 * part].reshape(n_dp, 3, part, channels).transpose(1, 0, 2, 3)
    w_taps = w_taps.reshape(6 * rows, channels)
    mix_res = got[:, 4 * part :].reshape(2, half_dp, half_rows, channels).transpose(1, 0, 2, 3)
    mix_res = mix_res.reshape(channels, channels)
    e_k = got[:, 3 * part : 3 * part + n_e, : 4 * rows].astype(f32).sum(axis=0)
    e_cat = e_k[:, : 2 * rows] + e_k[:, 2 * rows :]
    a_got = got[:, 3 * part : 4 * part, 4 * rows :]
    a_all = jnp.concatenate(
        [
            a_got[:, :, :rows],
            a_got[:, 0:1, 2 * rows : 3 * rows],
            a_got[:, :, rows : 2 * rows],
            a_got[:, 1:2, 2 * rows : 3 * rows],
        ],
        axis=1,
    )
    a_all = a_all.transpose(1, 0, 2).reshape(18, n_dp * rows)
    a_hi, a_lo = a_all[:9], a_all[9:]

    gap = jnp.zeros((8 - half, channels), bf16)
    w_start = jnp.concatenate(
        [sw_hi.T, gap, sw_hi.T, gap, sw_lo.T, gap, jnp.zeros((8, channels), bf16)], axis=0
    )
    fields, w_start = lax.optimization_barrier((fields, w_start))

    length = lengths[0]
    b_hi, b_lo = split(gate_bias[0][None])
    a_cat = jnp.concatenate(
        [a_hi, a_hi, a_lo, b_hi, b_lo, jnp.zeros((3, 2 * channels), bf16)], axis=0
    ).T
    w_hi, w_lo = (
        jnp.concatenate([jnp.pad(x, ((0, 0), (3, 6 - half)))] * 3 + [jnp.zeros((channels, 5), bf16)], axis=1)
        for x in (sw_hi, sw_lo)
    )
    ec_hi, ec_lo = split(e_cat)
    gap = jnp.zeros((2, 2 * rows), bf16)
    e_pair = jnp.concatenate([ec_hi, gap, ec_lo, gap], axis=0)
    e_up = pad_to(jnp.concatenate([ec_hi, gap, ec_hi, gap, ec_lo], axis=0), 32, 2 * rows).T
    bias1 = strided(gate_bias[1][None]).T
    info = jnp.stack([length, k])
    pair = 2 * rows
    main = 2 * shard_len
    wide = epochs + 2 * (dilations[1] + 128)
    smem = pl.BlockSpec(memory_space=pltpu.SMEM)
    shapes = jax.ShapeDtypeStruct
    params = pltpu.CompilerParams(
        dimension_semantics=("arbitrary",), vmem_limit_bytes=60000 * 1024
    )
    forward = pl.pallas_call(
        functools.partial(forward_kernel, dilations[0], dilations[1], half),
        grid=(epochs // main,),
        in_specs=[
            smem,
            whole((n_ctx, n_pad, shard_len)),
            whole(a_cat.shape),
            whole(w_hi.shape),
            whole(w_lo.shape),
            whole(mix_res.shape),
            whole(w_taps.shape),
            whole(bias1.shape),
            whole(e_pair.shape),
        ],
        out_specs=[columns(channels, main)] * 3
        + [columns(32, main), whole((pair, epochs)), whole((rows, epochs)),
           whole((rows, epochs)), whole((n_ctx, 32, shard_len))],
        out_shape=[shapes((channels, epochs), bf16)] * 3
        + [shapes((32, epochs), bf16), shapes((pair, epochs), bf16), shapes((rows, epochs), f32),
           shapes((rows, epochs), f32), shapes((n_ctx, 32, shard_len), f32)],
        scratch_shapes=[
            pltpu.VMEM((8, epochs + 512), f32),
            pltpu.VMEM((32, main), f32),
            pltpu.VMEM((2 * pair, wide), bf16),
            pltpu.VMEM((pair, epochs), f32),
            pltpu.VMEM((pair, shard_len), f32),
            pltpu.VMEM((rows, epochs), bf16),
            pltpu.VMEM((3 * pair, channels), bf16),
            pltpu.VMEM((3 * pair, 32), bf16),
        ],
        compiler_params=params,
        name="layers_forward",
    )
    g0, du0, dv0, s_all, g_own, du1, dv1, packed = forward(
        info, fields, a_cat, w_hi, w_lo, mix_res, w_taps, bias1, e_pair
    )
    got = exchange(packed.reshape(n_ctx * 32, shard_len), "ctx").reshape(n_ctx, 32, shard_len)

    n_mix = channels // n_dp
    n_conv = 3 * pair // n_dp
    per = n_mix + n_conv + 8
    backward = pl.pallas_call(
        functools.partial(backward_kernel, dilations[1], half),
        grid=(epochs // main,),
        in_specs=[
            smem,
            whole((n_ctx, 32, shard_len)),
            whole((n_ctx, n_pad, shard_len)),
            whole((2 * half, shard_len)),
            whole((pair, 32)),
            whole((pair, epochs)),
            whole((rows, epochs)),
            whole((rows, epochs)),
            whole((3 * pair, channels)),
            whole((channels, 3 * pair)),
            whole((channels, channels)),
            whole((channels, 3 * pair)),
            whole((32, channels)),
        ]
        + [columns(channels, main)] * 3
        + [columns(32, main)],
        out_specs=[whole((1, half, shard_len)), whole((n_dp, per, channels))],
        out_shape=[shapes((1, half, shard_len), f32), shapes((n_dp, per, channels), bf16)],
        scratch_shapes=[
            pltpu.VMEM((32, shard_len), f32),
            pltpu.VMEM((32, shard_len), f32),
            pltpu.VMEM((pair, wide), bf16),
            pltpu.VMEM((8, wide), f32),
            pltpu.VMEM((rows, epochs), f32),
            pltpu.VMEM((3 * pair, epochs), bf16),
            pltpu.VMEM((3 * pair, channels), f32),
            pltpu.VMEM((channels, channels), f32),
            pltpu.VMEM((32, 2 * channels), f32),
            pltpu.VMEM((32, 3 * pair), f32),
            pltpu.VMEM((16, pair), f32),
            pltpu.VMEM((16, pair), f32),
            pltpu.VMEM((channels, main), f32),
            pltpu.VMEM((16, 2 * channels), f32),
            pltpu.VMEM((8, 256), f32),
            pltpu.VMEM((3 * pair, channels), f32),
            pltpu.VMEM((32, 3 * pair), f32),
        ],
        compiler_params=params,
        name="layers_backward",
    )
    coupled, packed = backward(
        info, got, fields, light_flux[0], e_up, g_own, du1, dv1, w_taps, w_taps.T, mix_res,
        dot(mix_res, w_taps, 0, 1).astype(bf16), w_start, g0, du0, dv0, s_all,
    )
    got = exchange(packed.reshape(n_dp * per, channels), "dp").reshape(n_dp, per, channels)
    got = got.astype(f32).sum(axis=0)
    mix_piece = got[:n_mix]
    conv_piece = got[n_mix : n_mix + n_conv].astype(bf16)
    smalls = got[n_mix + n_conv :]
    m_first = smalls[:, :128] + smalls[:, 384:]
    m_rest = smalls[4:6, 128:256] + smalls[6:8, 128:256]
    m_own = lax.dynamic_slice(
        jnp.concatenate([m_first, m_rest], axis=0), (0, rows * (dp % 2)), (10, rows)
    )
    start_own = jnp.where(dp < channels // 128, smalls[1 : 1 + half, 128:256], 0.0)
    g_own_sum = smalls[: 2 * half, 256:384]
    bias1_own = smalls[0:1, 128:256] + smalls[6:7, 256:384]
    mo_hi, mo_lo = split(m_own)
    mo_pair = jnp.concatenate([mo_hi[:9], mo_lo[:9]], axis=0)
    start_t = 0.0
    for tap in range(3):
        up = dot(mo_pair, conv0[:, tap * channels : (tap + 1) * channels])
        start_t = start_t + up[half * tap : half * tap + half] + up[9 + half * tap : 9 + half * tap + half]
    spot = lax.dynamic_update_slice(
        jnp.zeros((half, channels), f32), start_own, (0, 128 * (dp % (channels // 128)))
    )
    start_t = start_t + spot
    end_last = dot(g_own_sum[:, rows:], mix_last_k, 1, 1, highest)
    end_skip = jnp.where(low, 0.0, dot(g_own_sum[:, :rows], mix_skip_k, 1, 1, highest))
    g_rows = jnp.concatenate([g_own_sum, bias1_own], axis=0)
    parts = jnp.concatenate(
        [
            m_own,
            pad_to(g_rows, 10, 2 * rows),
            pad_to(jnp.concatenate([end_last, end_skip], axis=1), 10, last_rows + rows),
        ],
        axis=1,
    )
    width = parts.shape[1]
    parts_hi, parts_lo = split(parts)
    start_hi, start_lo = split(start_t)
    pack_rows = [
        conv_piece,
        mix_piece.astype(bf16),
        pad_to(jnp.concatenate([parts_hi, parts_lo[:, : 3 * rows]], axis=1), 10, channels),
        start_hi,
        start_lo,
    ]
    packed = jnp.concatenate(pack_rows, axis=0)
    per0 = packed.shape[0]
    per = -(-per0 // 8) * 8
    packed = pad_to(packed, per, channels)
    got = exchange(
        jnp.broadcast_to(packed[None], (n_ctx, per, channels)).reshape(n_ctx * per, channels), "ctx"
    ).reshape(n_ctx, per, channels)
    grad_conv1 = got[:, :n_conv].reshape(n_ctx, 3, part, channels).transpose(0, 2, 1, 3)
    grad_conv1 = grad_conv1.reshape(rows, 3 * channels).astype(f32)
    mix_rows = got[:, n_conv : n_conv + n_mix].astype(f32).sum(axis=0)
    base = n_conv + n_mix
    parts = got[:, base : base + 10].astype(f32)
    parts_lo = parts[:, :, width : width + 3 * rows]
    parts = jnp.concatenate(
        [parts[:, :, : 3 * rows] + parts_lo, parts[:, :, 3 * rows : width]], axis=2
    )
    start_t = got[:, base + 10 : base + 10 + 2 * half].astype(f32).sum(axis=0)
    start_t = start_t[:half] + start_t[half:]
    m_own = parts[:, :, :rows].sum(axis=0)
    g_all = parts[:, : 2 * half, rows : 3 * rows]
    g0_all = g_all[:, :, :rows].transpose(1, 0, 2).reshape(2 * half, channels)
    g1_all = g_all[:, :, rows:].reshape(n_ctx, 2 * half, half_dp, part).transpose(1, 2, 0, 3)
    g1_all = g1_all.reshape(2 * half, channels)
    bias1_all = parts[:, 2 * half, rows : 3 * rows].reshape(n_ctx, n_dp, part).transpose(1, 0, 2)
    bias1_all = bias1_all.reshape(2 * channels)
    end_both = parts[:, : 2 * half, 3 * rows :].sum(axis=0)
    a_grad = m_own[:9].T
    grad_conv0 = jnp.concatenate(
        [
            dot(a_grad[:, half * tap : half * tap + half], start_weight, 1, 1, highest)
            for tap in range(3)
        ],
        axis=1,
    )
    grad_mix_last = dot(ew_last, g1_all, 0, 0, highest)
    skip_rows = dot(ew_skip, g0_all, 0, 0, highest)

    other = lax.ppermute(mix_rows, "dp", [(i + half_dp, i) for i in range(half_dp)])
    final = jnp.concatenate(
        [
            start_t.reshape(-1, 128),
            pad_to(end_both, 2 * half, 128),
            pad_to(m_own[9:10], 1, 128),
        ],
        axis=0,
    )
    per0 = final.shape[0]
    per = -(-per0 // 8) * 8
    final = pad_to(final, per, 128)
    got = exchange(
        jnp.broadcast_to(final[None], (n_dp, per, 128)).reshape(n_dp * per, 128), "dp"
    ).reshape(n_dp, per, 128)
    n_start = half * channels // 128
    grad_start = got[:, :n_start].sum(axis=0).reshape(half, channels).T
    ends = got[:, n_start : n_start + 2 * half]
    grad_end = ends[:, :, :last_rows].transpose(1, 0, 2).reshape(2 * half, channels)
    grad_end = grad_end + ends[half_dp:, :, last_rows : last_rows + rows].transpose(
        1, 0, 2
    ).reshape(2 * half, channels)
    bias0_all = got[:, n_start + 2 * half, :rows].reshape(2 * channels)
    grad_bias = jnp.stack([bias0_all, bias1_all])
    residual = jnp.concatenate([mix_rows, other], axis=0)
    grad_mix_first = jnp.where(low, residual, skip_rows)
    grad_conv = jnp.stack([grad_conv0, grad_conv1])
    return (coupled, grad_start, grad_conv, grad_bias, grad_mix_first, grad_mix_last, grad_end)


def solution(mesh):
    in_specs = (
        P("dp", None, "ctx"),
        P("dp"),
        P("dp", "ctx"),
        P(),
        P(None, "dp", None),
        P(),
        P("dp", None),
        P("dp", None),
        P(),
        P("dp", None, "ctx"),
    )
    out_specs = (
        P("dp", None, "ctx"),
        P(),
        P(None, "dp", None),
        P(),
        P("dp", None),
        P("dp", None),
        P(),
    )
    return jax.shard_map(local, mesh=mesh, in_specs=in_specs, out_specs=out_specs, check_vma=False)
```

```python
import functools

import jax
import jax.numpy as jnp
from jax import lax
from jax.experimental import pallas as pl
from jax.experimental.pallas import tpu as pltpu
from jax.sharding import PartitionSpec as P

BUCKETS = 4
highest = lax.Precision.HIGHEST
bf16 = jnp.bfloat16
f32 = jnp.float32


def dot(a, b, ca=1, cb=0, precision=None):
    return lax.dot_general(
        a, b, (((ca,), (cb,)), ((), ())), precision=precision, preferred_element_type=f32
    )


def split(x):
    hi = lax.reduce_precision(x, 8, 7)
    return hi.astype(bf16), (x - hi).astype(bf16)


def pad_to(x, rows, cols):
    return jnp.pad(x, ((0, rows - x.shape[0]), (0, cols - x.shape[1])))


def shift(x, n):
    total = x.shape[1]
    if n > 0:
        return jnp.pad(x[:, : total - n], ((0, 0), (n, 0)))
    return jnp.pad(x[:, -n:], ((0, 0), (0, -n)))


def tap_of(x, off, dilation, side):
    out = shift(x, side * dilation)
    for step in range(1, BUCKETS):
        out = jnp.where(off == step, shift(x, side * (dilation + step)), out)
    return out


def tap_back(x, off, dilation, side):
    out = 0.0
    for step in range(BUCKETS):
        out = out + shift(jnp.where(off == step, x, 0.0), -side * (dilation + step))
    return out


def exchange(x, axis):
    return lax.all_to_all(x, axis, 0, 0, tiled=True)


def nt(a, b):
    return dot(a, b, 1, 1)


def rolled(x, start, width):
    if start % 128 == 0:
        return x[:, start : start + width]
    return pltpu.roll(x, x.shape[1] - start, 1)[:, :width]


def steps_apart(shape):
    return (
        lax.broadcasted_iota(jnp.int32, shape, 0) - lax.broadcasted_iota(jnp.int32, shape, 1)
    ).astype(f32)


def one_hot(apart, target):
    return jnp.where(apart == target, 1.0, 0.0).astype(bf16)


def valid_row(c, width, length):
    at = lax.broadcasted_iota(jnp.int32, (1, width), 1) + c * width
    return (at < length).astype(f32)


def packet_kernel(
    info, conv, mix_first, mix_far, mix_last, start, ends,
    packet,
    sw, low_rows, ew, turn,
):
    dp = info[0]
    k = info[1]
    n_dp, per, channels = packet.shape
    half = start.shape[0]
    rows = mix_first.shape[0]
    last_rows = mix_last.shape[0]
    n_e = ends.shape[0]
    part = (per - 8 - rows // 2) // 3
    upper = dp >= n_dp // 2

    group = conv[1, pl.ds(pl.multiple_of((k // 2) * 2 * part, 2 * part), 2 * part), :].astype(f32)
    mine = jnp.where(k % 2 == 1, group[part:], group[:part]).astype(bf16)

    sw[...] = jnp.zeros(sw.shape, f32)
    sw[0:half, :] = start[...]
    full = sw[...]
    sw_hi = full.astype(bf16)
    sw_lo = (full - sw_hi.astype(f32)).astype(bf16)
    turn[...] = jnp.zeros(turn.shape, f32)
    for tap in range(3):
        block = conv[0, :, tap * channels : (tap + 1) * channels]
        one = nt(sw_hi, block) + nt(sw_lo, block)
        turn[half * tap : half * (tap + 1), 0:rows] = one[0:half]
    a_t = turn[...]
    a_hi = a_t[0:16].astype(bf16).astype(f32)
    a_lo = a_t[0:16] - a_hi
    lane = lax.broadcasted_iota(jnp.int32, (8, 128), 1)
    row = lax.broadcasted_iota(jnp.int32, (8, 128), 0)
    near = jnp.where(lane < rows, a_hi[0:8], pltpu.roll(a_lo[0:8], rows, 1))
    far = jnp.where(row == 0, a_hi[8:16], pltpu.roll(a_lo[8:16], 1, 0))

    ew[...] = jnp.zeros(ew.shape, f32)
    ew[0:n_e, :] = ends[...]
    e_all = ew[...]
    wide = lax.broadcasted_iota(jnp.int32, (8, 128), 1)

    def product(shift, count, source, keep):
        moved = pltpu.roll(e_all, lax.rem(channels - shift, channels), 1)[:, 0:128]
        moved = jnp.where(jnp.logical_and(wide < count, keep), moved, 0.0)
        hi = moved.astype(bf16)
        low = (moved - hi.astype(f32)).astype(bf16)
        low_rows[...] = jnp.zeros(low_rows.shape, bf16)
        low_rows[0:count, :] = source[...]
        out = dot(hi, low_rows[...]) + dot(low, low_rows[...])
        out_hi = out.astype(bf16)
        return out_hi, (out - out_hi.astype(f32)).astype(bf16)

    at = lax.broadcasted_iota(jnp.int32, (channels, 128), 0)
    col = lax.broadcasted_iota(jnp.int32, (channels, 128), 1)
    m = col - rows
    pick0 = jnp.where(jnp.logical_and(col < rows, at == rows * k + col), 1.0, 0.0).astype(bf16)
    target = (m >> 3) * rows + part * k + (m & 7)
    pick1 = jnp.where(jnp.logical_and(m >= 0, at == target), 1.0, 0.0).astype(bf16)
    e0_hi, e0_lo = product(
        rows * jnp.maximum(dp - n_dp // 2, 0), rows, mix_first, upper
    )
    e1_hi, e1_lo = product(last_rows * dp, last_rows, mix_last, dp >= 0)
    e_hi = dot(e0_hi, pick0) + dot(e1_hi, pick1)
    e_lo = dot(e0_lo, pick0) + dot(e1_lo, pick1)

    send = jnp.where(upper, mix_far[...].astype(f32), mix_first[0 : rows // 2, :].astype(f32))
    send = send.astype(bf16)
    base = 3 * part
    for j in range(n_dp):
        for tap in range(3):
            packet[j, tap * part : (tap + 1) * part, :] = mine[
                :, tap * channels : (tap + 1) * channels
            ]
        packet[j, base : base + 8, 0:128] = e_hi.astype(bf16)
        packet[j, base : base + 8, 128:256] = e_lo.astype(bf16)
        packet[j, base : base + 8, 256:384] = near.astype(bf16)
        packet[j, base : base + 8, 384:512] = far.astype(bf16)
        packet[j, base + 8 :, :] = send


def forward_kernel(
    dil0, dil1, half,
    info, fields, a_cat, w_hi, w_lo, weights, bias1, e_pair,
    g0_out, du0_out, dv0_out, s_out, gown_out, du1_out, dv1_out, packet, mix, w_taps,
    fpad, s_cat, prod, centre, pre_s, g_keep, w_mix, w_start,
):
    i = pl.program_id(0)
    nb = fields.shape[0]
    bw = fields.shape[2]
    rows = gown_out.shape[0] // 2
    channels = mix.shape[0]
    pad0 = 256
    pad1 = dil1 + 128
    length = info[0]
    k = info[1]

    @pl.when(i == 0)
    def _():
        fpad[:, 0:pad0] = jnp.zeros((8, pad0), f32)
        fpad[:, pad0 + nb * bw :] = jnp.zeros((8, pad0), f32)
        prod[:, 0:pad1] = jnp.zeros((prod.shape[0], pad1), bf16)
        prod[:, pad1 + nb * bw :] = jnp.zeros((prod.shape[0], pad1), bf16)
        n_dp = weights.shape[0]
        part = 2 * rows // n_dp
        half_rows = rows // 2
        for j in range(n_dp):
            for tap in range(3):
                to = tap * 2 * rows + j * part
                w_taps[to : to + part, :] = weights[j, tap * part : (tap + 1) * part, :]
            to = rows * (j % (n_dp // 2)) + half_rows * (j // (n_dp // 2))
            mix[to : to + half_rows, :] = weights[j, 4 * part :, :]
        w_mix[...] = dot(w_taps[...], mix[...]).astype(bf16)
        full = dot(w_taps[...], w_hi[...]) + dot(w_taps[...], w_lo[...])
        top = full.astype(bf16).astype(f32)
        col = lax.broadcasted_iota(jnp.int32, full.shape, 1)
        w_start[...] = jnp.where(col < 18, top, full - top).astype(bf16)
        s_cat[...] = jnp.zeros(s_cat.shape, f32)
        s_cat[27:29, :] = jnp.ones((2, g0_out.shape[1]), f32)
        packet[:, 24:32, :] = jnp.zeros((nb, 8, bw), f32)
        for c in range(nb):
            block = fields[c ^ k].astype(f32)
            valid = valid_row(c, bw, length)
            at = slice(pad0 + c * bw, pad0 + (c + 1) * bw)
            fpad[0:half, at] = block[0:half] * valid
            fpad[half : 2 * half, at] = block[2 * half : 3 * half] * valid
            fpad[6:7, at] = block[6 * half : 6 * half + 1]
            fpad[7:8, at] = valid

    mw = g0_out.shape[1]
    base = pl.multiple_of(i * mw, mw)
    near = fpad[:, pl.ds(pl.multiple_of(pad0 + base, 128), mw)]
    off = near[6:7]
    valid = near[7:8]
    behind = fpad[:, pl.ds(pl.multiple_of(base, 128), mw + 2 * dil0)]
    ahead = fpad[:, pl.ds(pl.multiple_of(pad0 + base, 128), mw + 2 * dil0)]
    left = rolled(behind, dil0, mw)
    right = rolled(ahead, dil0, mw)
    for step in range(1, BUCKETS):
        left = jnp.where(off == step, rolled(behind, dil0 - step, mw), left)
        right = jnp.where(off == step, rolled(ahead, dil0 + step, mw), right)
    for part, at in ((left, 0), (near, 3), (right, 6)):
        s_cat[at : at + half, :] = part[0:half]
        s_cat[9 + at : 9 + at + half, :] = part[half : 2 * half]
        s_cat[18 + at : 18 + at + half, :] = part[0:half]
    s_b = s_cat[...].astype(bf16)
    s_out[...] = s_b
    step_rows = 128
    for r in range(0, channels, step_rows):
        u = dot(a_cat[r : r + step_rows, :], s_b)
        v = dot(a_cat[channels + r : channels + r + step_rows, :], s_b)
        t = jnp.tanh(u)
        s = 0.5 * jnp.tanh(0.5 * v) + 0.5
        g = t * s
        g0_out[r : r + step_rows, :] = (g * valid).astype(bf16)
        du0_out[r : r + step_rows, :] = (s - g * t).astype(bf16)
        dv0_out[r : r + step_rows, :] = (g - g * s).astype(bf16)
    pair = 2 * rows
    g_b = g0_out[...]
    for tap in range(3):
        at = slice(tap * pair, (tap + 1) * pair)
        part = dot(w_mix[at, :], g_b) + dot(w_start[at, :], s_b)
        if tap == 1:
            centre[:, pl.ds(base, mw)] = part
        else:
            to = tap // 2 * pair
            cols = pl.ds(pl.multiple_of(pad1 + base, 128), mw)
            prod[to : to + pair, cols] = part.astype(bf16)
    g_keep[:, pl.ds(base, mw)] = g0_out[pl.ds(pl.multiple_of(rows * k, rows), rows), :]

    @pl.when(i == pl.num_programs(0) - 1)
    def _():
        apart = steps_apart((256, 128))

        def body(c, carry):
            base = pl.multiple_of(c * bw, bw)
            off = fpad[6:7, pl.ds(pl.multiple_of(pad0 + base, 128), bw)]
            for tile in range(bw // 128):
                lane = slice(tile * 128, (tile + 1) * 128)
                behind = prod[0:pair, pl.ds(pl.multiple_of(base + tile * 128, 128), 256)]
                ahead = prod[
                    pair:,
                    pl.ds(pl.multiple_of(pad1 + dil1 + base + tile * 128, 128), 256),
                ]
                pre_s[:, lane] = dot(behind, one_hot(apart, 128.0 - off[:, lane])) + dot(
                    ahead, one_hot(apart, off[:, lane])
                )
            pre = pre_s[...] + centre[:, pl.ds(base, bw)] + bias1[...]
            t = jnp.tanh(pre[:rows])
            s = 0.5 * jnp.tanh(0.5 * pre[rows:]) + 0.5
            g = t * s
            du1_out[:, pl.ds(base, bw)] = s - g * t
            dv1_out[:, pl.ds(base, bw)] = g - g * s
            gown_out[0:rows, pl.ds(base, bw)] = g_keep[:, pl.ds(base, bw)]
            gown_out[rows:, pl.ds(base, bw)] = g.astype(bf16)
            part = dot(e_pair[...], gown_out[:, pl.ds(base, bw)])
            part = part[0 : 2 * half] + part[8 : 8 + 2 * half]
            for d in range(nb):
                for h in range(half):
                    packet[d, pl.ds(h * nb + c, 1), :] = part[h : h + 1]
            packet[c, 24 : 24 + half, :] = part[half : 2 * half]
            return carry

        lax.fori_loop(0, nb, body, 0, unroll=2)


def backward_kernel(
    dil1, half,
    info, got, fields, flux, e_up, gown, du1, dv1, w_taps, w_taps_t, mix, w_mix_t, w_start,
    g0, du0, dv0, s_in,
    coupled, packet,
    ends, d_cat, dz_pad, off_pad, d_e0, d_taps, acc_q, acc_mix, acc_m, acc_s, acc_g, acc_b,
    dg, m_rows, share, acc_conv, small,
):
    i = pl.program_id(0)
    nb = fields.shape[0]
    bw = fields.shape[2]
    pair = gown.shape[0]
    rows = pair // 2
    channels = mix.shape[0]
    n_dp = packet.shape[0]
    pad1 = dil1 + 128
    length = info[0]
    k = info[1]

    @pl.when(i == 0)
    def _():
        for ref in (acc_q, acc_m, acc_s, acc_g, acc_b, d_cat, m_rows, share, small):
            ref[...] = jnp.zeros(ref.shape, f32)
        dz_pad[:, 0:pad1] = jnp.zeros((pair, pad1), bf16)
        dz_pad[:, pad1 + nb * bw :] = jnp.zeros((pair, pad1), bf16)
        off_pad[:, 0:pad1] = jnp.full((8, pad1), -1.0, f32)
        off_pad[:, pad1 + nb * bw :] = jnp.full((8, pad1), -1.0, f32)
        total = got[0]
        for src in range(1, nb):
            total = total + got[src]
        ends[...] = total
        mine = valid_row(k, bw, length)
        for h in range(half):
            growth = jnp.exp(ends[pl.ds(h * nb + k, 1), :])
            coupled[0, h : h + 1, :] = (
                growth * flux[half + h : half + h + 1] + ends[24 + h : 25 + h, :]
            ) * mine

        def first(c, carry):
            base = pl.multiple_of(c * bw, bw)
            at = pl.multiple_of(pad1 + base, 128)
            block = fields[c ^ k].astype(f32)
            valid = valid_row(c, bw, length)
            off_pad[0:1, pl.ds(at, bw)] = block[6 * half : 6 * half + 1]
            flux2 = block[half : 2 * half] + block[3 * half : 4 * half]
            cot = (block[4 * half : 5 * half] + block[5 * half : 6 * half]) * valid
            for h in range(half):
                growth = jnp.exp(ends[pl.ds(h * nb + c, 1), :])
                d_cat[h : h + 1, :] = cot[h : h + 1] * growth * flux2[h : h + 1]
            d_cat[half : 2 * half, :] = cot
            full = d_cat[0:8, :]
            hi = full.astype(bf16).astype(f32)
            lo = full - hi
            d_cat[8:16, :] = lo
            d_cat[16:24, :] = hi
            d_gated = dot(e_up[...], d_cat[...].astype(bf16))
            acc_g[...] += nt(d_cat[8:24, :].astype(bf16), gown[:, pl.ds(base, bw)])
            d_e0[:, pl.ds(base, bw)] = d_gated[:rows]
            up = d_gated[rows : 2 * rows]
            dz_pad[0:rows, pl.ds(at, bw)] = (up * du1[:, pl.ds(base, bw)]).astype(bf16)
            dz_pad[rows:, pl.ds(at, bw)] = (up * dv1[:, pl.ds(base, bw)]).astype(bf16)
            return carry

        lax.fori_loop(0, nb, first, 0, unroll=2)

        apart = steps_apart((128, 256))

        def second(c, carry):
            base = pl.multiple_of(c * bw, bw)
            valid = valid_row(c, bw, length)
            for tile in range(bw // 128):
                lane = pl.ds(pl.multiple_of(base + tile * 128, 128), 128)
                late = pl.ds(pl.multiple_of(pad1 + dil1 + base + tile * 128, 128), 256)
                early = pl.ds(pl.multiple_of(base + tile * 128, 128), 256)
                left = nt(dz_pad[:, late], one_hot(apart, -off_pad[0:1, late]))
                right = nt(dz_pad[:, early], one_hot(apart, off_pad[0:1, early] - 128.0))
                d_taps[0:pair, lane] = left.astype(bf16)
                d_taps[2 * pair :, lane] = (
                    right * valid[:, tile * 128 : (tile + 1) * 128]
                ).astype(bf16)
            centre = dz_pad[:, pl.ds(pl.multiple_of(pad1 + base, 128), bw)]
            d_taps[pair : 2 * pair, pl.ds(base, bw)] = centre
            acc_b[...] += nt(jnp.ones((16, bw), bf16), centre)
            return carry

        lax.fori_loop(0, nb, second, 0, unroll=2)

    mw = g0.shape[1]
    base = pl.multiple_of(i * mw, mw)
    d_blk = d_taps[:, pl.ds(base, mw)]
    s_b = s_in[...]
    acc_q[...] += nt(d_blk, g0[...])
    acc_s[...] += nt(s_b, d_blk)
    dg[...] = dot(w_mix_t[...], d_blk)
    own = pl.ds(pl.multiple_of(rows * k, rows), rows)
    dg[own, :] = dg[own, :] + d_e0[:, pl.ds(base, mw)]
    up = dg[...]
    acc_m[:, 0:channels] += nt(s_b, (up * du0[...].astype(f32)).astype(bf16))
    acc_m[:, channels:] += nt(s_b, (up * dv0[...].astype(f32)).astype(bf16))

    @pl.when(i == pl.num_programs(0) - 1)
    def _():
        per_mix = channels // n_dp
        eighth = pair // n_dp
        q = acc_q[...]
        q_hi = q.astype(bf16)
        small[0:half, :] = acc_s[3 : 3 + half, :] + acc_s[12 : 12 + half, :]
        seen = small[0:8, :]
        seen_hi = seen.astype(bf16).astype(f32)
        small[8:16, :] = seen - seen_hi
        small[16:24, :] = seen
        d_start = small[...].astype(bf16)
        acc_conv[...] = nt(q_hi, mix[...]) + dot(d_start, w_start[...], 0, 0)
        acc_mix[...] = dot(w_taps_t[...], q_hi)
        starts = dot(d_start, w_taps[...])
        starts = starts[0:half] + starts[8 : 8 + half]
        m_rows[0:9, :] = acc_m[0:9, :] + acc_m[9:18, :]
        m_rows[9:10, :] = acc_m[27:28, :]
        bias = acc_b[0:1, :]
        share[0:1, 0:128] = bias
        share[6:7, 128:256] = bias - bias.astype(bf16).astype(f32)
        share[0 : 2 * half, 128:256] = acc_g[8 : 8 + 2 * half, :] + acc_g[0 : 2 * half, :]
        for j in range(n_dp):
            row = 64 * (j % (n_dp // 2)) + per_mix * (j // (n_dp // 2))
            packet[j, 0:per_mix, :] = acc_mix[row : row + per_mix, :].astype(bf16)
            for tap in range(3):
                at = per_mix + tap * eighth
                row = tap * pair + j * eighth
                packet[j, at : at + eighth, :] = acc_conv[row : row + eighth, :].astype(bf16)
            if j < channels // 128:
                share[1 : 1 + half, 0:128] = starts[:, 128 * j : 128 * (j + 1)]
            else:
                share[1 : 1 + half, 0:128] = jnp.zeros((half, 128), f32)
            at = per_mix + 3 * eighth
            cols = slice(128 * (j // 2), 128 * (j // 2) + 128)
            share[6:8, 0:128] = m_rows[8:10, cols]
            low = m_rows[0:10, cols]
            low = low - low.astype(bf16).astype(f32)
            share[4:6, 0:128] = low[8:10]
            packet[j, at : at + 8, 0:128] = m_rows[0:8, cols].astype(bf16)
            packet[j, at : at + 8, 128:256] = share[:, 0:128].astype(bf16)
            packet[j, at : at + 8, 256:384] = share[:, 128:256].astype(bf16)
            packet[j, at : at + 8, 384:512] = low[0:8].astype(bf16)


def whole(shape):
    return pl.BlockSpec(shape, lambda i: (0,) * len(shape))


def columns(rows, width):
    return pl.BlockSpec((rows, width), lambda i: (0, i))


def local(
    light_flux,
    lengths,
    offsets,
    start_weight,
    conv_weight,
    gate_bias,
    mix_first,
    mix_last,
    end_weight,
    cotangent,
):
    n_dp = lax.axis_size("dp")
    n_ctx = lax.axis_size("ctx")
    half_dp = n_dp // 2
    dp = lax.axis_index("dp")
    k = lax.axis_index("ctx")
    low = dp < half_dp
    shard_len = light_flux.shape[2]
    half = light_flux.shape[1] // 2
    channels = start_weight.shape[0]
    epochs = shard_len * n_ctx
    dilations = (shard_len // 4, shard_len + shard_len // 2)
    rows = conv_weight.shape[1]
    last_rows = mix_last.shape[0]
    conv0, conv1 = conv_weight[0], conv_weight[1]
    part = rows // n_ctx
    n_e = 2 * half

    def strided(x):
        lead = x.shape[0]
        cols = x.shape[1]
        view = x.reshape(lead, cols // rows, n_ctx, part)
        return lax.dynamic_slice(
            view, (0, 0, k, 0), (lead, cols // rows, 1, part)
        ).reshape(lead, cols // n_ctx)

    half_rows = rows // 2
    mix_far = lax.ppermute(
        mix_first[half_rows:], "dp", [(i, i + half_dp) for i in range(half_dp)]
    )
    sw_hi, sw_lo = split(start_weight)
    ew_last = lax.dynamic_slice(end_weight, (0, last_rows * dp), (n_e, last_rows))
    ew_skip = lax.dynamic_slice(
        end_weight, (0, rows * jnp.maximum(dp - half_dp, 0)), (n_e, rows)
    )
    ew_skip = jnp.where(low, 0.0, ew_skip)
    mix_last_k = strided(mix_last).astype(f32)
    mix_skip_k = lax.dynamic_slice(mix_first, (0, rows * k), (rows, rows)).astype(f32)
    per = 3 * part + 8 + half_rows
    smem = pl.BlockSpec(memory_space=pltpu.SMEM)
    packets = pl.pallas_call(
        packet_kernel,
        in_specs=[smem] + [pl.BlockSpec(memory_space=pltpu.VMEM)] * 6,
        out_specs=pl.BlockSpec(memory_space=pltpu.VMEM),
        out_shape=jax.ShapeDtypeStruct((n_dp, per, channels), bf16),
        scratch_shapes=[
            pltpu.VMEM((16, channels), f32),
            pltpu.VMEM((128, channels), bf16),
            pltpu.VMEM((8, channels), f32),
            pltpu.VMEM((16, 128), f32),
        ],
        name="weight_packets",
    )(jnp.stack([dp, k]), conv_weight, mix_first, mix_far, mix_last, start_weight.T, end_weight)
    got = exchange(packets.reshape(n_dp * per, channels), "dp").reshape(n_dp, per, channels)
    flux_hi, flux_lo = split(light_flux[0])
    cot_hi, cot_lo = split(cotangent[0])
    n_in = 6 * half + 1
    inputs = jnp.concatenate(
        [flux_hi, flux_lo, cot_hi, cot_lo, offsets.astype(bf16)], axis=0
    )
    n_pad = -(-n_in // 8) * 8
    inputs = pad_to(inputs, n_pad, shard_len)

    fields = inputs[None]
    while fields.shape[0] < n_ctx:
        hop = fields.shape[0]
        other = lax.ppermute(fields, "ctx", [(c, c ^ hop) for c in range(n_ctx)])
        fields = jnp.concatenate([fields, other], axis=0)
    weights = got
    e_k = got[:, 3 * part : 3 * part + n_e, : 4 * rows].astype(f32).sum(axis=0)
    e_cat = e_k[:, : 2 * rows] + e_k[:, 2 * rows :]
    a_got = got[:, 3 * part : 4 * part, 4 * rows :]
    a_all = jnp.concatenate(
        [
            a_got[:, :, :rows],
            a_got[:, 0:1, 2 * rows : 3 * rows],
            a_got[:, :, rows : 2 * rows],
            a_got[:, 1:2, 2 * rows : 3 * rows],
        ],
        axis=1,
    )
    a_all = a_all.transpose(1, 0, 2).reshape(18, n_dp * rows)
    a_hi, a_lo = a_all[:9], a_all[9:]

    gap = jnp.zeros((8 - half, channels), bf16)
    w_start = jnp.concatenate(
        [sw_hi.T, gap, sw_hi.T, gap, sw_lo.T, gap, jnp.zeros((8, channels), bf16)], axis=0
    )
    fields, w_start = lax.optimization_barrier((fields, w_start))

    length = lengths[0]
    b_hi, b_lo = split(gate_bias[0][None])
    a_cat = jnp.concatenate(
        [a_hi, a_hi, a_lo, b_hi, b_lo, jnp.zeros((3, 2 * channels), bf16)], axis=0
    ).T
    w_hi, w_lo = (
        jnp.concatenate([jnp.pad(x, ((0, 0), (3, 6 - half)))] * 3 + [jnp.zeros((channels, 5), bf16)], axis=1)
        for x in (sw_hi, sw_lo)
    )
    ec_hi, ec_lo = split(e_cat)
    gap = jnp.zeros((2, 2 * rows), bf16)
    e_pair = jnp.concatenate([ec_hi, gap, ec_lo, gap], axis=0)
    e_up = pad_to(jnp.concatenate([ec_hi, gap, ec_hi, gap, ec_lo], axis=0), 32, 2 * rows).T
    bias1 = strided(gate_bias[1][None]).T
    info = jnp.stack([length, k])
    pair = 2 * rows
    main = 2 * shard_len
    wide = epochs + 2 * (dilations[1] + 128)
    smem = pl.BlockSpec(memory_space=pltpu.SMEM)
    shapes = jax.ShapeDtypeStruct
    params = pltpu.CompilerParams(
        dimension_semantics=("arbitrary",), vmem_limit_bytes=60000 * 1024
    )
    forward = pl.pallas_call(
        functools.partial(forward_kernel, dilations[0], dilations[1], half),
        grid=(epochs // main,),
        in_specs=[
            smem,
            whole((n_ctx, n_pad, shard_len)),
            whole(a_cat.shape),
            whole(w_hi.shape),
            whole(w_lo.shape),
            whole(weights.shape),
            whole(bias1.shape),
            whole(e_pair.shape),
        ],
        out_specs=[columns(channels, main)] * 3
        + [columns(32, main), whole((pair, epochs)), whole((rows, epochs)),
           whole((rows, epochs)), whole((n_ctx, 32, shard_len)),
           whole((channels, channels)), whole((3 * pair, channels))],
        out_shape=[shapes((channels, epochs), bf16)] * 3
        + [shapes((32, epochs), bf16), shapes((pair, epochs), bf16), shapes((rows, epochs), f32),
           shapes((rows, epochs), f32), shapes((n_ctx, 32, shard_len), f32),
           shapes((channels, channels), bf16), shapes((3 * pair, channels), bf16)],
        scratch_shapes=[
            pltpu.VMEM((8, epochs + 512), f32),
            pltpu.VMEM((32, main), f32),
            pltpu.VMEM((2 * pair, wide), bf16),
            pltpu.VMEM((pair, epochs), f32),
            pltpu.VMEM((pair, shard_len), f32),
            pltpu.VMEM((rows, epochs), bf16),
            pltpu.VMEM((3 * pair, channels), bf16),
            pltpu.VMEM((3 * pair, 32), bf16),
        ],
        compiler_params=params,
        name="layers_forward",
    )
    g0, du0, dv0, s_all, g_own, du1, dv1, packed, mix_res, w_taps = forward(
        info, fields, a_cat, w_hi, w_lo, weights, bias1, e_pair
    )
    got = exchange(packed.reshape(n_ctx * 32, shard_len), "ctx").reshape(n_ctx, 32, shard_len)

    n_mix = channels // n_dp
    n_conv = 3 * pair // n_dp
    per = n_mix + n_conv + 8
    backward = pl.pallas_call(
        functools.partial(backward_kernel, dilations[1], half),
        grid=(epochs // main,),
        in_specs=[
            smem,
            whole((n_ctx, 32, shard_len)),
            whole((n_ctx, n_pad, shard_len)),
            whole((2 * half, shard_len)),
            whole((pair, 32)),
            whole((pair, epochs)),
            whole((rows, epochs)),
            whole((rows, epochs)),
            whole((3 * pair, channels)),
            whole((channels, 3 * pair)),
            whole((channels, channels)),
            whole((channels, 3 * pair)),
            whole((32, channels)),
        ]
        + [columns(channels, main)] * 3
        + [columns(32, main)],
        out_specs=[whole((1, half, shard_len)), whole((n_dp, per, channels))],
        out_shape=[shapes((1, half, shard_len), f32), shapes((n_dp, per, channels), bf16)],
        scratch_shapes=[
            pltpu.VMEM((32, shard_len), f32),
            pltpu.VMEM((32, shard_len), f32),
            pltpu.VMEM((pair, wide), bf16),
            pltpu.VMEM((8, wide), f32),
            pltpu.VMEM((rows, epochs), f32),
            pltpu.VMEM((3 * pair, epochs), bf16),
            pltpu.VMEM((3 * pair, channels), f32),
            pltpu.VMEM((channels, channels), f32),
            pltpu.VMEM((32, 2 * channels), f32),
            pltpu.VMEM((32, 3 * pair), f32),
            pltpu.VMEM((16, pair), f32),
            pltpu.VMEM((16, pair), f32),
            pltpu.VMEM((channels, main), f32),
            pltpu.VMEM((16, 2 * channels), f32),
            pltpu.VMEM((8, 256), f32),
            pltpu.VMEM((3 * pair, channels), f32),
            pltpu.VMEM((32, 3 * pair), f32),
        ],
        compiler_params=params,
        name="layers_backward",
    )
    coupled, packed = backward(
        info, got, fields, light_flux[0], e_up, g_own, du1, dv1, w_taps, w_taps.T, mix_res,
        dot(mix_res, w_taps, 0, 1).astype(bf16), w_start, g0, du0, dv0, s_all,
    )
    got = exchange(packed.reshape(n_dp * per, channels), "dp").reshape(n_dp, per, channels)
    got = got.astype(f32).sum(axis=0)
    mix_piece = got[:n_mix]
    conv_piece = got[n_mix : n_mix + n_conv].astype(bf16)
    smalls = got[n_mix + n_conv :]
    m_first = smalls[:, :128] + smalls[:, 384:]
    m_rest = smalls[4:6, 128:256] + smalls[6:8, 128:256]
    m_own = lax.dynamic_slice(
        jnp.concatenate([m_first, m_rest], axis=0), (0, rows * (dp % 2)), (10, rows)
    )
    start_own = jnp.where(dp < channels // 128, smalls[1 : 1 + half, 128:256], 0.0)
    g_own_sum = smalls[: 2 * half, 256:384]
    bias1_own = smalls[0:1, 128:256] + smalls[6:7, 256:384]
    mo_hi, mo_lo = split(m_own)
    mo_pair = jnp.concatenate([mo_hi[:9], mo_lo[:9]], axis=0)
    start_t = 0.0
    for tap in range(3):
        up = dot(mo_pair, conv0[:, tap * channels : (tap + 1) * channels])
        start_t = start_t + up[half * tap : half * tap + half] + up[9 + half * tap : 9 + half * tap + half]
    spot = lax.dynamic_update_slice(
        jnp.zeros((half, channels), f32), start_own, (0, 128 * (dp % (channels // 128)))
    )
    start_t = start_t + spot
    end_last = dot(g_own_sum[:, rows:], mix_last_k, 1, 1, highest)
    end_skip = jnp.where(low, 0.0, dot(g_own_sum[:, :rows], mix_skip_k, 1, 1, highest))
    g_rows = jnp.concatenate([g_own_sum, bias1_own], axis=0)
    parts = jnp.concatenate(
        [
            m_own,
            pad_to(g_rows, 10, 2 * rows),
            pad_to(jnp.concatenate([end_last, end_skip], axis=1), 10, last_rows + rows),
        ],
        axis=1,
    )
    width = parts.shape[1]
    parts_hi, parts_lo = split(parts)
    start_hi, start_lo = split(start_t)
    pack_rows = [
        conv_piece,
        mix_piece.astype(bf16),
        pad_to(jnp.concatenate([parts_hi, parts_lo[:, : 3 * rows]], axis=1), 10, channels),
        start_hi,
        start_lo,
    ]
    packed = jnp.concatenate(pack_rows, axis=0)
    per0 = packed.shape[0]
    per = -(-per0 // 8) * 8
    packed = pad_to(packed, per, channels)
    got = exchange(
        jnp.broadcast_to(packed[None], (n_ctx, per, channels)).reshape(n_ctx * per, channels), "ctx"
    ).reshape(n_ctx, per, channels)
    grad_conv1 = got[:, :n_conv].reshape(n_ctx, 3, part, channels).transpose(0, 2, 1, 3)
    grad_conv1 = grad_conv1.reshape(rows, 3 * channels).astype(f32)
    mix_rows = got[:, n_conv : n_conv + n_mix].astype(f32).sum(axis=0)
    base = n_conv + n_mix
    parts = got[:, base : base + 10].astype(f32)
    parts_lo = parts[:, :, width : width + 3 * rows]
    parts = jnp.concatenate(
        [parts[:, :, : 3 * rows] + parts_lo, parts[:, :, 3 * rows : width]], axis=2
    )
    start_t = got[:, base + 10 : base + 10 + 2 * half].astype(f32).sum(axis=0)
    start_t = start_t[:half] + start_t[half:]
    m_own = parts[:, :, :rows].sum(axis=0)
    g_all = parts[:, : 2 * half, rows : 3 * rows]
    g0_all = g_all[:, :, :rows].transpose(1, 0, 2).reshape(2 * half, channels)
    g1_all = g_all[:, :, rows:].reshape(n_ctx, 2 * half, half_dp, part).transpose(1, 2, 0, 3)
    g1_all = g1_all.reshape(2 * half, channels)
    bias1_all = parts[:, 2 * half, rows : 3 * rows].reshape(n_ctx, n_dp, part).transpose(1, 0, 2)
    bias1_all = bias1_all.reshape(2 * channels)
    end_both = parts[:, : 2 * half, 3 * rows :].sum(axis=0)
    a_grad = m_own[:9].T
    grad_conv0 = jnp.concatenate(
        [
            dot(a_grad[:, half * tap : half * tap + half], start_weight, 1, 1, highest)
            for tap in range(3)
        ],
        axis=1,
    )
    grad_mix_last = dot(ew_last, g1_all, 0, 0, highest)
    skip_rows = dot(ew_skip, g0_all, 0, 0, highest)

    other = lax.ppermute(mix_rows, "dp", [(i + half_dp, i) for i in range(half_dp)])
    final = jnp.concatenate(
        [
            start_t.reshape(-1, 128),
            pad_to(end_both, 2 * half, 128),
            pad_to(m_own[9:10], 1, 128),
        ],
        axis=0,
    )
    per0 = final.shape[0]
    per = -(-per0 // 8) * 8
    final = pad_to(final, per, 128)
    got = exchange(
        jnp.broadcast_to(final[None], (n_dp, per, 128)).reshape(n_dp * per, 128), "dp"
    ).reshape(n_dp, per, 128)
    n_start = half * channels // 128
    grad_start = got[:, :n_start].sum(axis=0).reshape(half, channels).T
    ends = got[:, n_start : n_start + 2 * half]
    grad_end = ends[:, :, :last_rows].transpose(1, 0, 2).reshape(2 * half, channels)
    grad_end = grad_end + ends[half_dp:, :, last_rows : last_rows + rows].transpose(
        1, 0, 2
    ).reshape(2 * half, channels)
    bias0_all = got[:, n_start + 2 * half, :rows].reshape(2 * channels)
    grad_bias = jnp.stack([bias0_all, bias1_all])
    residual = jnp.concatenate([mix_rows, other], axis=0)
    grad_mix_first = jnp.where(low, residual, skip_rows)
    grad_conv = jnp.stack([grad_conv0, grad_conv1])
    return (coupled, grad_start, grad_conv, grad_bias, grad_mix_first, grad_mix_last, grad_end)


def solution(mesh):
    in_specs = (
        P("dp", None, "ctx"),
        P("dp"),
        P("dp", "ctx"),
        P(),
        P(None, "dp", None),
        P(),
        P("dp", None),
        P("dp", None),
        P(),
        P("dp", None, "ctx"),
    )
    out_specs = (
        P("dp", None, "ctx"),
        P(),
        P(None, "dp", None),
        P(),
        P("dp", None),
        P("dp", None),
        P(),
    )
    return jax.shard_map(local, mesh=mesh, in_specs=in_specs, out_specs=out_specs, check_vma=False)
```

```python
import functools

import jax
import jax.numpy as jnp
from jax import lax
from jax.experimental import pallas as pl
from jax.experimental.pallas import tpu as pltpu
from jax.sharding import PartitionSpec as P

BUCKETS = 4
highest = lax.Precision.HIGHEST
bf16 = jnp.bfloat16
f32 = jnp.float32


def dot(a, b, ca=1, cb=0, precision=None):
    return lax.dot_general(
        a, b, (((ca,), (cb,)), ((), ())), precision=precision, preferred_element_type=f32
    )


def split(x):
    hi = lax.reduce_precision(x, 8, 7)
    return hi.astype(bf16), (x - hi).astype(bf16)


def pad_to(x, rows, cols):
    return jnp.pad(x, ((0, rows - x.shape[0]), (0, cols - x.shape[1])))


def shift(x, n):
    total = x.shape[1]
    if n > 0:
        return jnp.pad(x[:, : total - n], ((0, 0), (n, 0)))
    return jnp.pad(x[:, -n:], ((0, 0), (0, -n)))


def tap_of(x, off, dilation, side):
    out = shift(x, side * dilation)
    for step in range(1, BUCKETS):
        out = jnp.where(off == step, shift(x, side * (dilation + step)), out)
    return out


def tap_back(x, off, dilation, side):
    out = 0.0
    for step in range(BUCKETS):
        out = out + shift(jnp.where(off == step, x, 0.0), -side * (dilation + step))
    return out


def exchange(x, axis):
    return lax.all_to_all(x, axis, 0, 0, tiled=True)


def nt(a, b):
    return dot(a, b, 1, 1)


def rolled(x, start, width):
    if start % 128 == 0:
        return x[:, start : start + width]
    return pltpu.roll(x, x.shape[1] - start, 1)[:, :width]


def steps_apart(shape):
    return (
        lax.broadcasted_iota(jnp.int32, shape, 0) - lax.broadcasted_iota(jnp.int32, shape, 1)
    ).astype(f32)


def one_hot(apart, target):
    return jnp.where(apart == target, 1.0, 0.0).astype(bf16)


def valid_row(c, width, length):
    at = lax.broadcasted_iota(jnp.int32, (1, width), 1) + c * width
    return (at < length).astype(f32)


def packet_kernel(
    info, conv, mix_first, mix_far, mix_last, start, ends,
    packet,
    sw, low_rows, ew, turn,
):
    dp = info[0]
    k = info[1]
    n_dp, per, channels = packet.shape
    half = start.shape[0]
    rows = mix_first.shape[0]
    last_rows = mix_last.shape[0]
    n_e = ends.shape[0]
    part = (per - 8 - rows // 2) // 3
    upper = dp >= n_dp // 2

    group = conv[1, pl.ds(pl.multiple_of((k // 2) * 2 * part, 2 * part), 2 * part), :].astype(f32)
    mine = jnp.where(k % 2 == 1, group[part:], group[:part]).astype(bf16)

    sw[...] = jnp.zeros(sw.shape, f32)
    sw[0:half, :] = start[...]
    full = sw[...]
    sw_hi = full.astype(bf16)
    sw_lo = (full - sw_hi.astype(f32)).astype(bf16)
    turn[...] = jnp.zeros(turn.shape, f32)
    for tap in range(3):
        block = conv[0, :, tap * channels : (tap + 1) * channels]
        one = nt(sw_hi, block) + nt(sw_lo, block)
        turn[half * tap : half * (tap + 1), 0:rows] = one[0:half]
    a_t = turn[...]
    a_hi = a_t[0:16].astype(bf16).astype(f32)
    a_lo = a_t[0:16] - a_hi
    lane = lax.broadcasted_iota(jnp.int32, (8, 128), 1)
    row = lax.broadcasted_iota(jnp.int32, (8, 128), 0)
    near = jnp.where(lane < rows, a_hi[0:8], pltpu.roll(a_lo[0:8], rows, 1))
    far = jnp.where(row == 0, a_hi[8:16], pltpu.roll(a_lo[8:16], 1, 0))

    ew[...] = jnp.zeros(ew.shape, f32)
    ew[0:n_e, :] = ends[...]
    e_all = ew[...]
    wide = lax.broadcasted_iota(jnp.int32, (8, 128), 1)

    def product(shift, count, source, keep):
        moved = pltpu.roll(e_all, lax.rem(channels - shift, channels), 1)[:, 0:128]
        moved = jnp.where(jnp.logical_and(wide < count, keep), moved, 0.0)
        hi = moved.astype(bf16)
        low = (moved - hi.astype(f32)).astype(bf16)
        low_rows[...] = jnp.zeros(low_rows.shape, bf16)
        low_rows[0:count, :] = source[...]
        out = dot(hi, low_rows[...]) + dot(low, low_rows[...])
        out_hi = out.astype(bf16)
        return out_hi, (out - out_hi.astype(f32)).astype(bf16)

    at = lax.broadcasted_iota(jnp.int32, (channels, 128), 0)
    col = lax.broadcasted_iota(jnp.int32, (channels, 128), 1)
    m = col - rows
    pick0 = jnp.where(jnp.logical_and(col < rows, at == rows * k + col), 1.0, 0.0).astype(bf16)
    target = (m >> 3) * rows + part * k + (m & 7)
    pick1 = jnp.where(jnp.logical_and(m >= 0, at == target), 1.0, 0.0).astype(bf16)
    e0_hi, e0_lo = product(
        rows * jnp.maximum(dp - n_dp // 2, 0), rows, mix_first, upper
    )
    e1_hi, e1_lo = product(last_rows * dp, last_rows, mix_last, dp >= 0)
    e_hi = dot(e0_hi, pick0) + dot(e1_hi, pick1)
    e_lo = dot(e0_lo, pick0) + dot(e1_lo, pick1)

    send = jnp.where(upper, mix_far[...].astype(f32), mix_first[0 : rows // 2, :].astype(f32))
    send = send.astype(bf16)
    base = 3 * part
    for j in range(n_dp):
        for tap in range(3):
            packet[j, tap * part : (tap + 1) * part, :] = mine[
                :, tap * channels : (tap + 1) * channels
            ]
        packet[j, base : base + 8, 0:128] = e_hi.astype(bf16)
        packet[j, base : base + 8, 128:256] = e_lo.astype(bf16)
        packet[j, base : base + 8, 256:384] = near.astype(bf16)
        packet[j, base : base + 8, 384:512] = far.astype(bf16)
        packet[j, base + 8 :, :] = send


def forward_kernel(
    dil0, dil1, half,
    info, fields, a_cat, w_hi, w_lo, weights, bias1, e_pair,
    g0_out, du0_out, dv0_out, s_out, gown_out, du1_out, dv1_out, packet, mix, w_taps,
    fpad, s_cat, prod, centre, pre_s, g_keep, w_mix, w_start,
):
    i = pl.program_id(0)
    nb = fields.shape[0]
    bw = fields.shape[2]
    rows = gown_out.shape[0] // 2
    channels = mix.shape[0]
    pad0 = 256
    pad1 = dil1 + 128
    length = info[0]
    k = info[1]

    @pl.when(i == 0)
    def _():
        fpad[:, 0:pad0] = jnp.zeros((8, pad0), f32)
        fpad[:, pad0 + nb * bw :] = jnp.zeros((8, pad0), f32)
        prod[:, 0:pad1] = jnp.zeros((prod.shape[0], pad1), bf16)
        prod[:, pad1 + nb * bw :] = jnp.zeros((prod.shape[0], pad1), bf16)
        n_dp = weights.shape[0]
        part = 2 * rows // n_dp
        half_rows = rows // 2
        for j in range(n_dp):
            for tap in range(3):
                to = tap * 2 * rows + j * part
                w_taps[to : to + part, :] = weights[j, tap * part : (tap + 1) * part, :]
            to = rows * (j % (n_dp // 2)) + half_rows * (j // (n_dp // 2))
            mix[to : to + half_rows, :] = weights[j, 4 * part :, :]
        w_mix[...] = dot(w_taps[...], mix[...]).astype(bf16)
        full = dot(w_taps[...], w_hi[...]) + dot(w_taps[...], w_lo[...])
        top = full.astype(bf16).astype(f32)
        col = lax.broadcasted_iota(jnp.int32, full.shape, 1)
        w_start[...] = jnp.where(col < 18, top, full - top).astype(bf16)
        s_cat[...] = jnp.zeros(s_cat.shape, f32)
        s_cat[27:29, :] = jnp.ones((2, g0_out.shape[1]), f32)
        packet[:, 24:32, :] = jnp.zeros((nb, 8, bw), f32)
        for c in range(nb):
            block = fields[c ^ k].astype(f32)
            valid = valid_row(c, bw, length)
            at = slice(pad0 + c * bw, pad0 + (c + 1) * bw)
            fpad[0:half, at] = block[0:half] * valid
            fpad[half : 2 * half, at] = block[2 * half : 3 * half] * valid
            fpad[6:7, at] = block[6 * half : 6 * half + 1]
            fpad[7:8, at] = valid

    mw = g0_out.shape[1]
    base = pl.multiple_of(i * mw, mw)
    near = fpad[:, pl.ds(pl.multiple_of(pad0 + base, 128), mw)]
    off = near[6:7]
    valid = near[7:8]
    behind = fpad[:, pl.ds(pl.multiple_of(base, 128), mw + 2 * dil0)]
    ahead = fpad[:, pl.ds(pl.multiple_of(pad0 + base, 128), mw + 2 * dil0)]
    left = rolled(behind, dil0, mw)
    right = rolled(ahead, dil0, mw)
    for step in range(1, BUCKETS):
        left = jnp.where(off == step, rolled(behind, dil0 - step, mw), left)
        right = jnp.where(off == step, rolled(ahead, dil0 + step, mw), right)
    for part, at in ((left, 0), (near, 3), (right, 6)):
        s_cat[at : at + half, :] = part[0:half]
        s_cat[9 + at : 9 + at + half, :] = part[half : 2 * half]
        s_cat[18 + at : 18 + at + half, :] = part[0:half]
    s_b = s_cat[...].astype(bf16)
    s_out[...] = s_b
    step_rows = 128
    for r in range(0, channels, step_rows):
        u = dot(a_cat[r : r + step_rows, :], s_b)
        v = dot(a_cat[channels + r : channels + r + step_rows, :], s_b)
        t = jnp.tanh(u)
        s = 0.5 * jnp.tanh(0.5 * v) + 0.5
        g = t * s
        g0_out[r : r + step_rows, :] = (g * valid).astype(bf16)
        du0_out[r : r + step_rows, :] = (s - g * t).astype(bf16)
        dv0_out[r : r + step_rows, :] = (g - g * s).astype(bf16)
    pair = 2 * rows
    g_b = g0_out[...]
    for tap in range(3):
        at = slice(tap * pair, (tap + 1) * pair)
        part = dot(w_mix[at, :], g_b) + dot(w_start[at, :], s_b)
        if tap == 1:
            centre[:, pl.ds(base, mw)] = part
        else:
            to = tap // 2 * pair
            cols = pl.ds(pl.multiple_of(pad1 + base, 128), mw)
            prod[to : to + pair, cols] = part.astype(bf16)
    g_keep[:, pl.ds(base, mw)] = g0_out[pl.ds(pl.multiple_of(rows * k, rows), rows), :]

    @pl.when(i == pl.num_programs(0) - 1)
    def _():
        apart = steps_apart((256, 128))

        def body(c, carry):
            base = pl.multiple_of(c * bw, bw)
            off = fpad[6:7, pl.ds(pl.multiple_of(pad0 + base, 128), bw)]
            for tile in range(bw // 128):
                lane = slice(tile * 128, (tile + 1) * 128)
                behind = prod[0:pair, pl.ds(pl.multiple_of(base + tile * 128, 128), 256)]
                ahead = prod[
                    pair:,
                    pl.ds(pl.multiple_of(pad1 + dil1 + base + tile * 128, 128), 256),
                ]
                pre_s[:, lane] = dot(behind, one_hot(apart, 128.0 - off[:, lane])) + dot(
                    ahead, one_hot(apart, off[:, lane])
                )
            pre = pre_s[...] + centre[:, pl.ds(base, bw)] + bias1[...]
            t = jnp.tanh(pre[:rows])
            s = 0.5 * jnp.tanh(0.5 * pre[rows:]) + 0.5
            g = t * s
            du1_out[:, pl.ds(base, bw)] = s - g * t
            dv1_out[:, pl.ds(base, bw)] = g - g * s
            gown_out[0:rows, pl.ds(base, bw)] = g_keep[:, pl.ds(base, bw)]
            gown_out[rows:, pl.ds(base, bw)] = g.astype(bf16)
            part = dot(e_pair[...], gown_out[:, pl.ds(base, bw)])
            part = part[0 : 2 * half] + part[8 : 8 + 2 * half]
            for d in range(nb):
                for h in range(half):
                    packet[d, pl.ds(h * nb + c, 1), :] = part[h : h + 1]
            packet[c, 24 : 24 + half, :] = part[half : 2 * half]
            return carry

        lax.fori_loop(0, nb, body, 0, unroll=2)


def backward_kernel(
    dil1, half,
    info, got, fields, flux, e_up, gown, du1, dv1, w_taps, w_taps_t, mix, w_mix_t, w_start,
    g0, du0, dv0, s_in,
    coupled, packet,
    ends, d_cat, dz_pad, off_pad, d_e0, d_taps, acc_q, acc_mix, acc_m, acc_s, acc_g, acc_b,
    dg, m_rows, share, acc_conv, small,
):
    i = pl.program_id(0)
    nb = fields.shape[0]
    bw = fields.shape[2]
    pair = gown.shape[0]
    rows = pair // 2
    channels = mix.shape[0]
    n_dp = packet.shape[0]
    pad1 = dil1 + 128
    length = info[0]
    k = info[1]

    @pl.when(i == 0)
    def _():
        for ref in (acc_q, acc_m, acc_s, acc_g, acc_b, d_cat, m_rows, share, small):
            ref[...] = jnp.zeros(ref.shape, f32)
        dz_pad[:, 0:pad1] = jnp.zeros((pair, pad1), bf16)
        dz_pad[:, pad1 + nb * bw :] = jnp.zeros((pair, pad1), bf16)
        off_pad[:, 0:pad1] = jnp.full((8, pad1), -1.0, f32)
        off_pad[:, pad1 + nb * bw :] = jnp.full((8, pad1), -1.0, f32)
        total = got[0]
        for src in range(1, nb):
            total = total + got[src]
        ends[...] = total
        mine = valid_row(k, bw, length)
        for h in range(half):
            growth = jnp.exp(ends[pl.ds(h * nb + k, 1), :])
            coupled[0, h : h + 1, :] = (
                growth * flux[half + h : half + h + 1] + ends[24 + h : 25 + h, :]
            ) * mine

        def first(c, carry):
            base = pl.multiple_of(c * bw, bw)
            at = pl.multiple_of(pad1 + base, 128)
            block = fields[c ^ k].astype(f32)
            valid = valid_row(c, bw, length)
            off_pad[0:1, pl.ds(at, bw)] = block[6 * half : 6 * half + 1]
            flux2 = block[half : 2 * half] + block[3 * half : 4 * half]
            cot = (block[4 * half : 5 * half] + block[5 * half : 6 * half]) * valid
            for h in range(half):
                growth = jnp.exp(ends[pl.ds(h * nb + c, 1), :])
                d_cat[h : h + 1, :] = cot[h : h + 1] * growth * flux2[h : h + 1]
            d_cat[half : 2 * half, :] = cot
            full = d_cat[0:8, :]
            hi = full.astype(bf16).astype(f32)
            lo = full - hi
            d_cat[8:16, :] = lo
            d_cat[16:24, :] = hi
            d_gated = dot(e_up[...], d_cat[...].astype(bf16))
            acc_g[...] += nt(d_cat[8:24, :].astype(bf16), gown[:, pl.ds(base, bw)])
            d_e0[:, pl.ds(base, bw)] = d_gated[:rows]
            up = d_gated[rows : 2 * rows]
            dz_pad[0:rows, pl.ds(at, bw)] = (up * du1[:, pl.ds(base, bw)]).astype(bf16)
            dz_pad[rows:, pl.ds(at, bw)] = (up * dv1[:, pl.ds(base, bw)]).astype(bf16)
            return carry

        lax.fori_loop(0, nb, first, 0, unroll=4)

        apart = steps_apart((128, 256))

        def second(c, carry):
            base = pl.multiple_of(c * bw, bw)
            valid = valid_row(c, bw, length)
            for tile in range(bw // 128):
                lane = pl.ds(pl.multiple_of(base + tile * 128, 128), 128)
                late = pl.ds(pl.multiple_of(pad1 + dil1 + base + tile * 128, 128), 256)
                early = pl.ds(pl.multiple_of(base + tile * 128, 128), 256)
                left = nt(dz_pad[:, late], one_hot(apart, -off_pad[0:1, late]))
                right = nt(dz_pad[:, early], one_hot(apart, off_pad[0:1, early] - 128.0))
                d_taps[0:pair, lane] = left.astype(bf16)
                d_taps[2 * pair :, lane] = (
                    right * valid[:, tile * 128 : (tile + 1) * 128]
                ).astype(bf16)
            centre = dz_pad[:, pl.ds(pl.multiple_of(pad1 + base, 128), bw)]
            d_taps[pair : 2 * pair, pl.ds(base, bw)] = centre
            acc_b[...] += nt(jnp.ones((16, bw), bf16), centre)
            return carry

        lax.fori_loop(0, nb, second, 0, unroll=4)

    mw = g0.shape[1]
    base = pl.multiple_of(i * mw, mw)
    d_blk = d_taps[:, pl.ds(base, mw)]
    s_b = s_in[...]
    acc_q[...] += nt(d_blk, g0[...])
    acc_s[...] += nt(s_b, d_blk)
    dg[...] = dot(w_mix_t[...], d_blk)
    own = pl.ds(pl.multiple_of(rows * k, rows), rows)
    dg[own, :] = dg[own, :] + d_e0[:, pl.ds(base, mw)]
    up = dg[...]
    acc_m[:, 0:channels] += nt(s_b, (up * du0[...].astype(f32)).astype(bf16))
    acc_m[:, channels:] += nt(s_b, (up * dv0[...].astype(f32)).astype(bf16))

    @pl.when(i == pl.num_programs(0) - 1)
    def _():
        per_mix = channels // n_dp
        eighth = pair // n_dp
        q = acc_q[...]
        q_hi = q.astype(bf16)
        small[0:half, :] = acc_s[3 : 3 + half, :] + acc_s[12 : 12 + half, :]
        seen = small[0:8, :]
        seen_hi = seen.astype(bf16).astype(f32)
        small[8:16, :] = seen - seen_hi
        small[16:24, :] = seen
        d_start = small[...].astype(bf16)
        acc_conv[...] = nt(q_hi, mix[...]) + dot(d_start, w_start[...], 0, 0)
        acc_mix[...] = dot(w_taps_t[...], q_hi)
        starts = dot(d_start, w_taps[...])
        starts = starts[0:half] + starts[8 : 8 + half]
        m_rows[0:9, :] = acc_m[0:9, :] + acc_m[9:18, :]
        m_rows[9:10, :] = acc_m[27:28, :]
        bias = acc_b[0:1, :]
        share[0:1, 0:128] = bias
        share[6:7, 128:256] = bias - bias.astype(bf16).astype(f32)
        share[0 : 2 * half, 128:256] = acc_g[8 : 8 + 2 * half, :] + acc_g[0 : 2 * half, :]
        for j in range(n_dp):
            row = 64 * (j % (n_dp // 2)) + per_mix * (j // (n_dp // 2))
            packet[j, 0:per_mix, :] = acc_mix[row : row + per_mix, :].astype(bf16)
            for tap in range(3):
                at = per_mix + tap * eighth
                row = tap * pair + j * eighth
                packet[j, at : at + eighth, :] = acc_conv[row : row + eighth, :].astype(bf16)
            if j < channels // 128:
                share[1 : 1 + half, 0:128] = starts[:, 128 * j : 128 * (j + 1)]
            else:
                share[1 : 1 + half, 0:128] = jnp.zeros((half, 128), f32)
            at = per_mix + 3 * eighth
            cols = slice(128 * (j // 2), 128 * (j // 2) + 128)
            share[6:8, 0:128] = m_rows[8:10, cols]
            low = m_rows[0:10, cols]
            low = low - low.astype(bf16).astype(f32)
            share[4:6, 0:128] = low[8:10]
            packet[j, at : at + 8, 0:128] = m_rows[0:8, cols].astype(bf16)
            packet[j, at : at + 8, 128:256] = share[:, 0:128].astype(bf16)
            packet[j, at : at + 8, 256:384] = share[:, 128:256].astype(bf16)
            packet[j, at : at + 8, 384:512] = low[0:8].astype(bf16)


def whole(shape):
    return pl.BlockSpec(shape, lambda i: (0,) * len(shape))


def columns(rows, width):
    return pl.BlockSpec((rows, width), lambda i: (0, i))


def local(
    light_flux,
    lengths,
    offsets,
    start_weight,
    conv_weight,
    gate_bias,
    mix_first,
    mix_last,
    end_weight,
    cotangent,
):
    n_dp = lax.axis_size("dp")
    n_ctx = lax.axis_size("ctx")
    half_dp = n_dp // 2
    dp = lax.axis_index("dp")
    k = lax.axis_index("ctx")
    low = dp < half_dp
    shard_len = light_flux.shape[2]
    half = light_flux.shape[1] // 2
    channels = start_weight.shape[0]
    epochs = shard_len * n_ctx
    dilations = (shard_len // 4, shard_len + shard_len // 2)
    rows = conv_weight.shape[1]
    last_rows = mix_last.shape[0]
    conv0, conv1 = conv_weight[0], conv_weight[1]
    part = rows // n_ctx
    n_e = 2 * half

    def strided(x):
        lead = x.shape[0]
        cols = x.shape[1]
        view = x.reshape(lead, cols // rows, n_ctx, part)
        return lax.dynamic_slice(
            view, (0, 0, k, 0), (lead, cols // rows, 1, part)
        ).reshape(lead, cols // n_ctx)

    half_rows = rows // 2
    mix_far = lax.ppermute(
        mix_first[half_rows:], "dp", [(i, i + half_dp) for i in range(half_dp)]
    )
    sw_hi, sw_lo = split(start_weight)
    ew_last = lax.dynamic_slice(end_weight, (0, last_rows * dp), (n_e, last_rows))
    ew_skip = lax.dynamic_slice(
        end_weight, (0, rows * jnp.maximum(dp - half_dp, 0)), (n_e, rows)
    )
    ew_skip = jnp.where(low, 0.0, ew_skip)
    mix_last_k = strided(mix_last).astype(f32)
    mix_skip_k = lax.dynamic_slice(mix_first, (0, rows * k), (rows, rows)).astype(f32)
    per = 3 * part + 8 + half_rows
    smem = pl.BlockSpec(memory_space=pltpu.SMEM)
    packets = pl.pallas_call(
        packet_kernel,
        in_specs=[smem] + [pl.BlockSpec(memory_space=pltpu.VMEM)] * 6,
        out_specs=pl.BlockSpec(memory_space=pltpu.VMEM),
        out_shape=jax.ShapeDtypeStruct((n_dp, per, channels), bf16),
        scratch_shapes=[
            pltpu.VMEM((16, channels), f32),
            pltpu.VMEM((128, channels), bf16),
            pltpu.VMEM((8, channels), f32),
            pltpu.VMEM((16, 128), f32),
        ],
        name="weight_packets",
    )(jnp.stack([dp, k]), conv_weight, mix_first, mix_far, mix_last, start_weight.T, end_weight)
    got = exchange(packets.reshape(n_dp * per, channels), "dp").reshape(n_dp, per, channels)
    flux_hi, flux_lo = split(light_flux[0])
    cot_hi, cot_lo = split(cotangent[0])
    n_in = 6 * half + 1
    inputs = jnp.concatenate(
        [flux_hi, flux_lo, cot_hi, cot_lo, offsets.astype(bf16)], axis=0
    )
    n_pad = -(-n_in // 8) * 8
    inputs = pad_to(inputs, n_pad, shard_len)

    fields = inputs[None]
    while fields.shape[0] < n_ctx:
        hop = fields.shape[0]
        other = lax.ppermute(fields, "ctx", [(c, c ^ hop) for c in range(n_ctx)])
        fields = jnp.concatenate([fields, other], axis=0)
    weights = got
    e_k = got[:, 3 * part : 3 * part + n_e, : 4 * rows].astype(f32).sum(axis=0)
    e_cat = e_k[:, : 2 * rows] + e_k[:, 2 * rows :]
    a_got = got[:, 3 * part : 4 * part, 4 * rows :]
    a_all = jnp.concatenate(
        [
            a_got[:, :, :rows],
            a_got[:, 0:1, 2 * rows : 3 * rows],
            a_got[:, :, rows : 2 * rows],
            a_got[:, 1:2, 2 * rows : 3 * rows],
        ],
        axis=1,
    )
    a_all = a_all.transpose(1, 0, 2).reshape(18, n_dp * rows)
    a_hi, a_lo = a_all[:9], a_all[9:]

    gap = jnp.zeros((8 - half, channels), bf16)
    w_start = jnp.concatenate(
        [sw_hi.T, gap, sw_hi.T, gap, sw_lo.T, gap, jnp.zeros((8, channels), bf16)], axis=0
    )
    fields, w_start = lax.optimization_barrier((fields, w_start))

    length = lengths[0]
    b_hi, b_lo = split(gate_bias[0][None])
    a_cat = jnp.concatenate(
        [a_hi, a_hi, a_lo, b_hi, b_lo, jnp.zeros((3, 2 * channels), bf16)], axis=0
    ).T
    w_hi, w_lo = (
        jnp.concatenate([jnp.pad(x, ((0, 0), (3, 6 - half)))] * 3 + [jnp.zeros((channels, 5), bf16)], axis=1)
        for x in (sw_hi, sw_lo)
    )
    ec_hi, ec_lo = split(e_cat)
    gap = jnp.zeros((2, 2 * rows), bf16)
    e_pair = jnp.concatenate([ec_hi, gap, ec_lo, gap], axis=0)
    e_up = pad_to(jnp.concatenate([ec_hi, gap, ec_hi, gap, ec_lo], axis=0), 32, 2 * rows).T
    bias1 = strided(gate_bias[1][None]).T
    info = jnp.stack([length, k])
    pair = 2 * rows
    main = 2 * shard_len
    wide = epochs + 2 * (dilations[1] + 128)
    smem = pl.BlockSpec(memory_space=pltpu.SMEM)
    shapes = jax.ShapeDtypeStruct
    params = pltpu.CompilerParams(
        dimension_semantics=("arbitrary",), vmem_limit_bytes=60000 * 1024
    )
    forward = pl.pallas_call(
        functools.partial(forward_kernel, dilations[0], dilations[1], half),
        grid=(epochs // main,),
        in_specs=[
            smem,
            whole((n_ctx, n_pad, shard_len)),
            whole(a_cat.shape),
            whole(w_hi.shape),
            whole(w_lo.shape),
            whole(weights.shape),
            whole(bias1.shape),
            whole(e_pair.shape),
        ],
        out_specs=[columns(channels, main)] * 3
        + [columns(32, main), whole((pair, epochs)), whole((rows, epochs)),
           whole((rows, epochs)), whole((n_ctx, 32, shard_len)),
           whole((channels, channels)), whole((3 * pair, channels))],
        out_shape=[shapes((channels, epochs), bf16)] * 3
        + [shapes((32, epochs), bf16), shapes((pair, epochs), bf16), shapes((rows, epochs), f32),
           shapes((rows, epochs), f32), shapes((n_ctx, 32, shard_len), f32),
           shapes((channels, channels), bf16), shapes((3 * pair, channels), bf16)],
        scratch_shapes=[
            pltpu.VMEM((8, epochs + 512), f32),
            pltpu.VMEM((32, main), f32),
            pltpu.VMEM((2 * pair, wide), bf16),
            pltpu.VMEM((pair, epochs), f32),
            pltpu.VMEM((pair, shard_len), f32),
            pltpu.VMEM((rows, epochs), bf16),
            pltpu.VMEM((3 * pair, channels), bf16),
            pltpu.VMEM((3 * pair, 32), bf16),
        ],
        compiler_params=params,
        name="layers_forward",
    )
    g0, du0, dv0, s_all, g_own, du1, dv1, packed, mix_res, w_taps = forward(
        info, fields, a_cat, w_hi, w_lo, weights, bias1, e_pair
    )
    got = exchange(packed.reshape(n_ctx * 32, shard_len), "ctx").reshape(n_ctx, 32, shard_len)

    n_mix = channels // n_dp
    n_conv = 3 * pair // n_dp
    per = n_mix + n_conv + 8
    backward = pl.pallas_call(
        functools.partial(backward_kernel, dilations[1], half),
        grid=(n_ctx,),
        in_specs=[
            smem,
            whole((n_ctx, 32, shard_len)),
            whole((n_ctx, n_pad, shard_len)),
            whole((2 * half, shard_len)),
            whole((pair, 32)),
            whole((pair, epochs)),
            whole((rows, epochs)),
            whole((rows, epochs)),
            whole((3 * pair, channels)),
            whole((channels, 3 * pair)),
            whole((channels, channels)),
            whole((channels, 3 * pair)),
            whole((32, channels)),
        ]
        + [columns(channels, shard_len)] * 3
        + [columns(32, shard_len)],
        out_specs=[whole((1, half, shard_len)), whole((n_dp, per, channels))],
        out_shape=[shapes((1, half, shard_len), f32), shapes((n_dp, per, channels), bf16)],
        scratch_shapes=[
            pltpu.VMEM((32, shard_len), f32),
            pltpu.VMEM((32, shard_len), f32),
            pltpu.VMEM((pair, wide), bf16),
            pltpu.VMEM((8, wide), f32),
            pltpu.VMEM((rows, epochs), f32),
            pltpu.VMEM((3 * pair, epochs), bf16),
            pltpu.VMEM((3 * pair, channels), f32),
            pltpu.VMEM((channels, channels), f32),
            pltpu.VMEM((32, 2 * channels), f32),
            pltpu.VMEM((32, 3 * pair), f32),
            pltpu.VMEM((16, pair), f32),
            pltpu.VMEM((16, pair), f32),
            pltpu.VMEM((channels, shard_len), f32),
            pltpu.VMEM((16, 2 * channels), f32),
            pltpu.VMEM((8, 256), f32),
            pltpu.VMEM((3 * pair, channels), f32),
            pltpu.VMEM((32, 3 * pair), f32),
        ],
        compiler_params=params,
        name="layers_backward",
    )
    coupled, packed = backward(
        info, got, fields, light_flux[0], e_up, g_own, du1, dv1, w_taps, w_taps.T, mix_res,
        dot(mix_res, w_taps, 0, 1).astype(bf16), w_start, g0, du0, dv0, s_all,
    )
    got = exchange(packed.reshape(n_dp * per, channels), "dp").reshape(n_dp, per, channels)
    got = got.astype(f32).sum(axis=0)
    mix_piece = got[:n_mix]
    conv_piece = got[n_mix : n_mix + n_conv].astype(bf16)
    smalls = got[n_mix + n_conv :]
    m_first = smalls[:, :128] + smalls[:, 384:]
    m_rest = smalls[4:6, 128:256] + smalls[6:8, 128:256]
    m_own = lax.dynamic_slice(
        jnp.concatenate([m_first, m_rest], axis=0), (0, rows * (dp % 2)), (10, rows)
    )
    start_own = jnp.where(dp < channels // 128, smalls[1 : 1 + half, 128:256], 0.0)
    g_own_sum = smalls[: 2 * half, 256:384]
    bias1_own = smalls[0:1, 128:256] + smalls[6:7, 256:384]
    mo_hi, mo_lo = split(m_own)
    mo_pair = jnp.concatenate([mo_hi[:9], mo_lo[:9]], axis=0)
    start_t = 0.0
    for tap in range(3):
        up = dot(mo_pair, conv0[:, tap * channels : (tap + 1) * channels])
        start_t = start_t + up[half * tap : half * tap + half] + up[9 + half * tap : 9 + half * tap + half]
    spot = lax.dynamic_update_slice(
        jnp.zeros((half, channels), f32), start_own, (0, 128 * (dp % (channels // 128)))
    )
    start_t = start_t + spot
    end_last = dot(g_own_sum[:, rows:], mix_last_k, 1, 1, highest)
    end_skip = jnp.where(low, 0.0, dot(g_own_sum[:, :rows], mix_skip_k, 1, 1, highest))
    g_rows = jnp.concatenate([g_own_sum, bias1_own], axis=0)
    parts = jnp.concatenate(
        [
            m_own,
            pad_to(g_rows, 10, 2 * rows),
            pad_to(jnp.concatenate([end_last, end_skip], axis=1), 10, last_rows + rows),
        ],
        axis=1,
    )
    width = parts.shape[1]
    parts_hi, parts_lo = split(parts)
    start_hi, start_lo = split(start_t)
    pack_rows = [
        conv_piece,
        mix_piece.astype(bf16),
        pad_to(jnp.concatenate([parts_hi, parts_lo[:, : 3 * rows]], axis=1), 10, channels),
        start_hi,
        start_lo,
    ]
    packed = jnp.concatenate(pack_rows, axis=0)
    per0 = packed.shape[0]
    per = -(-per0 // 8) * 8
    packed = pad_to(packed, per, channels)
    got = exchange(
        jnp.broadcast_to(packed[None], (n_ctx, per, channels)).reshape(n_ctx * per, channels), "ctx"
    ).reshape(n_ctx, per, channels)
    grad_conv1 = got[:, :n_conv].reshape(n_ctx, 3, part, channels).transpose(0, 2, 1, 3)
    grad_conv1 = grad_conv1.reshape(rows, 3 * channels).astype(f32)
    mix_rows = got[:, n_conv : n_conv + n_mix].astype(f32).sum(axis=0)
    base = n_conv + n_mix
    parts = got[:, base : base + 10].astype(f32)
    parts_lo = parts[:, :, width : width + 3 * rows]
    parts = jnp.concatenate(
        [parts[:, :, : 3 * rows] + parts_lo, parts[:, :, 3 * rows : width]], axis=2
    )
    start_t = got[:, base + 10 : base + 10 + 2 * half].astype(f32).sum(axis=0)
    start_t = start_t[:half] + start_t[half:]
    m_own = parts[:, :, :rows].sum(axis=0)
    g_all = parts[:, : 2 * half, rows : 3 * rows]
    g0_all = g_all[:, :, :rows].transpose(1, 0, 2).reshape(2 * half, channels)
    g1_all = g_all[:, :, rows:].reshape(n_ctx, 2 * half, half_dp, part).transpose(1, 2, 0, 3)
    g1_all = g1_all.reshape(2 * half, channels)
    bias1_all = parts[:, 2 * half, rows : 3 * rows].reshape(n_ctx, n_dp, part).transpose(1, 0, 2)
    bias1_all = bias1_all.reshape(2 * channels)
    end_both = parts[:, : 2 * half, 3 * rows :].sum(axis=0)
    a_grad = m_own[:9].T
    grad_conv0 = jnp.concatenate(
        [
            dot(a_grad[:, half * tap : half * tap + half], start_weight, 1, 1, highest)
            for tap in range(3)
        ],
        axis=1,
    )
    grad_mix_last = dot(ew_last, g1_all, 0, 0, highest)
    skip_rows = dot(ew_skip, g0_all, 0, 0, highest)

    other = lax.ppermute(mix_rows, "dp", [(i + half_dp, i) for i in range(half_dp)])
    final = jnp.concatenate(
        [
            start_t.reshape(-1, 128),
            pad_to(end_both, 2 * half, 128),
            pad_to(m_own[9:10], 1, 128),
        ],
        axis=0,
    )
    per0 = final.shape[0]
    per = -(-per0 // 8) * 8
    final = pad_to(final, per, 128)
    got = exchange(
        jnp.broadcast_to(final[None], (n_dp, per, 128)).reshape(n_dp * per, 128), "dp"
    ).reshape(n_dp, per, 128)
    n_start = half * channels // 128
    grad_start = got[:, :n_start].sum(axis=0).reshape(half, channels).T
    ends = got[:, n_start : n_start + 2 * half]
    grad_end = ends[:, :, :last_rows].transpose(1, 0, 2).reshape(2 * half, channels)
    grad_end = grad_end + ends[half_dp:, :, last_rows : last_rows + rows].transpose(
        1, 0, 2
    ).reshape(2 * half, channels)
    bias0_all = got[:, n_start + 2 * half, :rows].reshape(2 * channels)
    grad_bias = jnp.stack([bias0_all, bias1_all])
    residual = jnp.concatenate([mix_rows, other], axis=0)
    grad_mix_first = jnp.where(low, residual, skip_rows)
    grad_conv = jnp.stack([grad_conv0, grad_conv1])
    return (coupled, grad_start, grad_conv, grad_bias, grad_mix_first, grad_mix_last, grad_end)


def solution(mesh):
    in_specs = (
        P("dp", None, "ctx"),
        P("dp"),
        P("dp", "ctx"),
        P(),
        P(None, "dp", None),
        P(),
        P("dp", None),
        P("dp", None),
        P(),
        P("dp", None, "ctx"),
    )
    out_specs = (
        P("dp", None, "ctx"),
        P(),
        P(None, "dp", None),
        P(),
        P("dp", None),
        P("dp", None),
        P(),
    )
    return jax.shard_map(local, mesh=mesh, in_specs=in_specs, out_specs=out_specs, check_vma=False)
```

```python
import functools

import jax
import jax.numpy as jnp
from jax import lax
from jax.experimental import pallas as pl
from jax.experimental.pallas import tpu as pltpu
from jax.sharding import PartitionSpec as P

BUCKETS = 4
highest = lax.Precision.HIGHEST
bf16 = jnp.bfloat16
f32 = jnp.float32


def dot(a, b, ca=1, cb=0, precision=None):
    return lax.dot_general(
        a, b, (((ca,), (cb,)), ((), ())), precision=precision, preferred_element_type=f32
    )


def split(x):
    hi = lax.reduce_precision(x, 8, 7)
    return hi.astype(bf16), (x - hi).astype(bf16)


def pad_to(x, rows, cols):
    return jnp.pad(x, ((0, rows - x.shape[0]), (0, cols - x.shape[1])))


def shift(x, n):
    total = x.shape[1]
    if n > 0:
        return jnp.pad(x[:, : total - n], ((0, 0), (n, 0)))
    return jnp.pad(x[:, -n:], ((0, 0), (0, -n)))


def tap_of(x, off, dilation, side):
    out = shift(x, side * dilation)
    for step in range(1, BUCKETS):
        out = jnp.where(off == step, shift(x, side * (dilation + step)), out)
    return out


def tap_back(x, off, dilation, side):
    out = 0.0
    for step in range(BUCKETS):
        out = out + shift(jnp.where(off == step, x, 0.0), -side * (dilation + step))
    return out


def exchange(x, axis):
    return lax.all_to_all(x, axis, 0, 0, tiled=True)


def nt(a, b):
    return dot(a, b, 1, 1)


def rolled(x, start, width):
    if start % 128 == 0:
        return x[:, start : start + width]
    return pltpu.roll(x, x.shape[1] - start, 1)[:, :width]


def steps_apart(shape):
    return (
        lax.broadcasted_iota(jnp.int32, shape, 0) - lax.broadcasted_iota(jnp.int32, shape, 1)
    ).astype(f32)


def one_hot(apart, target):
    return jnp.where(apart == target, 1.0, 0.0).astype(bf16)


def valid_row(c, width, length):
    at = lax.broadcasted_iota(jnp.int32, (1, width), 1) + c * width
    return (at < length).astype(f32)


def packet_kernel(
    info, conv, mix_first, mix_far, mix_last, start, ends,
    packet,
    sw, low_rows, ew, turn,
):
    dp = info[0]
    k = info[1]
    n_dp, per, channels = packet.shape
    half = start.shape[0]
    rows = mix_first.shape[0]
    last_rows = mix_last.shape[0]
    n_e = ends.shape[0]
    part = (per - 8 - rows // 2) // 3
    upper = dp >= n_dp // 2

    group = conv[1, pl.ds(pl.multiple_of((k // 2) * 2 * part, 2 * part), 2 * part), :].astype(f32)
    mine = jnp.where(k % 2 == 1, group[part:], group[:part]).astype(bf16)

    sw[...] = jnp.zeros(sw.shape, f32)
    sw[0:half, :] = start[...]
    full = sw[...]
    sw_hi = full.astype(bf16)
    sw_lo = (full - sw_hi.astype(f32)).astype(bf16)
    turn[...] = jnp.zeros(turn.shape, f32)
    for tap in range(3):
        block = conv[0, :, tap * channels : (tap + 1) * channels]
        one = nt(sw_hi, block) + nt(sw_lo, block)
        turn[half * tap : half * (tap + 1), 0:rows] = one[0:half]
    a_t = turn[...]
    a_hi = a_t[0:16].astype(bf16).astype(f32)
    a_lo = a_t[0:16] - a_hi
    lane = lax.broadcasted_iota(jnp.int32, (8, 128), 1)
    row = lax.broadcasted_iota(jnp.int32, (8, 128), 0)
    near = jnp.where(lane < rows, a_hi[0:8], pltpu.roll(a_lo[0:8], rows, 1))
    far = jnp.where(row == 0, a_hi[8:16], pltpu.roll(a_lo[8:16], 1, 0))

    ew[...] = jnp.zeros(ew.shape, f32)
    ew[0:n_e, :] = ends[...]
    e_all = ew[...]
    wide = lax.broadcasted_iota(jnp.int32, (8, 128), 1)

    def product(shift, count, source, keep):
        moved = pltpu.roll(e_all, lax.rem(channels - shift, channels), 1)[:, 0:128]
        moved = jnp.where(jnp.logical_and(wide < count, keep), moved, 0.0)
        hi = moved.astype(bf16)
        low = (moved - hi.astype(f32)).astype(bf16)
        low_rows[...] = jnp.zeros(low_rows.shape, bf16)
        low_rows[0:count, :] = source[...]
        out = dot(hi, low_rows[...]) + dot(low, low_rows[...])
        out_hi = out.astype(bf16)
        return out_hi, (out - out_hi.astype(f32)).astype(bf16)

    at = lax.broadcasted_iota(jnp.int32, (channels, 128), 0)
    col = lax.broadcasted_iota(jnp.int32, (channels, 128), 1)
    m = col - rows
    pick0 = jnp.where(jnp.logical_and(col < rows, at == rows * k + col), 1.0, 0.0).astype(bf16)
    target = (m >> 3) * rows + part * k + (m & 7)
    pick1 = jnp.where(jnp.logical_and(m >= 0, at == target), 1.0, 0.0).astype(bf16)
    e0_hi, e0_lo = product(
        rows * jnp.maximum(dp - n_dp // 2, 0), rows, mix_first, upper
    )
    e1_hi, e1_lo = product(last_rows * dp, last_rows, mix_last, dp >= 0)
    e_hi = dot(e0_hi, pick0) + dot(e1_hi, pick1)
    e_lo = dot(e0_lo, pick0) + dot(e1_lo, pick1)

    send = jnp.where(
        upper, mix_far[rows // 2 :, :].astype(f32), mix_first[0 : rows // 2, :].astype(f32)
    )
    send = send.astype(bf16)
    base = 3 * part
    for j in range(n_dp):
        for tap in range(3):
            packet[j, tap * part : (tap + 1) * part, :] = mine[
                :, tap * channels : (tap + 1) * channels
            ]
        packet[j, base : base + 8, 0:128] = e_hi.astype(bf16)
        packet[j, base : base + 8, 128:256] = e_lo.astype(bf16)
        packet[j, base : base + 8, 256:384] = near.astype(bf16)
        packet[j, base : base + 8, 384:512] = far.astype(bf16)
        packet[j, base + 8 :, :] = send


def forward_kernel(
    dil0, dil1, half,
    info, fields, a_cat, w_hi, w_lo, weights, bias1, e_pair,
    g0_out, du0_out, dv0_out, s_out, gown_out, du1_out, dv1_out, packet, mix, w_taps,
    fpad, s_cat, prod, centre, pre_s, g_keep, w_mix, w_start,
):
    i = pl.program_id(0)
    nb = fields.shape[0]
    bw = fields.shape[2]
    rows = gown_out.shape[0] // 2
    channels = mix.shape[0]
    pad0 = 256
    pad1 = dil1 + 128
    length = info[0]
    k = info[1]

    @pl.when(i == 0)
    def _():
        fpad[:, 0:pad0] = jnp.zeros((8, pad0), f32)
        fpad[:, pad0 + nb * bw :] = jnp.zeros((8, pad0), f32)
        prod[:, 0:pad1] = jnp.zeros((prod.shape[0], pad1), bf16)
        prod[:, pad1 + nb * bw :] = jnp.zeros((prod.shape[0], pad1), bf16)
        n_dp = weights.shape[0]
        part = 2 * rows // n_dp
        half_rows = rows // 2
        for j in range(n_dp):
            for tap in range(3):
                to = tap * 2 * rows + j * part
                w_taps[to : to + part, :] = weights[j, tap * part : (tap + 1) * part, :]
            to = rows * (j % (n_dp // 2)) + half_rows * (j // (n_dp // 2))
            mix[to : to + half_rows, :] = weights[j, 4 * part :, :]
        w_mix[...] = dot(w_taps[...], mix[...]).astype(bf16)
        full = dot(w_taps[...], w_hi[...]) + dot(w_taps[...], w_lo[...])
        top = full.astype(bf16).astype(f32)
        col = lax.broadcasted_iota(jnp.int32, full.shape, 1)
        w_start[...] = jnp.where(col < 18, top, full - top).astype(bf16)
        s_cat[...] = jnp.zeros(s_cat.shape, f32)
        s_cat[27:29, :] = jnp.ones((2, g0_out.shape[1]), f32)
        packet[:, 24:32, :] = jnp.zeros((nb, 8, bw), f32)
        for c in range(nb):
            block = fields[c ^ k].astype(f32)
            valid = valid_row(c, bw, length)
            at = slice(pad0 + c * bw, pad0 + (c + 1) * bw)
            fpad[0:half, at] = block[0:half] * valid
            fpad[half : 2 * half, at] = block[2 * half : 3 * half] * valid
            fpad[6:7, at] = block[6 * half : 6 * half + 1]
            fpad[7:8, at] = valid

    mw = g0_out.shape[1]
    base = pl.multiple_of(i * mw, mw)
    near = fpad[:, pl.ds(pl.multiple_of(pad0 + base, 128), mw)]
    off = near[6:7]
    valid = near[7:8]
    behind = fpad[:, pl.ds(pl.multiple_of(base, 128), mw + 2 * dil0)]
    ahead = fpad[:, pl.ds(pl.multiple_of(pad0 + base, 128), mw + 2 * dil0)]
    left = rolled(behind, dil0, mw)
    right = rolled(ahead, dil0, mw)
    for step in range(1, BUCKETS):
        left = jnp.where(off == step, rolled(behind, dil0 - step, mw), left)
        right = jnp.where(off == step, rolled(ahead, dil0 + step, mw), right)
    for part, at in ((left, 0), (near, 3), (right, 6)):
        s_cat[at : at + half, :] = part[0:half]
        s_cat[9 + at : 9 + at + half, :] = part[half : 2 * half]
        s_cat[18 + at : 18 + at + half, :] = part[0:half]
    s_b = s_cat[...].astype(bf16)
    s_out[...] = s_b
    step_rows = 128
    for r in range(0, channels, step_rows):
        u = dot(a_cat[r : r + step_rows, :], s_b)
        v = dot(a_cat[channels + r : channels + r + step_rows, :], s_b)
        t = jnp.tanh(u)
        s = 0.5 * jnp.tanh(0.5 * v) + 0.5
        g = t * s
        g0_out[r : r + step_rows, :] = (g * valid).astype(bf16)
        du0_out[r : r + step_rows, :] = (s - g * t).astype(bf16)
        dv0_out[r : r + step_rows, :] = (g - g * s).astype(bf16)
    pair = 2 * rows
    g_b = g0_out[...]
    for tap in range(3):
        at = slice(tap * pair, (tap + 1) * pair)
        part = dot(w_mix[at, :], g_b) + dot(w_start[at, :], s_b)
        if tap == 1:
            centre[:, pl.ds(base, mw)] = part
        else:
            to = tap // 2 * pair
            cols = pl.ds(pl.multiple_of(pad1 + base, 128), mw)
            prod[to : to + pair, cols] = part.astype(bf16)
    g_keep[:, pl.ds(base, mw)] = g0_out[pl.ds(pl.multiple_of(rows * k, rows), rows), :]

    @pl.when(i == pl.num_programs(0) - 1)
    def _():
        apart = steps_apart((256, 128))

        def body(c, carry):
            base = pl.multiple_of(c * bw, bw)
            off = fpad[6:7, pl.ds(pl.multiple_of(pad0 + base, 128), bw)]
            for tile in range(bw // 128):
                lane = slice(tile * 128, (tile + 1) * 128)
                behind = prod[0:pair, pl.ds(pl.multiple_of(base + tile * 128, 128), 256)]
                ahead = prod[
                    pair:,
                    pl.ds(pl.multiple_of(pad1 + dil1 + base + tile * 128, 128), 256),
                ]
                pre_s[:, lane] = dot(behind, one_hot(apart, 128.0 - off[:, lane])) + dot(
                    ahead, one_hot(apart, off[:, lane])
                )
            pre = pre_s[...] + centre[:, pl.ds(base, bw)] + bias1[...]
            t = jnp.tanh(pre[:rows])
            s = 0.5 * jnp.tanh(0.5 * pre[rows:]) + 0.5
            g = t * s
            du1_out[:, pl.ds(base, bw)] = s - g * t
            dv1_out[:, pl.ds(base, bw)] = g - g * s
            gown_out[0:rows, pl.ds(base, bw)] = g_keep[:, pl.ds(base, bw)]
            gown_out[rows:, pl.ds(base, bw)] = g.astype(bf16)
            part = dot(e_pair[...], gown_out[:, pl.ds(base, bw)])
            part = part[0 : 2 * half] + part[8 : 8 + 2 * half]
            for d in range(nb):
                for h in range(half):
                    packet[d, pl.ds(h * nb + c, 1), :] = part[h : h + 1]
            packet[c, 24 : 24 + half, :] = part[half : 2 * half]
            return carry

        lax.fori_loop(0, nb, body, 0, unroll=2)


def backward_kernel(
    dil1, half,
    info, got, fields, flux, e_up, gown, du1, dv1, w_taps, w_taps_t, mix, w_mix_t, w_start,
    g0, du0, dv0, s_in,
    coupled, packet,
    ends, d_cat, dz_pad, off_pad, d_e0, d_taps, acc_q, acc_mix, acc_m, acc_s, acc_g, acc_b,
    dg, m_rows, share, acc_conv, small,
):
    i = pl.program_id(0)
    nb = fields.shape[0]
    bw = fields.shape[2]
    pair = gown.shape[0]
    rows = pair // 2
    channels = mix.shape[0]
    n_dp = packet.shape[0]
    pad1 = dil1 + 128
    length = info[0]
    k = info[1]

    @pl.when(i == 0)
    def _():
        for ref in (acc_q, acc_m, acc_s, acc_g, acc_b, d_cat, m_rows, share, small):
            ref[...] = jnp.zeros(ref.shape, f32)
        dz_pad[:, 0:pad1] = jnp.zeros((pair, pad1), bf16)
        dz_pad[:, pad1 + nb * bw :] = jnp.zeros((pair, pad1), bf16)
        off_pad[:, 0:pad1] = jnp.full((8, pad1), -1.0, f32)
        off_pad[:, pad1 + nb * bw :] = jnp.full((8, pad1), -1.0, f32)
        total = got[0]
        for src in range(1, nb):
            total = total + got[src]
        ends[...] = total
        mine = valid_row(k, bw, length)
        for h in range(half):
            growth = jnp.exp(ends[pl.ds(h * nb + k, 1), :])
            coupled[0, h : h + 1, :] = (
                growth * flux[half + h : half + h + 1] + ends[24 + h : 25 + h, :]
            ) * mine

        def first(c, carry):
            base = pl.multiple_of(c * bw, bw)
            at = pl.multiple_of(pad1 + base, 128)
            block = fields[c ^ k].astype(f32)
            valid = valid_row(c, bw, length)
            off_pad[0:1, pl.ds(at, bw)] = block[6 * half : 6 * half + 1]
            flux2 = block[half : 2 * half] + block[3 * half : 4 * half]
            cot = (block[4 * half : 5 * half] + block[5 * half : 6 * half]) * valid
            for h in range(half):
                growth = jnp.exp(ends[pl.ds(h * nb + c, 1), :])
                d_cat[h : h + 1, :] = cot[h : h + 1] * growth * flux2[h : h + 1]
            d_cat[half : 2 * half, :] = cot
            full = d_cat[0:8, :]
            hi = full.astype(bf16).astype(f32)
            lo = full - hi
            d_cat[8:16, :] = lo
            d_cat[16:24, :] = hi
            d_gated = dot(e_up[...], d_cat[...].astype(bf16))
            acc_g[...] += nt(d_cat[8:24, :].astype(bf16), gown[:, pl.ds(base, bw)])
            d_e0[:, pl.ds(base, bw)] = d_gated[:rows]
            up = d_gated[rows : 2 * rows]
            dz_pad[0:rows, pl.ds(at, bw)] = (up * du1[:, pl.ds(base, bw)]).astype(bf16)
            dz_pad[rows:, pl.ds(at, bw)] = (up * dv1[:, pl.ds(base, bw)]).astype(bf16)
            return carry

        lax.fori_loop(0, nb, first, 0, unroll=2)

        apart = steps_apart((128, 256))

        def second(c, carry):
            base = pl.multiple_of(c * bw, bw)
            valid = valid_row(c, bw, length)
            for tile in range(bw // 128):
                lane = pl.ds(pl.multiple_of(base + tile * 128, 128), 128)
                late = pl.ds(pl.multiple_of(pad1 + dil1 + base + tile * 128, 128), 256)
                early = pl.ds(pl.multiple_of(base + tile * 128, 128), 256)
                left = nt(dz_pad[:, late], one_hot(apart, -off_pad[0:1, late]))
                right = nt(dz_pad[:, early], one_hot(apart, off_pad[0:1, early] - 128.0))
                d_taps[0:pair, lane] = left.astype(bf16)
                d_taps[2 * pair :, lane] = (
                    right * valid[:, tile * 128 : (tile + 1) * 128]
                ).astype(bf16)
            centre = dz_pad[:, pl.ds(pl.multiple_of(pad1 + base, 128), bw)]
            d_taps[pair : 2 * pair, pl.ds(base, bw)] = centre
            acc_b[...] += nt(jnp.ones((16, bw), bf16), centre)
            return carry

        lax.fori_loop(0, nb, second, 0, unroll=2)

    mw = g0.shape[1]
    base = pl.multiple_of(i * mw, mw)
    d_blk = d_taps[:, pl.ds(base, mw)]
    s_b = s_in[...]
    acc_q[...] += nt(d_blk, g0[...])
    acc_s[...] += nt(s_b, d_blk)
    dg[...] = dot(w_mix_t[...], d_blk)
    own = pl.ds(pl.multiple_of(rows * k, rows), rows)
    dg[own, :] = dg[own, :] + d_e0[:, pl.ds(base, mw)]
    up = dg[...]
    acc_m[:, 0:channels] += nt(s_b, (up * du0[...].astype(f32)).astype(bf16))
    acc_m[:, channels:] += nt(s_b, (up * dv0[...].astype(f32)).astype(bf16))

    @pl.when(i == pl.num_programs(0) - 1)
    def _():
        per_mix = channels // n_dp
        eighth = pair // n_dp
        q = acc_q[...]
        q_hi = q.astype(bf16)
        small[0:half, :] = acc_s[3 : 3 + half, :] + acc_s[12 : 12 + half, :]
        seen = small[0:8, :]
        seen_hi = seen.astype(bf16).astype(f32)
        small[8:16, :] = seen - seen_hi
        small[16:24, :] = seen
        d_start = small[...].astype(bf16)
        acc_conv[...] = nt(q_hi, mix[...]) + dot(d_start, w_start[...], 0, 0)
        acc_mix[...] = dot(w_taps_t[...], q_hi)
        starts = dot(d_start, w_taps[...])
        starts = starts[0:half] + starts[8 : 8 + half]
        m_rows[0:9, :] = acc_m[0:9, :] + acc_m[9:18, :]
        m_rows[9:10, :] = acc_m[27:28, :]
        bias = acc_b[0:1, :]
        share[0:1, 0:128] = bias
        share[6:7, 128:256] = bias - bias.astype(bf16).astype(f32)
        share[0 : 2 * half, 128:256] = acc_g[8 : 8 + 2 * half, :] + acc_g[0 : 2 * half, :]
        for j in range(n_dp):
            row = 64 * (j % (n_dp // 2)) + per_mix * (j // (n_dp // 2))
            packet[j, 0:per_mix, :] = acc_mix[row : row + per_mix, :].astype(bf16)
            for tap in range(3):
                at = per_mix + tap * eighth
                row = tap * pair + j * eighth
                packet[j, at : at + eighth, :] = acc_conv[row : row + eighth, :].astype(bf16)
            if j < channels // 128:
                share[1 : 1 + half, 0:128] = starts[:, 128 * j : 128 * (j + 1)]
            else:
                share[1 : 1 + half, 0:128] = jnp.zeros((half, 128), f32)
            at = per_mix + 3 * eighth
            cols = slice(128 * (j // 2), 128 * (j // 2) + 128)
            share[6:8, 0:128] = m_rows[8:10, cols]
            low = m_rows[0:10, cols]
            low = low - low.astype(bf16).astype(f32)
            share[4:6, 0:128] = low[8:10]
            packet[j, at : at + 8, 0:128] = m_rows[0:8, cols].astype(bf16)
            packet[j, at : at + 8, 128:256] = share[:, 0:128].astype(bf16)
            packet[j, at : at + 8, 256:384] = share[:, 128:256].astype(bf16)
            packet[j, at : at + 8, 384:512] = low[0:8].astype(bf16)


def whole(shape):
    return pl.BlockSpec(shape, lambda i: (0,) * len(shape))


def columns(rows, width):
    return pl.BlockSpec((rows, width), lambda i: (0, i))


def local(
    light_flux,
    lengths,
    offsets,
    start_weight,
    conv_weight,
    gate_bias,
    mix_first,
    mix_last,
    end_weight,
    cotangent,
):
    n_dp = lax.axis_size("dp")
    n_ctx = lax.axis_size("ctx")
    half_dp = n_dp // 2
    dp = lax.axis_index("dp")
    k = lax.axis_index("ctx")
    low = dp < half_dp
    shard_len = light_flux.shape[2]
    half = light_flux.shape[1] // 2
    channels = start_weight.shape[0]
    epochs = shard_len * n_ctx
    dilations = (shard_len // 4, shard_len + shard_len // 2)
    rows = conv_weight.shape[1]
    last_rows = mix_last.shape[0]
    conv0, conv1 = conv_weight[0], conv_weight[1]
    part = rows // n_ctx
    n_e = 2 * half

    def strided(x):
        lead = x.shape[0]
        cols = x.shape[1]
        view = x.reshape(lead, cols // rows, n_ctx, part)
        return lax.dynamic_slice(
            view, (0, 0, k, 0), (lead, cols // rows, 1, part)
        ).reshape(lead, cols // n_ctx)

    half_rows = rows // 2
    mix_far = lax.ppermute(
        mix_first, "dp", [(i, i + half_dp) for i in range(half_dp)]
    )
    sw_hi, sw_lo = split(start_weight)
    ew_last = lax.dynamic_slice(end_weight, (0, last_rows * dp), (n_e, last_rows))
    ew_skip = lax.dynamic_slice(
        end_weight, (0, rows * jnp.maximum(dp - half_dp, 0)), (n_e, rows)
    )
    ew_skip = jnp.where(low, 0.0, ew_skip)
    mix_last_k = strided(mix_last).astype(f32)
    mix_skip_k = lax.dynamic_slice(mix_first, (0, rows * k), (rows, rows)).astype(f32)
    per = 3 * part + 8 + half_rows
    smem = pl.BlockSpec(memory_space=pltpu.SMEM)
    packets = pl.pallas_call(
        packet_kernel,
        in_specs=[smem] + [pl.BlockSpec(memory_space=pltpu.VMEM)] * 6,
        out_specs=pl.BlockSpec(memory_space=pltpu.VMEM),
        out_shape=jax.ShapeDtypeStruct((n_dp, per, channels), bf16),
        scratch_shapes=[
            pltpu.VMEM((16, channels), f32),
            pltpu.VMEM((128, channels), bf16),
            pltpu.VMEM((8, channels), f32),
            pltpu.VMEM((16, 128), f32),
        ],
        name="weight_packets",
    )(jnp.stack([dp, k]), conv_weight, mix_first, mix_far, mix_last, start_weight.T, end_weight)
    got = exchange(packets.reshape(n_dp * per, channels), "dp").reshape(n_dp, per, channels)
    flux_hi, flux_lo = split(light_flux[0])
    cot_hi, cot_lo = split(cotangent[0])
    n_in = 6 * half + 1
    inputs = jnp.concatenate(
        [flux_hi, flux_lo, cot_hi, cot_lo, offsets.astype(bf16)], axis=0
    )
    n_pad = -(-n_in // 8) * 8
    inputs = pad_to(inputs, n_pad, shard_len)

    fields = inputs[None]
    while fields.shape[0] < n_ctx:
        hop = fields.shape[0]
        other = lax.ppermute(fields, "ctx", [(c, c ^ hop) for c in range(n_ctx)])
        fields = jnp.concatenate([fields, other], axis=0)
    weights = got
    e_k = got[:, 3 * part : 3 * part + n_e, : 4 * rows].astype(f32).sum(axis=0)
    e_cat = e_k[:, : 2 * rows] + e_k[:, 2 * rows :]
    a_got = got[:, 3 * part : 4 * part, 4 * rows :]
    a_all = jnp.concatenate(
        [
            a_got[:, :, :rows],
            a_got[:, 0:1, 2 * rows : 3 * rows],
            a_got[:, :, rows : 2 * rows],
            a_got[:, 1:2, 2 * rows : 3 * rows],
        ],
        axis=1,
    )
    a_all = a_all.transpose(1, 0, 2).reshape(18, n_dp * rows)
    a_hi, a_lo = a_all[:9], a_all[9:]

    gap = jnp.zeros((8 - half, channels), bf16)
    w_start = jnp.concatenate(
        [sw_hi.T, gap, sw_hi.T, gap, sw_lo.T, gap, jnp.zeros((8, channels), bf16)], axis=0
    )
    fields, w_start = lax.optimization_barrier((fields, w_start))

    length = lengths[0]
    b_hi, b_lo = split(gate_bias[0][None])
    a_cat = jnp.concatenate(
        [a_hi, a_hi, a_lo, b_hi, b_lo, jnp.zeros((3, 2 * channels), bf16)], axis=0
    ).T
    w_hi, w_lo = (
        jnp.concatenate([jnp.pad(x, ((0, 0), (3, 6 - half)))] * 3 + [jnp.zeros((channels, 5), bf16)], axis=1)
        for x in (sw_hi, sw_lo)
    )
    ec_hi, ec_lo = split(e_cat)
    gap = jnp.zeros((2, 2 * rows), bf16)
    e_pair = jnp.concatenate([ec_hi, gap, ec_lo, gap], axis=0)
    e_up = pad_to(jnp.concatenate([ec_hi, gap, ec_hi, gap, ec_lo], axis=0), 32, 2 * rows).T
    bias1 = strided(gate_bias[1][None]).T
    info = jnp.stack([length, k])
    pair = 2 * rows
    main = 2 * shard_len
    wide = epochs + 2 * (dilations[1] + 128)
    smem = pl.BlockSpec(memory_space=pltpu.SMEM)
    shapes = jax.ShapeDtypeStruct
    params = pltpu.CompilerParams(
        dimension_semantics=("arbitrary",), vmem_limit_bytes=60000 * 1024
    )
    forward = pl.pallas_call(
        functools.partial(forward_kernel, dilations[0], dilations[1], half),
        grid=(epochs // main,),
        in_specs=[
            smem,
            whole((n_ctx, n_pad, shard_len)),
            whole(a_cat.shape),
            whole(w_hi.shape),
            whole(w_lo.shape),
            whole(weights.shape),
            whole(bias1.shape),
            whole(e_pair.shape),
        ],
        out_specs=[columns(channels, main)] * 3
        + [columns(32, main), whole((pair, epochs)), whole((rows, epochs)),
           whole((rows, epochs)), whole((n_ctx, 32, shard_len)),
           whole((channels, channels)), whole((3 * pair, channels))],
        out_shape=[shapes((channels, epochs), bf16)] * 3
        + [shapes((32, epochs), bf16), shapes((pair, epochs), bf16), shapes((rows, epochs), f32),
           shapes((rows, epochs), f32), shapes((n_ctx, 32, shard_len), f32),
           shapes((channels, channels), bf16), shapes((3 * pair, channels), bf16)],
        scratch_shapes=[
            pltpu.VMEM((8, epochs + 512), f32),
            pltpu.VMEM((32, main), f32),
            pltpu.VMEM((2 * pair, wide), bf16),
            pltpu.VMEM((pair, epochs), f32),
            pltpu.VMEM((pair, shard_len), f32),
            pltpu.VMEM((rows, epochs), bf16),
            pltpu.VMEM((3 * pair, channels), bf16),
            pltpu.VMEM((3 * pair, 32), bf16),
        ],
        compiler_params=params,
        name="layers_forward",
    )
    g0, du0, dv0, s_all, g_own, du1, dv1, packed, mix_res, w_taps = forward(
        info, fields, a_cat, w_hi, w_lo, weights, bias1, e_pair
    )
    got = exchange(packed.reshape(n_ctx * 32, shard_len), "ctx").reshape(n_ctx, 32, shard_len)

    n_mix = channels // n_dp
    n_conv = 3 * pair // n_dp
    per = n_mix + n_conv + 8
    backward = pl.pallas_call(
        functools.partial(backward_kernel, dilations[1], half),
        grid=(epochs // main,),
        in_specs=[
            smem,
            whole((n_ctx, 32, shard_len)),
            whole((n_ctx, n_pad, shard_len)),
            whole((2 * half, shard_len)),
            whole((pair, 32)),
            whole((pair, epochs)),
            whole((rows, epochs)),
            whole((rows, epochs)),
            whole((3 * pair, channels)),
            whole((channels, 3 * pair)),
            whole((channels, channels)),
            whole((channels, 3 * pair)),
            whole((32, channels)),
        ]
        + [columns(channels, main)] * 3
        + [columns(32, main)],
        out_specs=[whole((1, half, shard_len)), whole((n_dp, per, channels))],
        out_shape=[shapes((1, half, shard_len), f32), shapes((n_dp, per, channels), bf16)],
        scratch_shapes=[
            pltpu.VMEM((32, shard_len), f32),
            pltpu.VMEM((32, shard_len), f32),
            pltpu.VMEM((pair, wide), bf16),
            pltpu.VMEM((8, wide), f32),
            pltpu.VMEM((rows, epochs), f32),
            pltpu.VMEM((3 * pair, epochs), bf16),
            pltpu.VMEM((3 * pair, channels), f32),
            pltpu.VMEM((channels, channels), f32),
            pltpu.VMEM((32, 2 * channels), f32),
            pltpu.VMEM((32, 3 * pair), f32),
            pltpu.VMEM((16, pair), f32),
            pltpu.VMEM((16, pair), f32),
            pltpu.VMEM((channels, main), f32),
            pltpu.VMEM((16, 2 * channels), f32),
            pltpu.VMEM((8, 256), f32),
            pltpu.VMEM((3 * pair, channels), f32),
            pltpu.VMEM((32, 3 * pair), f32),
        ],
        compiler_params=params,
        name="layers_backward",
    )
    coupled, packed = backward(
        info, got, fields, light_flux[0], e_up, g_own, du1, dv1, w_taps, w_taps.T, mix_res,
        dot(mix_res, w_taps, 0, 1).astype(bf16), w_start, g0, du0, dv0, s_all,
    )
    got = exchange(packed.reshape(n_dp * per, channels), "dp").reshape(n_dp, per, channels)
    got = got.astype(f32).sum(axis=0)
    mix_piece = got[:n_mix]
    conv_piece = got[n_mix : n_mix + n_conv].astype(bf16)
    smalls = got[n_mix + n_conv :]
    m_first = smalls[:, :128] + smalls[:, 384:]
    m_rest = smalls[4:6, 128:256] + smalls[6:8, 128:256]
    m_own = lax.dynamic_slice(
        jnp.concatenate([m_first, m_rest], axis=0), (0, rows * (dp % 2)), (10, rows)
    )
    start_own = jnp.where(dp < channels // 128, smalls[1 : 1 + half, 128:256], 0.0)
    g_own_sum = smalls[: 2 * half, 256:384]
    bias1_own = smalls[0:1, 128:256] + smalls[6:7, 256:384]
    mo_hi, mo_lo = split(m_own)
    mo_pair = jnp.concatenate([mo_hi[:9], mo_lo[:9]], axis=0)
    start_t = 0.0
    for tap in range(3):
        up = dot(mo_pair, conv0[:, tap * channels : (tap + 1) * channels])
        start_t = start_t + up[half * tap : half * tap + half] + up[9 + half * tap : 9 + half * tap + half]
    spot = lax.dynamic_update_slice(
        jnp.zeros((half, channels), f32), start_own, (0, 128 * (dp % (channels // 128)))
    )
    start_t = start_t + spot
    end_last = dot(g_own_sum[:, rows:], mix_last_k, 1, 1, highest)
    end_skip = jnp.where(low, 0.0, dot(g_own_sum[:, :rows], mix_skip_k, 1, 1, highest))
    g_rows = jnp.concatenate([g_own_sum, bias1_own], axis=0)
    parts = jnp.concatenate(
        [
            m_own,
            pad_to(g_rows, 10, 2 * rows),
            pad_to(jnp.concatenate([end_last, end_skip], axis=1), 10, last_rows + rows),
        ],
        axis=1,
    )
    width = parts.shape[1]
    parts_hi, parts_lo = split(parts)
    start_hi, start_lo = split(start_t)
    pack_rows = [
        conv_piece,
        mix_piece.astype(bf16),
        pad_to(jnp.concatenate([parts_hi, parts_lo[:, : 3 * rows]], axis=1), 10, channels),
        start_hi,
        start_lo,
    ]
    packed = jnp.concatenate(pack_rows, axis=0)
    per0 = packed.shape[0]
    per = -(-per0 // 8) * 8
    packed = pad_to(packed, per, channels)
    got = exchange(
        jnp.broadcast_to(packed[None], (n_ctx, per, channels)).reshape(n_ctx * per, channels), "ctx"
    ).reshape(n_ctx, per, channels)
    grad_conv1 = got[:, :n_conv].reshape(n_ctx, 3, part, channels).transpose(0, 2, 1, 3)
    grad_conv1 = grad_conv1.reshape(rows, 3 * channels).astype(f32)
    mix_rows = got[:, n_conv : n_conv + n_mix].astype(f32).sum(axis=0)
    base = n_conv + n_mix
    parts = got[:, base : base + 10].astype(f32)
    parts_lo = parts[:, :, width : width + 3 * rows]
    parts = jnp.concatenate(
        [parts[:, :, : 3 * rows] + parts_lo, parts[:, :, 3 * rows : width]], axis=2
    )
    start_t = got[:, base + 10 : base + 10 + 2 * half].astype(f32).sum(axis=0)
    start_t = start_t[:half] + start_t[half:]
    m_own = parts[:, :, :rows].sum(axis=0)
    g_all = parts[:, : 2 * half, rows : 3 * rows]
    g0_all = g_all[:, :, :rows].transpose(1, 0, 2).reshape(2 * half, channels)
    g1_all = g_all[:, :, rows:].reshape(n_ctx, 2 * half, half_dp, part).transpose(1, 2, 0, 3)
    g1_all = g1_all.reshape(2 * half, channels)
    bias1_all = parts[:, 2 * half, rows : 3 * rows].reshape(n_ctx, n_dp, part).transpose(1, 0, 2)
    bias1_all = bias1_all.reshape(2 * channels)
    end_both = parts[:, : 2 * half, 3 * rows :].sum(axis=0)
    a_grad = m_own[:9].T
    grad_conv0 = jnp.concatenate(
        [
            dot(a_grad[:, half * tap : half * tap + half], start_weight, 1, 1, highest)
            for tap in range(3)
        ],
        axis=1,
    )
    grad_mix_last = dot(ew_last, g1_all, 0, 0, highest)
    skip_rows = dot(ew_skip, g0_all, 0, 0, highest)

    other = lax.ppermute(
        mix_rows.astype(bf16), "dp", [(i + half_dp, i) for i in range(half_dp)]
    ).astype(f32)
    final = jnp.concatenate(
        [
            start_t.reshape(-1, 128),
            pad_to(end_both, 2 * half, 128),
            pad_to(m_own[9:10], 1, 128),
        ],
        axis=0,
    )
    per0 = final.shape[0]
    per = -(-per0 // 8) * 8
    final = pad_to(final, per, 128)
    got = exchange(
        jnp.broadcast_to(final[None], (n_dp, per, 128)).reshape(n_dp * per, 128), "dp"
    ).reshape(n_dp, per, 128)
    n_start = half * channels // 128
    grad_start = got[:, :n_start].sum(axis=0).reshape(half, channels).T
    ends = got[:, n_start : n_start + 2 * half]
    grad_end = ends[:, :, :last_rows].transpose(1, 0, 2).reshape(2 * half, channels)
    grad_end = grad_end + ends[half_dp:, :, last_rows : last_rows + rows].transpose(
        1, 0, 2
    ).reshape(2 * half, channels)
    bias0_all = got[:, n_start + 2 * half, :rows].reshape(2 * channels)
    grad_bias = jnp.stack([bias0_all, bias1_all])
    residual = jnp.concatenate([mix_rows, other], axis=0)
    grad_mix_first = jnp.where(low, residual, skip_rows)
    grad_conv = jnp.stack([grad_conv0, grad_conv1])
    return (coupled, grad_start, grad_conv, grad_bias, grad_mix_first, grad_mix_last, grad_end)


def solution(mesh):
    in_specs = (
        P("dp", None, "ctx"),
        P("dp"),
        P("dp", "ctx"),
        P(),
        P(None, "dp", None),
        P(),
        P("dp", None),
        P("dp", None),
        P(),
        P("dp", None, "ctx"),
    )
    out_specs = (
        P("dp", None, "ctx"),
        P(),
        P(None, "dp", None),
        P(),
        P("dp", None),
        P("dp", None),
        P(),
    )
    return jax.shard_map(local, mesh=mesh, in_specs=in_specs, out_specs=out_specs, check_vma=False)
```

```python
import functools

import jax
import jax.numpy as jnp
from jax import lax
from jax.experimental import pallas as pl
from jax.experimental.pallas import tpu as pltpu
from jax.sharding import PartitionSpec as P

BUCKETS = 4
highest = lax.Precision.HIGHEST
bf16 = jnp.bfloat16
f32 = jnp.float32


def dot(a, b, ca=1, cb=0, precision=None):
    return lax.dot_general(
        a, b, (((ca,), (cb,)), ((), ())), precision=precision, preferred_element_type=f32
    )


def split(x):
    hi = lax.reduce_precision(x, 8, 7)
    return hi.astype(bf16), (x - hi).astype(bf16)


def pad_to(x, rows, cols):
    return jnp.pad(x, ((0, rows - x.shape[0]), (0, cols - x.shape[1])))


def shift(x, n):
    total = x.shape[1]
    if n > 0:
        return jnp.pad(x[:, : total - n], ((0, 0), (n, 0)))
    return jnp.pad(x[:, -n:], ((0, 0), (0, -n)))


def tap_of(x, off, dilation, side):
    out = shift(x, side * dilation)
    for step in range(1, BUCKETS):
        out = jnp.where(off == step, shift(x, side * (dilation + step)), out)
    return out


def tap_back(x, off, dilation, side):
    out = 0.0
    for step in range(BUCKETS):
        out = out + shift(jnp.where(off == step, x, 0.0), -side * (dilation + step))
    return out


def exchange(x, axis):
    return lax.all_to_all(x, axis, 0, 0, tiled=True)


def nt(a, b):
    return dot(a, b, 1, 1)


def rolled(x, start, width):
    if start % 128 == 0:
        return x[:, start : start + width]
    return pltpu.roll(x, x.shape[1] - start, 1)[:, :width]


def steps_apart(shape):
    return (
        lax.broadcasted_iota(jnp.int32, shape, 0) - lax.broadcasted_iota(jnp.int32, shape, 1)
    ).astype(f32)


def one_hot(apart, target):
    return jnp.where(apart == target, 1.0, 0.0).astype(bf16)


def valid_row(c, width, length):
    at = lax.broadcasted_iota(jnp.int32, (1, width), 1) + c * width
    return (at < length).astype(f32)


def packet_kernel(
    info, conv, mix_first, mix_far, mix_last, start, ends,
    packet,
    sw, low_rows, ew, turn,
):
    dp = info[0]
    k = info[1]
    n_dp, per, channels = packet.shape
    half = start.shape[0]
    rows = mix_first.shape[0]
    last_rows = mix_last.shape[0]
    n_e = ends.shape[0]
    part = (per - 8 - rows // 2) // 3
    upper = dp >= n_dp // 2

    group = conv[1, pl.ds(pl.multiple_of((k // 2) * 2 * part, 2 * part), 2 * part), :].astype(f32)
    mine = jnp.where(k % 2 == 1, group[part:], group[:part]).astype(bf16)

    sw[...] = jnp.zeros(sw.shape, f32)
    sw[0:half, :] = start[...]
    full = sw[...]
    sw_hi = full.astype(bf16)
    sw_lo = (full - sw_hi.astype(f32)).astype(bf16)
    turn[...] = jnp.zeros(turn.shape, f32)
    for tap in range(3):
        block = conv[0, :, tap * channels : (tap + 1) * channels]
        one = nt(sw_hi, block) + nt(sw_lo, block)
        turn[half * tap : half * (tap + 1), 0:rows] = one[0:half]
    a_t = turn[...]
    a_hi = a_t[0:16].astype(bf16).astype(f32)
    a_lo = a_t[0:16] - a_hi
    lane = lax.broadcasted_iota(jnp.int32, (8, 128), 1)
    row = lax.broadcasted_iota(jnp.int32, (8, 128), 0)
    near = jnp.where(lane < rows, a_hi[0:8], pltpu.roll(a_lo[0:8], rows, 1))
    far = jnp.where(row == 0, a_hi[8:16], pltpu.roll(a_lo[8:16], 1, 0))

    ew[...] = jnp.zeros(ew.shape, f32)
    ew[0:n_e, :] = ends[...]
    e_all = ew[...]
    wide = lax.broadcasted_iota(jnp.int32, (8, 128), 1)

    def product(shift, count, source, keep):
        moved = pltpu.roll(e_all, lax.rem(channels - shift, channels), 1)[:, 0:128]
        moved = jnp.where(jnp.logical_and(wide < count, keep), moved, 0.0)
        hi = moved.astype(bf16)
        low = (moved - hi.astype(f32)).astype(bf16)
        low_rows[...] = jnp.zeros(low_rows.shape, bf16)
        low_rows[0:count, :] = source[...]
        out = dot(hi, low_rows[...]) + dot(low, low_rows[...])
        out_hi = out.astype(bf16)
        return out_hi, (out - out_hi.astype(f32)).astype(bf16)

    at = lax.broadcasted_iota(jnp.int32, (channels, 128), 0)
    col = lax.broadcasted_iota(jnp.int32, (channels, 128), 1)
    m = col - rows
    pick0 = jnp.where(jnp.logical_and(col < rows, at == rows * k + col), 1.0, 0.0).astype(bf16)
    target = (m >> 3) * rows + part * k + (m & 7)
    pick1 = jnp.where(jnp.logical_and(m >= 0, at == target), 1.0, 0.0).astype(bf16)
    e0_hi, e0_lo = product(
        rows * jnp.maximum(dp - n_dp // 2, 0), rows, mix_first, upper
    )
    e1_hi, e1_lo = product(last_rows * dp, last_rows, mix_last, dp >= 0)
    e_hi = dot(e0_hi, pick0) + dot(e1_hi, pick1)
    e_lo = dot(e0_lo, pick0) + dot(e1_lo, pick1)

    send = jnp.where(
        upper, mix_far[rows // 2 :, :].astype(f32), mix_first[0 : rows // 2, :].astype(f32)
    )
    send = send.astype(bf16)
    base = 3 * part
    for j in range(n_dp):
        for tap in range(3):
            packet[j, tap * part : (tap + 1) * part, :] = mine[
                :, tap * channels : (tap + 1) * channels
            ]
        packet[j, base : base + 8, 0:128] = e_hi.astype(bf16)
        packet[j, base : base + 8, 128:256] = e_lo.astype(bf16)
        packet[j, base : base + 8, 256:384] = near.astype(bf16)
        packet[j, base : base + 8, 384:512] = far.astype(bf16)
        packet[j, base + 8 :, :] = send


def forward_kernel(
    dil0, dil1, half,
    info, fields, a_cat, w_hi, w_lo, weights, bias1, e_pair,
    g0_out, du0_out, dv0_out, s_out, gown_out, du1_out, dv1_out, packet, mix, w_taps,
    fpad, s_cat, prod, centre, pre_s, g_keep, w_mix, w_start,
):
    i = pl.program_id(0)
    nb = fields.shape[0]
    bw = fields.shape[2]
    rows = gown_out.shape[0] // 2
    channels = mix.shape[0]
    pad0 = 256
    pad1 = dil1 + 128
    length = info[0]
    k = info[1]

    @pl.when(i == 0)
    def _():
        fpad[:, 0:pad0] = jnp.zeros((8, pad0), f32)
        fpad[:, pad0 + nb * bw :] = jnp.zeros((8, pad0), f32)
        prod[:, 0:pad1] = jnp.zeros((prod.shape[0], pad1), bf16)
        prod[:, pad1 + nb * bw :] = jnp.zeros((prod.shape[0], pad1), bf16)
        n_dp = weights.shape[0]
        part = 2 * rows // n_dp
        half_rows = rows // 2
        for j in range(n_dp):
            for tap in range(3):
                to = tap * 2 * rows + j * part
                w_taps[to : to + part, :] = weights[j, tap * part : (tap + 1) * part, :]
            to = rows * (j % (n_dp // 2)) + half_rows * (j // (n_dp // 2))
            mix[to : to + half_rows, :] = weights[j, 4 * part :, :]
        w_mix[...] = dot(w_taps[...], mix[...]).astype(bf16)
        full = dot(w_taps[...], w_hi[...]) + dot(w_taps[...], w_lo[...])
        top = full.astype(bf16).astype(f32)
        col = lax.broadcasted_iota(jnp.int32, full.shape, 1)
        w_start[...] = jnp.where(col < 18, top, full - top).astype(bf16)
        s_cat[...] = jnp.zeros(s_cat.shape, f32)
        s_cat[27:29, :] = jnp.ones((2, g0_out.shape[1]), f32)
        packet[:, 24:32, :] = jnp.zeros((nb, 8, bw), f32)
        for c in range(nb):
            block = fields[c ^ k].astype(f32)
            valid = valid_row(c, bw, length)
            at = slice(pad0 + c * bw, pad0 + (c + 1) * bw)
            fpad[0:half, at] = block[0:half] * valid
            fpad[half : 2 * half, at] = block[2 * half : 3 * half] * valid
            fpad[6:7, at] = block[6 * half : 6 * half + 1]
            fpad[7:8, at] = valid

    mw = g0_out.shape[1]
    base = pl.multiple_of(i * mw, mw)
    near = fpad[:, pl.ds(pl.multiple_of(pad0 + base, 128), mw)]
    off = near[6:7]
    valid = near[7:8]
    behind = fpad[:, pl.ds(pl.multiple_of(base, 128), mw + 2 * dil0)]
    ahead = fpad[:, pl.ds(pl.multiple_of(pad0 + base, 128), mw + 2 * dil0)]
    left = rolled(behind, dil0, mw)
    right = rolled(ahead, dil0, mw)
    for step in range(1, BUCKETS):
        left = jnp.where(off == step, rolled(behind, dil0 - step, mw), left)
        right = jnp.where(off == step, rolled(ahead, dil0 + step, mw), right)
    for part, at in ((left, 0), (near, 3), (right, 6)):
        s_cat[at : at + half, :] = part[0:half]
        s_cat[9 + at : 9 + at + half, :] = part[half : 2 * half]
        s_cat[18 + at : 18 + at + half, :] = part[0:half]
    s_b = s_cat[...].astype(bf16)
    s_out[...] = s_b
    step_rows = 128
    for r in range(0, channels, step_rows):
        u = dot(a_cat[r : r + step_rows, :], s_b)
        v = dot(a_cat[channels + r : channels + r + step_rows, :], s_b)
        t = jnp.tanh(u)
        s = 0.5 * jnp.tanh(0.5 * v) + 0.5
        g = t * s
        g0_out[r : r + step_rows, :] = (g * valid).astype(bf16)
        du0_out[r : r + step_rows, :] = (s - g * t).astype(bf16)
        dv0_out[r : r + step_rows, :] = (g - g * s).astype(bf16)
    pair = 2 * rows
    g_b = g0_out[...]
    for tap in range(3):
        at = slice(tap * pair, (tap + 1) * pair)
        part = dot(w_mix[at, :], g_b) + dot(w_start[at, :], s_b)
        if tap == 1:
            centre[:, pl.ds(base, mw)] = part
        else:
            to = tap // 2 * pair
            cols = pl.ds(pl.multiple_of(pad1 + base, 128), mw)
            prod[to : to + pair, cols] = part.astype(bf16)
    g_keep[:, pl.ds(base, mw)] = g0_out[pl.ds(pl.multiple_of(rows * k, rows), rows), :]

    @pl.when(i == pl.num_programs(0) - 1)
    def _():
        apart = steps_apart((256, 128))

        def body(c, carry):
            base = pl.multiple_of(c * bw, bw)
            off = fpad[6:7, pl.ds(pl.multiple_of(pad0 + base, 128), bw)]
            for tile in range(bw // 128):
                lane = slice(tile * 128, (tile + 1) * 128)
                behind = prod[0:pair, pl.ds(pl.multiple_of(base + tile * 128, 128), 256)]
                ahead = prod[
                    pair:,
                    pl.ds(pl.multiple_of(pad1 + dil1 + base + tile * 128, 128), 256),
                ]
                pre_s[:, lane] = dot(behind, one_hot(apart, 128.0 - off[:, lane])) + dot(
                    ahead, one_hot(apart, off[:, lane])
                )
            pre = pre_s[...] + centre[:, pl.ds(base, bw)] + bias1[...]
            t = jnp.tanh(pre[:rows])
            s = 0.5 * jnp.tanh(0.5 * pre[rows:]) + 0.5
            g = t * s
            du1_out[:, pl.ds(base, bw)] = s - g * t
            dv1_out[:, pl.ds(base, bw)] = g - g * s
            gown_out[0:rows, pl.ds(base, bw)] = g_keep[:, pl.ds(base, bw)]
            gown_out[rows:, pl.ds(base, bw)] = g.astype(bf16)
            part = dot(e_pair[...], gown_out[:, pl.ds(base, bw)])
            part = part[0 : 2 * half] + part[8 : 8 + 2 * half]
            for d in range(nb):
                for h in range(half):
                    packet[d, pl.ds(h * nb + c, 1), :] = part[h : h + 1]
            packet[c, 24 : 24 + half, :] = part[half : 2 * half]
            return carry

        lax.fori_loop(0, nb, body, 0, unroll=2)


def backward_kernel(
    dil1, half,
    info, got, fields, flux, e_up, gown, du1, dv1, w_taps, w_taps_t, mix, w_mix_t, w_start,
    g0, du0, dv0, s_in,
    coupled, packet,
    ends, d_cat, dz_pad, off_pad, d_e0, d_taps, acc_q, acc_mix, acc_m, acc_s, acc_g, acc_b,
    dg, m_rows, share, acc_conv, small,
):
    i = pl.program_id(0)
    nb = fields.shape[0]
    bw = fields.shape[2]
    pair = gown.shape[0]
    rows = pair // 2
    channels = mix.shape[0]
    n_dp = packet.shape[0]
    pad1 = dil1 + 128
    length = info[0]
    k = info[1]

    @pl.when(i == 0)
    def _():
        for ref in (acc_q, acc_m, acc_s, acc_g, acc_b, d_cat, m_rows, share, small):
            ref[...] = jnp.zeros(ref.shape, f32)
        dz_pad[:, 0:pad1] = jnp.zeros((pair, pad1), bf16)
        dz_pad[:, pad1 + nb * bw :] = jnp.zeros((pair, pad1), bf16)
        off_pad[:, 0:pad1] = jnp.full((8, pad1), -1.0, f32)
        off_pad[:, pad1 + nb * bw :] = jnp.full((8, pad1), -1.0, f32)
        total = got[0]
        for src in range(1, nb):
            total = total + got[src]
        ends[...] = total
        mine = valid_row(k, bw, length)
        for h in range(half):
            growth = jnp.exp(ends[pl.ds(h * nb + k, 1), :])
            coupled[0, h : h + 1, :] = (
                growth * flux[half + h : half + h + 1] + ends[24 + h : 25 + h, :]
            ) * mine

        def first(c, carry):
            base = pl.multiple_of(c * bw, bw)
            at = pl.multiple_of(pad1 + base, 128)
            block = fields[c ^ k].astype(f32)
            valid = valid_row(c, bw, length)
            off_pad[0:1, pl.ds(at, bw)] = block[6 * half : 6 * half + 1]
            flux2 = block[half : 2 * half] + block[3 * half : 4 * half]
            cot = (block[4 * half : 5 * half] + block[5 * half : 6 * half]) * valid
            for h in range(half):
                growth = jnp.exp(ends[pl.ds(h * nb + c, 1), :])
                d_cat[h : h + 1, :] = cot[h : h + 1] * growth * flux2[h : h + 1]
            d_cat[half : 2 * half, :] = cot
            full = d_cat[0:8, :]
            hi = full.astype(bf16).astype(f32)
            lo = full - hi
            d_cat[8:16, :] = lo
            d_cat[16:24, :] = hi
            d_gated = dot(e_up[...], d_cat[...].astype(bf16))
            acc_g[...] += nt(d_cat[8:24, :].astype(bf16), gown[:, pl.ds(base, bw)])
            d_e0[:, pl.ds(base, bw)] = d_gated[:rows]
            up = d_gated[rows : 2 * rows]
            dz_pad[0:rows, pl.ds(at, bw)] = (up * du1[:, pl.ds(base, bw)]).astype(bf16)
            dz_pad[rows:, pl.ds(at, bw)] = (up * dv1[:, pl.ds(base, bw)]).astype(bf16)
            return carry

        lax.fori_loop(0, nb, first, 0, unroll=2)

        apart = steps_apart((128, 256))

        def second(c, carry):
            base = pl.multiple_of(c * bw, bw)
            valid = valid_row(c, bw, length)
            for tile in range(bw // 128):
                lane = pl.ds(pl.multiple_of(base + tile * 128, 128), 128)
                late = pl.ds(pl.multiple_of(pad1 + dil1 + base + tile * 128, 128), 256)
                early = pl.ds(pl.multiple_of(base + tile * 128, 128), 256)
                left = nt(dz_pad[:, late], one_hot(apart, -off_pad[0:1, late]))
                right = nt(dz_pad[:, early], one_hot(apart, off_pad[0:1, early] - 128.0))
                d_taps[0:pair, lane] = left.astype(bf16)
                d_taps[2 * pair :, lane] = (
                    right * valid[:, tile * 128 : (tile + 1) * 128]
                ).astype(bf16)
            centre = dz_pad[:, pl.ds(pl.multiple_of(pad1 + base, 128), bw)]
            d_taps[pair : 2 * pair, pl.ds(base, bw)] = centre
            acc_b[...] += nt(jnp.ones((16, bw), bf16), centre)
            return carry

        lax.fori_loop(0, nb, second, 0, unroll=2)

    mw = g0.shape[1]
    base = pl.multiple_of(i * mw, mw)
    d_blk = d_taps[:, pl.ds(base, mw)]
    s_b = s_in[...]
    acc_q[...] += nt(d_blk, g0[...])
    acc_s[...] += nt(s_b, d_blk)
    dg[...] = dot(w_mix_t[...], d_blk)
    own = pl.ds(pl.multiple_of(rows * k, rows), rows)
    dg[own, :] = dg[own, :] + d_e0[:, pl.ds(base, mw)]
    up = dg[...]
    acc_m[:, 0:channels] += nt(s_b, (up * du0[...].astype(f32)).astype(bf16))
    acc_m[:, channels:] += nt(s_b, (up * dv0[...].astype(f32)).astype(bf16))

    @pl.when(i == pl.num_programs(0) - 1)
    def _():
        per_mix = channels // n_dp
        eighth = pair // n_dp
        q = acc_q[...]
        q_hi = q.astype(bf16)
        small[0:half, :] = acc_s[3 : 3 + half, :] + acc_s[12 : 12 + half, :]
        seen = small[0:8, :]
        seen_hi = seen.astype(bf16).astype(f32)
        small[8:16, :] = seen - seen_hi
        small[16:24, :] = seen
        d_start = small[...].astype(bf16)
        acc_conv[...] = nt(q_hi, mix[...]) + dot(d_start, w_start[...], 0, 0)
        acc_mix[...] = dot(w_taps_t[...], q_hi)
        starts = dot(d_start, w_taps[...])
        starts = starts[0:half] + starts[8 : 8 + half]
        m_rows[0:9, :] = acc_m[0:9, :] + acc_m[9:18, :]
        m_rows[9:10, :] = acc_m[27:28, :]
        bias = acc_b[0:1, :]
        share[0:1, 0:128] = bias
        share[6:7, 128:256] = bias - bias.astype(bf16).astype(f32)
        share[0 : 2 * half, 128:256] = acc_g[8 : 8 + 2 * half, :] + acc_g[0 : 2 * half, :]
        for j in range(n_dp):
            row = 64 * (j % (n_dp // 2)) + per_mix * (j // (n_dp // 2))
            packet[j, 0:per_mix, :] = acc_mix[row : row + per_mix, :].astype(bf16)
            for tap in range(3):
                at = per_mix + tap * eighth
                row = tap * pair + j * eighth
                packet[j, at : at + eighth, :] = acc_conv[row : row + eighth, :].astype(bf16)
            if j < channels // 128:
                share[1 : 1 + half, 0:128] = starts[:, 128 * j : 128 * (j + 1)]
            else:
                share[1 : 1 + half, 0:128] = jnp.zeros((half, 128), f32)
            at = per_mix + 3 * eighth
            cols = slice(128 * (j // 2), 128 * (j // 2) + 128)
            share[6:8, 0:128] = m_rows[8:10, cols]
            low = m_rows[0:10, cols]
            low = low - low.astype(bf16).astype(f32)
            share[4:6, 0:128] = low[8:10]
            packet[j, at : at + 8, 0:128] = m_rows[0:8, cols].astype(bf16)
            packet[j, at : at + 8, 128:256] = share[:, 0:128].astype(bf16)
            packet[j, at : at + 8, 256:384] = share[:, 128:256].astype(bf16)
            packet[j, at : at + 8, 384:512] = low[0:8].astype(bf16)


def whole(shape):
    return pl.BlockSpec(shape, lambda i: (0,) * len(shape))


def columns(rows, width):
    return pl.BlockSpec((rows, width), lambda i: (0, i))


def local(
    light_flux,
    lengths,
    offsets,
    start_weight,
    conv_weight,
    gate_bias,
    mix_first,
    mix_last,
    end_weight,
    cotangent,
):
    n_dp = lax.axis_size("dp")
    n_ctx = lax.axis_size("ctx")
    half_dp = n_dp // 2
    dp = lax.axis_index("dp")
    k = lax.axis_index("ctx")
    low = dp < half_dp
    shard_len = light_flux.shape[2]
    half = light_flux.shape[1] // 2
    channels = start_weight.shape[0]
    epochs = shard_len * n_ctx
    dilations = (shard_len // 4, shard_len + shard_len // 2)
    rows = conv_weight.shape[1]
    last_rows = mix_last.shape[0]
    conv0, conv1 = conv_weight[0], conv_weight[1]
    part = rows // n_ctx
    n_e = 2 * half

    def strided(x):
        lead = x.shape[0]
        cols = x.shape[1]
        view = x.reshape(lead, cols // rows, n_ctx, part)
        return lax.dynamic_slice(
            view, (0, 0, k, 0), (lead, cols // rows, 1, part)
        ).reshape(lead, cols // n_ctx)

    half_rows = rows // 2
    mix_far = lax.ppermute(
        mix_first, "dp", [(i, i + half_dp) for i in range(half_dp)]
    )
    sw_hi, sw_lo = split(start_weight)
    ew_last = lax.dynamic_slice(end_weight, (0, last_rows * dp), (n_e, last_rows))
    ew_skip = lax.dynamic_slice(
        end_weight, (0, rows * jnp.maximum(dp - half_dp, 0)), (n_e, rows)
    )
    ew_skip = jnp.where(low, 0.0, ew_skip)
    mix_last_k = strided(mix_last).astype(f32)
    mix_skip_k = lax.dynamic_slice(mix_first, (0, rows * k), (rows, rows)).astype(f32)
    per = 3 * part + 8 + half_rows
    smem = pl.BlockSpec(memory_space=pltpu.SMEM)
    packets = pl.pallas_call(
        packet_kernel,
        in_specs=[smem] + [pl.BlockSpec(memory_space=pltpu.VMEM)] * 6,
        out_specs=pl.BlockSpec(memory_space=pltpu.VMEM),
        out_shape=jax.ShapeDtypeStruct((n_dp, per, channels), bf16),
        scratch_shapes=[
            pltpu.VMEM((16, channels), f32),
            pltpu.VMEM((128, channels), bf16),
            pltpu.VMEM((8, channels), f32),
            pltpu.VMEM((16, 128), f32),
        ],
        name="weight_packets",
    )(jnp.stack([dp, k]), conv_weight, mix_first, mix_far, mix_last, start_weight.T, end_weight)
    got = exchange(packets.reshape(n_dp * per, channels), "dp").reshape(n_dp, per, channels)
    flux_hi, flux_lo = split(light_flux[0])
    cot_hi, cot_lo = split(cotangent[0])
    n_in = 6 * half + 1
    inputs = jnp.concatenate(
        [flux_hi, flux_lo, cot_hi, cot_lo, offsets.astype(bf16)], axis=0
    )
    n_pad = -(-n_in // 8) * 8
    inputs = pad_to(inputs, n_pad, shard_len)

    fields = inputs[None]
    while fields.shape[0] < n_ctx:
        hop = fields.shape[0]
        other = lax.ppermute(fields, "ctx", [(c, c ^ hop) for c in range(n_ctx)])
        fields = jnp.concatenate([fields, other], axis=0)
    weights = got
    e_k = got[:, 3 * part : 3 * part + n_e, : 4 * rows].astype(f32).sum(axis=0)
    e_cat = e_k[:, : 2 * rows] + e_k[:, 2 * rows :]
    a_got = got[:, 3 * part : 4 * part, 4 * rows :]
    a_all = jnp.concatenate(
        [
            a_got[:, :, :rows],
            a_got[:, 0:1, 2 * rows : 3 * rows],
            a_got[:, :, rows : 2 * rows],
            a_got[:, 1:2, 2 * rows : 3 * rows],
        ],
        axis=1,
    )
    a_all = a_all.transpose(1, 0, 2).reshape(18, n_dp * rows)
    a_hi, a_lo = a_all[:9], a_all[9:]

    gap = jnp.zeros((8 - half, channels), bf16)
    w_start = jnp.concatenate(
        [sw_hi.T, gap, sw_hi.T, gap, sw_lo.T, gap, jnp.zeros((8, channels), bf16)], axis=0
    )
    fields, w_start = lax.optimization_barrier((fields, w_start))

    length = lengths[0]
    b_hi, b_lo = split(gate_bias[0][None])
    a_cat = jnp.concatenate(
        [a_hi, a_hi, a_lo, b_hi, b_lo, jnp.zeros((3, 2 * channels), bf16)], axis=0
    ).T
    w_hi, w_lo = (
        jnp.concatenate([jnp.pad(x, ((0, 0), (3, 6 - half)))] * 3 + [jnp.zeros((channels, 5), bf16)], axis=1)
        for x in (sw_hi, sw_lo)
    )
    ec_hi, ec_lo = split(e_cat)
    gap = jnp.zeros((2, 2 * rows), bf16)
    e_pair = jnp.concatenate([ec_hi, gap, ec_lo, gap], axis=0)
    e_up = pad_to(jnp.concatenate([ec_hi, gap, ec_hi, gap, ec_lo], axis=0), 32, 2 * rows).T
    bias1 = strided(gate_bias[1][None]).T
    info = jnp.stack([length, k])
    pair = 2 * rows
    main = 2 * shard_len
    wide = epochs + 2 * (dilations[1] + 128)
    smem = pl.BlockSpec(memory_space=pltpu.SMEM)
    shapes = jax.ShapeDtypeStruct
    params = pltpu.CompilerParams(
        dimension_semantics=("arbitrary",), vmem_limit_bytes=60000 * 1024
    )
    forward = pl.pallas_call(
        functools.partial(forward_kernel, dilations[0], dilations[1], half),
        grid=(epochs // main,),
        in_specs=[
            smem,
            whole((n_ctx, n_pad, shard_len)),
            whole(a_cat.shape),
            whole(w_hi.shape),
            whole(w_lo.shape),
            whole(weights.shape),
            whole(bias1.shape),
            whole(e_pair.shape),
        ],
        out_specs=[columns(channels, main)] * 3
        + [columns(32, main), whole((pair, epochs)), whole((rows, epochs)),
           whole((rows, epochs)), whole((n_ctx, 32, shard_len)),
           whole((channels, channels)), whole((3 * pair, channels))],
        out_shape=[shapes((channels, epochs), bf16)] * 3
        + [shapes((32, epochs), bf16), shapes((pair, epochs), bf16), shapes((rows, epochs), f32),
           shapes((rows, epochs), f32), shapes((n_ctx, 32, shard_len), f32),
           shapes((channels, channels), bf16), shapes((3 * pair, channels), bf16)],
        scratch_shapes=[
            pltpu.VMEM((8, epochs + 512), f32),
            pltpu.VMEM((32, main), f32),
            pltpu.VMEM((2 * pair, wide), bf16),
            pltpu.VMEM((pair, epochs), f32),
            pltpu.VMEM((pair, shard_len), f32),
            pltpu.VMEM((rows, epochs), bf16),
            pltpu.VMEM((3 * pair, channels), bf16),
            pltpu.VMEM((3 * pair, 32), bf16),
        ],
        compiler_params=params,
        name="layers_forward",
    )
    g0, du0, dv0, s_all, g_own, du1, dv1, packed, mix_res, w_taps = forward(
        info, fields, a_cat, w_hi, w_lo, weights, bias1, e_pair
    )
    got = exchange(packed.reshape(n_ctx * 32, shard_len), "ctx").reshape(n_ctx, 32, shard_len)

    n_mix = channels // n_dp
    n_conv = 3 * pair // n_dp
    per = n_mix + n_conv + 8
    backward = pl.pallas_call(
        functools.partial(backward_kernel, dilations[1], half),
        grid=(epochs // main,),
        in_specs=[
            smem,
            whole((n_ctx, 32, shard_len)),
            whole((n_ctx, n_pad, shard_len)),
            whole((2 * half, shard_len)),
            whole((pair, 32)),
            whole((pair, epochs)),
            whole((rows, epochs)),
            whole((rows, epochs)),
            whole((3 * pair, channels)),
            whole((channels, 3 * pair)),
            whole((channels, channels)),
            whole((channels, 3 * pair)),
            whole((32, channels)),
        ]
        + [columns(channels, main)] * 3
        + [columns(32, main)],
        out_specs=[whole((1, half, shard_len)), whole((n_dp, per, channels))],
        out_shape=[shapes((1, half, shard_len), f32), shapes((n_dp, per, channels), bf16)],
        scratch_shapes=[
            pltpu.VMEM((32, shard_len), f32),
            pltpu.VMEM((32, shard_len), f32),
            pltpu.VMEM((pair, wide), bf16),
            pltpu.VMEM((8, wide), f32),
            pltpu.VMEM((rows, epochs), f32),
            pltpu.VMEM((3 * pair, epochs), bf16),
            pltpu.VMEM((3 * pair, channels), f32),
            pltpu.VMEM((channels, channels), f32),
            pltpu.VMEM((32, 2 * channels), f32),
            pltpu.VMEM((32, 3 * pair), f32),
            pltpu.VMEM((16, pair), f32),
            pltpu.VMEM((16, pair), f32),
            pltpu.VMEM((channels, main), f32),
            pltpu.VMEM((16, 2 * channels), f32),
            pltpu.VMEM((8, 256), f32),
            pltpu.VMEM((3 * pair, channels), f32),
            pltpu.VMEM((32, 3 * pair), f32),
        ],
        compiler_params=params,
        name="layers_backward",
    )
    coupled, packed = backward(
        info, got, fields, light_flux[0], e_up, g_own, du1, dv1, w_taps, w_taps.T, mix_res,
        dot(mix_res, w_taps, 0, 1).astype(bf16), w_start, g0, du0, dv0, s_all,
    )
    got = exchange(packed.reshape(n_dp * per, channels), "dp").reshape(n_dp, per, channels)
    got = got.astype(f32).sum(axis=0)
    mix_piece = got[:n_mix]
    conv_piece = got[n_mix : n_mix + n_conv].astype(bf16)
    smalls = got[n_mix + n_conv :]
    m_first = smalls[:, :128] + smalls[:, 384:]
    m_rest = smalls[4:6, 128:256] + smalls[6:8, 128:256]
    m_own = lax.dynamic_slice(
        jnp.concatenate([m_first, m_rest], axis=0), (0, rows * (dp % 2)), (10, rows)
    )
    start_own = jnp.where(dp < channels // 128, smalls[1 : 1 + half, 128:256], 0.0)
    g_own_sum = smalls[: 2 * half, 256:384]
    bias1_own = smalls[0:1, 128:256] + smalls[6:7, 256:384]
    mo_hi, mo_lo = split(m_own)
    mo_pair = jnp.concatenate([mo_hi[:9], mo_lo[:9]], axis=0)
    start_t = 0.0
    for tap in range(3):
        up = dot(mo_pair, conv0[:, tap * channels : (tap + 1) * channels])
        start_t = start_t + up[half * tap : half * tap + half] + up[9 + half * tap : 9 + half * tap + half]
    spot = lax.dynamic_update_slice(
        jnp.zeros((half, channels), f32), start_own, (0, 128 * (dp % (channels // 128)))
    )
    start_t = start_t + spot
    end_last = dot(g_own_sum[:, rows:], mix_last_k, 1, 1, highest)
    end_skip = jnp.where(low, 0.0, dot(g_own_sum[:, :rows], mix_skip_k, 1, 1, highest))
    g_rows = jnp.concatenate([g_own_sum, bias1_own], axis=0)
    parts = jnp.concatenate(
        [
            m_own,
            pad_to(g_rows, 10, 2 * rows),
            pad_to(jnp.concatenate([end_last, end_skip], axis=1), 10, last_rows + rows),
        ],
        axis=1,
    )
    width = parts.shape[1]
    parts_hi, parts_lo = split(parts)
    start_hi, start_lo = split(start_t)
    pack_rows = [
        conv_piece,
        mix_piece.astype(bf16),
        pad_to(jnp.concatenate([parts_hi, parts_lo[:, : 3 * rows]], axis=1), 10, channels),
        start_hi,
        start_lo,
    ]
    packed = jnp.concatenate(pack_rows, axis=0)
    per0 = packed.shape[0]
    per = -(-per0 // 8) * 8
    packed = pad_to(packed, per, channels)
    got = exchange(
        jnp.broadcast_to(packed[None], (n_ctx, per, channels)).reshape(n_ctx * per, channels), "ctx"
    ).reshape(n_ctx, per, channels)
    grad_conv1 = got[:, :n_conv].reshape(n_ctx, 3, part, channels).transpose(0, 2, 1, 3)
    grad_conv1 = grad_conv1.reshape(rows, 3 * channels).astype(f32)
    mix_rows = got[:, n_conv : n_conv + n_mix].astype(f32).sum(axis=0)
    base = n_conv + n_mix
    parts = got[:, base : base + 10].astype(f32)
    parts_lo = parts[:, :, width : width + 3 * rows]
    parts = jnp.concatenate(
        [parts[:, :, : 3 * rows] + parts_lo, parts[:, :, 3 * rows : width]], axis=2
    )
    start_t = got[:, base + 10 : base + 10 + 2 * half].astype(f32).sum(axis=0)
    start_t = start_t[:half] + start_t[half:]
    m_own = parts[:, :, :rows].sum(axis=0)
    g_all = parts[:, : 2 * half, rows : 3 * rows]
    g0_all = g_all[:, :, :rows].transpose(1, 0, 2).reshape(2 * half, channels)
    g1_all = g_all[:, :, rows:].reshape(n_ctx, 2 * half, half_dp, part).transpose(1, 2, 0, 3)
    g1_all = g1_all.reshape(2 * half, channels)
    bias1_all = parts[:, 2 * half, rows : 3 * rows].reshape(n_ctx, n_dp, part).transpose(1, 0, 2)
    bias1_all = bias1_all.reshape(2 * channels)
    end_both = parts[:, : 2 * half, 3 * rows :].sum(axis=0)
    a_grad = m_own[:9].T
    grad_conv0 = jnp.concatenate(
        [
            dot(a_grad[:, half * tap : half * tap + half], start_weight, 1, 1, highest)
            for tap in range(3)
        ],
        axis=1,
    )
    grad_mix_last = dot(ew_last, g1_all, 0, 0, highest)
    skip_rows = dot(ew_skip, g0_all, 0, 0, highest)

    other = lax.ppermute(
        mix_rows.astype(bf16), "dp", [(i + half_dp, i) for i in range(half_dp)]
    ).astype(f32)
    final = jnp.concatenate(
        [
            start_t.reshape(-1, 128),
            pad_to(end_both, 2 * half, 128),
            pad_to(m_own[9:10], 1, 128),
        ],
        axis=0,
    )
    per0 = final.shape[0]
    per = -(-per0 // 8) * 8
    final = pad_to(final, per, 128)
    final, _ = lax.optimization_barrier((final, mix_rows.astype(bf16)))
    got = exchange(
        jnp.broadcast_to(final[None], (n_dp, per, 128)).reshape(n_dp * per, 128), "dp"
    ).reshape(n_dp, per, 128)
    n_start = half * channels // 128
    grad_start = got[:, :n_start].sum(axis=0).reshape(half, channels).T
    ends = got[:, n_start : n_start + 2 * half]
    grad_end = ends[:, :, :last_rows].transpose(1, 0, 2).reshape(2 * half, channels)
    grad_end = grad_end + ends[half_dp:, :, last_rows : last_rows + rows].transpose(
        1, 0, 2
    ).reshape(2 * half, channels)
    bias0_all = got[:, n_start + 2 * half, :rows].reshape(2 * channels)
    grad_bias = jnp.stack([bias0_all, bias1_all])
    residual = jnp.concatenate([mix_rows, other], axis=0)
    grad_mix_first = jnp.where(low, residual, skip_rows)
    grad_conv = jnp.stack([grad_conv0, grad_conv1])
    return (coupled, grad_start, grad_conv, grad_bias, grad_mix_first, grad_mix_last, grad_end)


def solution(mesh):
    in_specs = (
        P("dp", None, "ctx"),
        P("dp"),
        P("dp", "ctx"),
        P(),
        P(None, "dp", None),
        P(),
        P("dp", None),
        P("dp", None),
        P(),
        P("dp", None, "ctx"),
    )
    out_specs = (
        P("dp", None, "ctx"),
        P(),
        P(None, "dp", None),
        P(),
        P("dp", None),
        P("dp", None),
        P(),
    )
    return jax.shard_map(local, mesh=mesh, in_specs=in_specs, out_specs=out_specs, check_vma=False)
```
